32 devices in a mesh: blk: 2 (over core), inner: 4 (over z), outer: 4 (over y, x).
Axes of the slice: x: 2, y: 2, z: 4, core: 2. Of those that a mesh axis runs over, the one named last changes fastest.
Arguments:
- hidden: bfloat16 [64, 256, 1152], P(('inner', 'outer'), 'blk'), may hold values from -6 to 6
- labels: int32 [64], P(('inner', 'outer')), may hold values from 0 to 1000
- steps_t: int32 [64], P(('inner', 'outer')), may hold values from 0 to 999
- live_slots: int32 [64], P(('inner', 'outer')), may hold values from 0 to 1, as said below
- label_table: bfloat16 [1001, 1152], replicated, may hold values from -6 to 6
- targets: bfloat16 [64, 256, 768], P(('inner', 'outer'), 'blk'), may hold values from -6 to 6
- cotangent: bfloat16 [64, 256, 1152], P(('inner', 'outer'), 'blk'), may hold values from -6 to 6
- weights: float32 [32014336], P(('inner', 'outer'))
- weight_momentum: float32 [32014336], P(('inner', 'outer')), may hold values from -320 to 320
- weight_average: float32 [32014336], P(('inner', 'outer'))
- biases: float32 [20992], P(('inner', 'outer')), may hold values from -1.25 to 1.25
- bias_momentum: float32 [20992], P(('inner', 'outer')), may hold values from -320 to 320
- bias_average: float32 [20992], P(('inner', 'outer')), may hold values from -1.25 to 1.25
Outputs:
- block_out: bfloat16 [64, 256, 1152], P(('inner', 'outer'), 'blk')
- grad_hidden: float32 [64, 256, 1152], P(('inner', 'outer'), 'blk')
- grad_cond: float32 [64, 1152], P(('inner', 'outer'))
- new_weight_momentum: float32 [32014336], P(('inner', 'outer'))
- new_weights: float32 [32014336], P(('inner', 'outer'))
- new_weights_low: bfloat16 [32014336], P(('inner', 'outer'))
- new_weight_average: float32 [32014336], P(('inner', 'outer'))
- new_bias_momentum: float32 [20992], P(('inner', 'outer'))
- new_biases: float32 [20992], P(('inner', 'outer'))
- new_biases_low: bfloat16 [20992], P(('inner', 'outer'))
- new_bias_average: float32 [20992], P(('inner', 'outer'))
The draws below stay inside these ranges and needn't reach their ends.
Inputs may be any that keep to these rules, and one draw needn't show every extreme that they name: `live_slots`: of the 4 slots that one index of inner and outer holds at least one is live, and in the last such index all are.
All inputs are finite; a program needn't handle non-finite values.
Results may differ from the reference program's by a relative error of at most 0.02.
The reference program's roundings to bfloat16 on the way count: a program that leaves them out, or rounds other values in their place, can miss the bound.
Values may be sent and summed in bfloat16 or wider, within the bound.
No kernel may reach another device: no remote copies, remote signals or barrier semaphores. Data moves between devices by JAX's collectives and lax.ppermute only.
A program may use at most 384 MiB of HBM per device.

```python
import math
import jax
import jax.numpy as jnp
from jax import lax

H = 16
E = 72
D = 1152
FF = 4608
PH = 2048
ZD = 768
CLASSES = 1001
TOK = 256
SLOTS = 4
GROUPS = 16
IMAGES = 64
WP = 32014336
BP = 20992


def matrix_scales():
    return [(D, 3 * D, D ** (-0.5)), (D, D, (8.0 / D) ** 0.5), (D, FF, D ** (-0.5)), (FF, D, FF ** (-0.5)), (D, 6 * D, D ** (-0.5)), (D, PH, D ** (-0.5)), (PH, PH, PH ** (-0.5)), (PH, ZD, PH ** (-0.5))]


def shard_major(key):
    segments = []
    for rows_all, cols_all, spread in matrix_scales():
        segments.append(jnp.full((rows_all // GROUPS * cols_all,), spread, jnp.float32))
    scale_row = jnp.concatenate(segments)
    random_part = jax.random.normal(key, (GROUPS, scale_row.shape[0]), jnp.float32)
    return (random_part * scale_row[None, :]).reshape(-1)


def draw_weights(key, part):
    return shard_major(jax.random.fold_in(key, 101))


def draw_weight_average(key, part):
    return shard_major(jax.random.fold_in(key, 202))


def draw_live_slots(key, part):
    group_ids = jnp.arange(GROUPS, dtype=jnp.int32)
    jitter = jax.random.randint(jax.random.fold_in(key, 303), (GROUPS,), 0, GROUPS, dtype=jnp.int32)
    counts = 1 + ((SLOTS - 1) * (group_ids + 1) + jitter) // GROUPS
    scores = jax.random.randint(jax.random.fold_in(key, 404), (GROUPS, SLOTS), 0, 1 << 20, dtype=jnp.int32)
    scores = scores * SLOTS + jnp.arange(SLOTS, dtype=jnp.int32)[None, :]
    rank_pos = jnp.argsort(jnp.argsort(scores, axis=1), axis=1)
    return (rank_pos < counts[:, None]).astype(jnp.int32).reshape(-1)


def set_ends(result, key, low, high):
    place = [jax.random.randint(jax.random.fold_in(key, axis), (), 0, length) for axis, length in enumerate(result.shape)]
    main_axis = result.shape.index(max(result.shape))
    next_to = place[:main_axis] + [(place[main_axis] + 1) % result.shape[main_axis]] + place[main_axis + 1:]
    return result.at[tuple(place)].set(low).at[tuple(next_to)].set(high)


def level_of(key, extent, shards, smallest, top_value):
    level, own = 1.0, jax.random.fold_in(key, 6)
    for axis_at, shards_of in shards:
        steps = jnp.exp(jax.random.uniform(jax.random.fold_in(own, axis_at), (shards_of,), jnp.float32, smallest / len(shards), top_value / len(shards)))
        level = level * jnp.repeat(steps, extent[axis_at] // shards_of).reshape([-1 if axis == axis_at else 1 for axis in range(len(extent))])
    return level


def bell_draw(key, extent, deviation, most, pieces=(), kind=jnp.bfloat16):
    drawn = deviation * jax.random.normal(key, extent, jnp.float32)
    if pieces:
        drawn = drawn * level_of(key, extent, pieces, -0.22, 0.18)
    return jnp.clip(drawn, -most, most).astype(kind)


def setup_inputs(seed: int = 0) -> dict:
    seeds = jax.random.split(jax.random.key(seed), 14)
    return {
        "hidden": bell_draw(seeds[0], (IMAGES, TOK, D), 1.0, 6.0, ((0, 16), (1, 2))),
        "labels": set_ends(jax.random.randint(seeds[1], (IMAGES,), 0, CLASSES), jax.random.fold_in(seeds[1], 1), 0, CLASSES - 1).astype(jnp.int32),
        "steps_t": set_ends(jax.random.randint(seeds[2], (IMAGES,), 0, 1000), jax.random.fold_in(seeds[2], 1), 0, 999).astype(jnp.int32),
        "live_slots": draw_live_slots(jax.random.fold_in(seeds[13], 71), 0),
        "label_table": bell_draw(seeds[4], (CLASSES, D), 1.0, 6.0),
        "targets": bell_draw(seeds[5], (IMAGES, TOK, ZD), 1.0, 6.0, ((0, 16), (1, 2))),
        "cotangent": bell_draw(seeds[6], (IMAGES, TOK, D), 1.0, 6.0, ((0, 16), (1, 2))),
        "weights": draw_weights(jax.random.fold_in(seeds[13], 71), 0),
        "weight_momentum": bell_draw(seeds[8], (WP,), (0.4 * (IMAGES * TOK) ** 0.5), 320.0, ((0, 16),), jnp.float32),
        "weight_average": draw_weight_average(jax.random.fold_in(seeds[13], 71), 0),
        "biases": bell_draw(seeds[10], (BP,), 0.2, 1.25, ((0, 16),), jnp.float32),
        "bias_momentum": bell_draw(seeds[11], (BP,), (0.4 * (IMAGES * TOK) ** 0.5), 320.0, ((0, 16),), jnp.float32),
        "bias_average": bell_draw(seeds[12], (BP,), 0.2, 1.25, ((0, 16),), jnp.float32),
    }


@jax.custom_vjp
def low(v):
    return lax.optimization_barrier(v.astype(jnp.bfloat16)).astype(jnp.float32)

@jax.custom_vjp
def low_back(v):
    return v

def low_keep(v):
    return (low(v), None)

def low_pass(kept, grad):
    return (grad,)

def back_keep(v):
    return (v, None)

def back_low(kept, grad):
    return (low(grad),)
low.defvjp(low_keep, low_pass)
low_back.defvjp(back_keep, back_low)
PRECISE = lax.Precision.HIGHEST
LAMBDA_REPA = 0.5
MOMENTUM = 0.5
AVERAGE = 0.5
LR_COEF = 0.04
BIAS_FACTOR = 4.0
EPS_NORM = 1e-06

def mat_shapes():
    return [(D, 3 * D), (D, D), (D, FF), (FF, D), (D, 6 * D), (D, PH), (PH, PH), (PH, ZD)]

def bias_shapes():
    return [(D,), (D,), (D,), (FF,), (D,), (6 * D,), (PH,), (PH,), (ZD,)]

def unpack_rows(flat_vec, shapes, blocks):
    line_grid = flat_vec.reshape(blocks, -1)
    segments = []
    offset = 0
    for shape_now in shapes:
        length = shape_now[0] // blocks * math.prod(shape_now[1:])
        segments.append(line_grid[:, offset:offset + length].reshape(shape_now))
        offset += length
    return segments

def time_embed(steps_t):
    half_dim = D // 2
    frequency = jnp.exp(-math.log(10000.0) * jnp.arange(half_dim, dtype=jnp.float32) / half_dim)
    angles = steps_t.astype(jnp.float32)[:, None] * frequency[None, :]
    return jnp.concatenate([jnp.cos(angles), jnp.sin(angles)], axis=1)

def layer_norm(values):
    center = values - lax.optimization_barrier(jnp.mean(values, axis=-1, keepdims=True))
    return center * lax.rsqrt(lax.optimization_barrier(jnp.mean(center * center, axis=-1, keepdims=True)) + EPS_NORM)

def rms_unit(values):
    return values * lax.rsqrt(lax.optimization_barrier(jnp.mean(values * values, axis=-1, keepdims=True)) + EPS_NORM)

def product(left_arr, right_arr):
    return jnp.einsum('...i,ij->...j', left_arr, right_arr, precision=PRECISE)

def forward(flat_w, flat_b, hidden_f, condition, targets_f, cotan_f, live_f):
    w_qkv, w_proj, w_up, w_down, w_ada, w_one, w_two, w_three = unpack_rows(flat_w, mat_shapes(), GROUPS)
    b_q, b_v, b_proj, b_up, b_down, b_ada, c_one, c_two, c_three = unpack_rows(flat_b, bias_shapes(), GROUPS)
    batch_count = hidden_f.shape[0]
    cond_low = low(jax.nn.silu(condition))
    modulation = low_back(product(cond_low, w_ada) + b_ada)
    shift_a, scale_a, gate_a, shift_m, scale_m, gate_m = [modulation[:, None, part_idx * D:(part_idx + 1) * D] for part_idx in range(6)]
    mixed_a = low(layer_norm(hidden_f) * (1.0 + scale_a) + shift_a)
    qkv_bias = jnp.concatenate([b_q, jnp.zeros((D,), jnp.float32), b_v])
    qkv_all = low(low_back(product(mixed_a, w_qkv) + qkv_bias))
    queries = qkv_all[..., :D].reshape(batch_count, TOK, H, E)
    key_part = qkv_all[..., D:2 * D].reshape(batch_count, TOK, H, E)
    value_part = qkv_all[..., 2 * D:].reshape(batch_count, TOK, H, E)
    scores = low_back(jnp.einsum('bnhe,bmhe->bhnm', queries, key_part, precision=PRECISE) * E ** (-0.5))
    probs_all = jax.nn.softmax(scores, axis=-1)
    attended = jnp.einsum('bhnm,bmhe->bnhe', low(probs_all), value_part, precision=PRECISE).reshape(batch_count, TOK, D)
    attended = low(low_back(attended))
    branch_a = low_back(product(attended, w_proj) + b_proj)
    residual = hidden_f + gate_a * branch_a
    mixed_m = low(layer_norm(residual) * (1.0 + scale_m) + shift_m)
    pre_act = low_back(product(mixed_m, w_up) + b_up)
    activated = low(jax.nn.gelu(pre_act, approximate=True))
    branch_m = low_back(product(activated, w_down) + b_down)
    output = residual + gate_m * branch_m
    out_low = low(output)
    hid_one = low_back(product(out_low, w_one) + c_one)
    act_one = low(jax.nn.silu(hid_one))
    hid_two = low_back(product(act_one, w_two) + c_two)
    act_two = low(jax.nn.silu(hid_two))
    projection = low_back(product(act_two, w_three) + c_three)
    weight_live = live_f[:, None, None]
    objective = jnp.sum(weight_live * (cotan_f * output)) - LAMBDA_REPA * jnp.sum(weight_live * (rms_unit(projection) * rms_unit(targets_f)))
    return (objective, output)

def reference(hidden, labels, steps_t, live_slots, label_table, targets, cotangent, weights, weight_momentum, weight_average, biases, bias_momentum, bias_average):
    flat_w = lax.optimization_barrier(weights.astype(jnp.bfloat16)).astype(jnp.float32)
    flat_b = lax.optimization_barrier(biases.astype(jnp.bfloat16)).astype(jnp.float32)
    condition = label_table[labels].astype(jnp.float32) + time_embed(steps_t)
    per_step = math.gcd(IMAGES, 16)
    rounds = IMAGES // per_step

    def batch_view(tensor):
        return tensor.reshape((rounds, per_step) + tuple(tensor.shape[1:]))
    batched = (batch_view(hidden.astype(jnp.float32)), batch_view(condition), batch_view(targets.astype(jnp.float32)), batch_view(cotangent.astype(jnp.float32)), batch_view(live_slots.astype(jnp.float32)))

    def one_round(carried, slices):
        hidden_s, cond_s, targets_s, cotan_s, live_s = slices

        def local_fn(weight_vec, bias_vec, hidden_v, cond_v):
            return forward(weight_vec, bias_vec, hidden_v, cond_v, targets_s, cotan_s, live_s)
        objective, pullback, output = jax.vjp(local_fn, flat_w, flat_b, hidden_s, cond_s, has_aux=True)
        grad_w, grad_b, grad_h, grad_c = pullback(jnp.ones_like(objective))
        return ((carried[0] + grad_w, carried[1] + grad_b), (output.astype(jnp.bfloat16), grad_h, grad_c))
    initial = (jnp.zeros_like(flat_w), jnp.zeros_like(flat_b))
    (grad_w, grad_b), (outputs, grad_h, grad_c) = lax.scan(one_round, initial, batched)
    rate_w = LR_COEF / math.sqrt(IMAGES * TOK)
    rate_b = BIAS_FACTOR * rate_w
    mom_w = MOMENTUM * weight_momentum + grad_w
    new_w = weights - rate_w * (grad_w + MOMENTUM * mom_w)
    avg_w = AVERAGE * weight_average + (1.0 - AVERAGE) * new_w
    mom_b = MOMENTUM * bias_momentum + grad_b
    new_b = biases - rate_b * (grad_b + MOMENTUM * mom_b)
    avg_b = AVERAGE * bias_average + (1.0 - AVERAGE) * new_b
    return (outputs.reshape(IMAGES, TOK, D), grad_h.reshape(IMAGES, TOK, D), grad_c.reshape(IMAGES, D), mom_w, new_w, new_w.astype(jnp.bfloat16), avg_w, mom_b, new_b, new_b.astype(jnp.bfloat16), avg_b)
```

```python
import math

import jax
import jax.numpy as jnp
from jax import lax
from jax.experimental import pallas as pl
from jax.experimental.pallas import tpu as pltpu
from jax.sharding import PartitionSpec as P

E = 72
D = 1152
FF = 4608
PH = 2048
ZD = 768


LAMBDA_REPA = 0.5
MOMENTUM = 0.5
AVERAGE = 0.5
LR_COEF = 0.04
BIAS_FACTOR = 4.0
EPS_NORM = 1e-06
GROUP = ("inner", "outer")
EVERY = ("blk", "inner", "outer")
LOW = jnp.bfloat16


def passed_along(block, axis, distance):
    devices = range(lax.axis_size(axis))
    route = [((i - distance) % len(devices), i) for i in devices]
    return lax.ppermute(block, axis, route)


def mat_shapes():
    return [(D, 3 * D), (D, D), (D, FF), (FF, D), (D, 6 * D), (D, PH), (PH, PH), (PH, ZD)]


def bias_shapes():
    return [(D,), (D,), (D,), (FF,), (D,), (6 * D,), (PH,), (PH,), (ZD,)]


def split_shard(flat_vec, shapes, blocks):
    segments = []
    offset = 0
    for shape_now in shapes:
        rows_here = shape_now[0] // blocks
        length = rows_here * math.prod(shape_now[1:])
        segments.append(
            flat_vec[offset : offset + length].reshape((rows_here,) + tuple(shape_now[1:]))
        )
        offset += length
    return segments


def unpack_rows(line_grid, shapes):
    blocks = line_grid.shape[0]
    segments = []
    offset = 0
    for shape_now in shapes:
        length = shape_now[0] // blocks * math.prod(shape_now[1:])
        segments.append(line_grid[:, offset : offset + length].reshape(shape_now))
        offset += length
    return segments


def flat_id(core, z_at, outer_at):
    return (core * 4 + z_at) * 4 + outer_at


def route_z(pairs_core0):
    route = []
    for z_from, z_to in pairs_core0:
        for outer_at in range(4):
            route.append((flat_id(0, z_from, outer_at), flat_id(0, z_to, outer_at)))
            route.append((flat_id(1, 3 - z_from, outer_at), flat_id(1, 3 - z_to, outer_at)))
    return route


def flipped(route):
    return [(target, source) for source, target in route]


def route_xy(step_core0, step_core1):
    route = []
    for z_at in range(4):
        for outer_at in range(4):
            for core, step in ((0, step_core0), (1, step_core1)):
                route.append((flat_id(core, z_at, outer_at), flat_id(core, z_at, outer_at ^ step)))
    return route


STEP_X, STEP_Y = 1, 2
NEAR_FIRST = route_xy(STEP_X, STEP_Y)
NEAR_SECOND = route_xy(STEP_Y, STEP_X)
Z_PAIR = route_z([(0, 1), (1, 0)])
Z_STRAIGHT = route_z([(0, 2), (1, 3)])
Z_CROSS = route_z([(0, 3), (1, 2)])
SWAP = [(0, 1), (1, 0)]
UP = [(0, 1), (1, 2), (2, 3), (3, 0)]
DOWN = [(1, 0), (2, 1), (3, 2), (0, 3)]
ACROSS = [(0, 2), (2, 0), (1, 3), (3, 1)]
OUT_X = [(0, 1), (1, 0), (2, 3), (3, 2)]
OUT_Y = [(0, 2), (2, 0), (1, 3), (3, 1)]


def place_blocks(sources, table, count):
    counts = [source.shape[0] for source in sources]

    def kernel(table_ref, *refs):
        source_refs = refs[: len(counts)]
        out_ref, sems = refs[len(counts) :]
        copies = []
        for source_ref, length in zip(source_refs, counts):
            for at in range(length):
                number = len(copies)
                copies.append(
                    pltpu.make_async_copy(
                        source_ref.at[at], out_ref.at[table_ref[number]], sems.at[number]
                    )
                )
        for copy in copies:
            copy.start()
        for copy in copies:
            copy.wait()

    shape = (count,) + sources[0].shape[1:]
    return pl.pallas_call(
        kernel,
        out_shape=jax.ShapeDtypeStruct(shape, sources[0].dtype),
        grid_spec=pltpu.PrefetchScalarGridSpec(
            num_scalar_prefetch=1,
            grid=(1,),
            in_specs=[pl.BlockSpec(memory_space=pl.ANY)] * len(sources),
            out_specs=pl.BlockSpec(memory_space=pl.ANY),
            scratch_shapes=[pltpu.SemaphoreType.DMA((count,))],
        ),
        name="place_blocks",
    )(table, *sources)


def pick_blocks(source, table, counts):
    total = sum(counts)

    def kernel(table_ref, source_ref, *refs):
        out_refs = refs[: len(counts)]
        sems = refs[len(counts)]
        copies = []
        for out_ref, length in zip(out_refs, counts):
            for at in range(length):
                number = len(copies)
                copies.append(
                    pltpu.make_async_copy(
                        source_ref.at[table_ref[number]], out_ref.at[at], sems.at[number]
                    )
                )
        for copy in copies:
            copy.start()
        for copy in copies:
            copy.wait()

    return pl.pallas_call(
        kernel,
        out_shape=[
            jax.ShapeDtypeStruct((length,) + source.shape[1:], source.dtype) for length in counts
        ],
        grid_spec=pltpu.PrefetchScalarGridSpec(
            num_scalar_prefetch=1,
            grid=(1,),
            in_specs=[pl.BlockSpec(memory_space=pl.ANY)],
            out_specs=[pl.BlockSpec(memory_space=pl.ANY)] * len(counts),
            scratch_shapes=[pltpu.SemaphoreType.DMA((total,))],
        ),
        name="pick_blocks",
    )(table, source)


class Staged:
    def __init__(self):
        self.core = lax.axis_index("blk")
        self.z_at = lax.axis_index("inner")
        outer_at = lax.axis_index("outer")
        self.y_at = outer_at // 2
        self.x_at = outer_at % 2
        self.own_half = (self.z_at // 2) == self.core
        self.own_row = self.z_at * 4 + outer_at

    def z_pair(self, core):
        low_bit = self.z_at % 2
        return 2 * core + low_bit, 2 * core + 1 - low_bit

    def near_order(self, core, picks):
        found = []
        for far, near in picks:
            first = jnp.where(core == 0, self.x_at, self.y_at) ^ near
            second = jnp.where(core == 0, self.y_at, self.x_at) ^ far
            y_now = jnp.where(core == 0, second, first)
            x_now = jnp.where(core == 0, first, second)
            found.append(y_now * 2 + x_now)
        return found

    def gather_rows(self, own):
        pair = lax.ppermute(own, EVERY, Z_PAIR)
        straight = lax.ppermute(own, EVERY, Z_STRAIGHT)
        cross = lax.ppermute(own, EVERY, Z_CROSS)
        two = jnp.where(
            self.own_half, jnp.stack([own, pair]), jnp.stack([straight, cross])
        )
        four = jnp.concatenate([two, lax.ppermute(two, EVERY, NEAR_FIRST)])
        far_four = lax.ppermute(four, EVERY, NEAR_SECOND)
        mate_four = lax.ppermute(four, "blk", SWAP)
        mate_far = lax.ppermute(far_four, "blk", SWAP)
        table = []
        for core in (self.core, 1 - self.core):
            for outer_at in self.near_order(core, [(0, 0), (0, 1), (1, 0), (1, 1)]):
                for z_now in self.z_pair(core):
                    table.append(z_now * 4 + outer_at)
        full = place_blocks(
            [four, far_four, mate_four, mate_far], jnp.stack(table).astype(jnp.int32), 16
        )
        return full.reshape(-1, own.shape[-1])

    def share_left(self, left):
        half = left.shape[-1] // 2
        tokens = left.reshape(-1, left.shape[-1])
        keep = lax.dynamic_slice_in_dim(tokens, self.core * half, half, 1)
        give = lax.dynamic_slice_in_dim(tokens, (1 - self.core) * half, half, 1)
        return jnp.concatenate([keep, lax.ppermute(give, "blk", SWAP)])

    def weight_grad(self, left, right):
        tokens = right.reshape(-1, right.shape[-1])
        both = jnp.concatenate([tokens, lax.ppermute(tokens, "blk", SWAP)])
        grad = jnp.einsum("ni,nj->ij", left, both, preferred_element_type=jnp.float32)
        blocks = grad.astype(LOW).reshape(8, -1, grad.shape[-1])
        low_bit = self.z_at % 2
        table = []
        for outer_at in self.near_order(self.core, [(1, 1), (1, 0), (0, 1), (0, 0)]):
            for z_now in (low_bit, 1 - low_bit):
                table.append(z_now * 4 + outer_at)
        give, keep = pick_blocks(blocks, jnp.stack(table).astype(jnp.int32), (4, 4))
        came = lax.ppermute(give, EVERY, NEAR_SECOND)
        give = (keep[:2].astype(jnp.float32) + came[:2].astype(jnp.float32)).astype(LOW)
        keep = (keep[2:].astype(jnp.float32) + came[2:].astype(jnp.float32)).astype(LOW)
        came = lax.ppermute(give, EVERY, NEAR_FIRST)
        first = (keep[0].astype(jnp.float32) + came[0].astype(jnp.float32)).astype(LOW)
        second = (keep[1].astype(jnp.float32) + came[1].astype(jnp.float32)).astype(LOW)
        pair = lax.ppermute(second, EVERY, flipped(Z_PAIR))
        straight = lax.ppermute(first, EVERY, flipped(Z_STRAIGHT))
        cross = lax.ppermute(second, EVERY, flipped(Z_CROSS))
        summed = (
            (first.astype(jnp.float32) + pair.astype(jnp.float32))
            + (straight.astype(jnp.float32) + cross.astype(jnp.float32))
        ).astype(LOW)
        mate = lax.ppermute(summed, "blk", SWAP)
        return jnp.where(self.own_half, summed, mate).astype(jnp.float32)

    def gather_slots(self, own):
        four = jnp.stack(
            [own]
            + [lax.ppermute(own, "inner", route) for route in (UP, DOWN, ACROSS)]
        )
        eight = jnp.stack([four, lax.ppermute(four, "outer", OUT_X)])
        full = jnp.stack([eight, lax.ppermute(eight, "outer", OUT_Y)])
        return full.reshape((16,) + own.shape)

    def reduce_slots(self, parts):
        parts = parts.reshape((2, 2, 4) + parts.shape[1:])
        eight = parts[0] + lax.ppermute(parts[1], "outer", OUT_Y)
        four = eight[0] + lax.ppermute(eight[1], "outer", OUT_X)
        return (
            (four[0] + lax.ppermute(four[1], "inner", DOWN))
            + (lax.ppermute(four[2], "inner", UP) + lax.ppermute(four[3], "inner", ACROSS))
        )

    def slots_seen_from(self, gathered):
        found = []
        for slot in range(16):
            back = (slot // 4) * 4 + (0, 2, 1, 3)[slot % 4]
            found.append(gathered[slot, back])
        return jnp.stack(found)

    def rows_in_order(self, slots):
        table = []
        for z_now in range(4):
            away = (z_now - self.z_at) % 4
            z_slot = jnp.where(away == 0, 0, jnp.where(away == 3, 1, jnp.where(away == 1, 2, 3)))
            for outer_now in range(4):
                flip = jnp.bitwise_xor(outer_now, self.y_at * 2 + self.x_at)
                table.append(flip * 4 + z_slot)
        flat = jnp.take(slots.reshape(16, -1), jnp.stack(table), axis=0)
        return flat.reshape(slots.shape)


def outer_sum(left_arr, right_arr):
    return jnp.einsum("sni,snj->ij", left_arr, right_arr, preferred_element_type=jnp.float32)


class Direct:
    def __init__(self):
        self.core = lax.axis_index("blk")
        self.own_row = lax.axis_index("inner") * lax.axis_size("outer") + lax.axis_index("outer")

    def gather_rows(self, own):
        return lax.all_gather(own, GROUP, axis=0, tiled=True)

    def share_left(self, left):
        return left

    def weight_grad(self, left, right):
        grad = outer_sum(left, right).astype(LOW)
        part = lax.psum_scatter(grad, GROUP, scatter_dimension=0, tiled=True)
        return lax.psum(part, "blk").astype(jnp.float32)

    def gather_slots(self, own):
        return lax.all_gather(own, GROUP, axis=0)

    def reduce_slots(self, parts):
        return lax.psum_scatter(parts, GROUP, scatter_dimension=0, tiled=False)

    def slots_seen_from(self, gathered):
        return lax.dynamic_index_in_dim(gathered, self.own_row, 1, keepdims=False)

    def rows_in_order(self, slots):
        return slots


def time_embed(steps_t):
    half_dim = D // 2
    frequency = jnp.exp(-math.log(10000.0) * jnp.arange(half_dim, dtype=jnp.float32) / half_dim)
    angles = steps_t.astype(jnp.float32)[:, None] * frequency[None, :]
    return jnp.concatenate([jnp.cos(angles), jnp.sin(angles)], axis=1)


def modulate(values, scale_v, shift_v):
    center = values - jnp.mean(values, axis=-1, keepdims=True)
    normed = center * lax.rsqrt(jnp.mean(center * center, axis=-1, keepdims=True) + EPS_NORM)
    return normed * (1.0 + scale_v[:, None, :]) + shift_v[:, None, :]


def gelu_tanh(values):
    return jax.nn.gelu(values, approximate=True)


def rms_unit(values):
    return values * lax.rsqrt(jnp.mean(values * values, axis=-1, keepdims=True) + EPS_NORM)


def matmul(left_arr, right_arr):
    return jnp.einsum("...i,ij->...j", left_arr, right_arr, preferred_element_type=jnp.float32)


def matmul_t(left_arr, right_arr):
    return jnp.einsum("...j,ij->...i", left_arr, right_arr, preferred_element_type=jnp.float32)


def column_sum(tensor):
    return jnp.sum(tensor.astype(jnp.float32), axis=(0, 1))


def head_view(tensor):
    return tensor.reshape(tensor.shape[0], tensor.shape[1], -1, E)


def score_block(queries, kv_pair):
    raw_scores = jnp.einsum(
        "snhe,smhe->shnm",
        head_view(queries),
        head_view(kv_pair[..., :D]),
        preferred_element_type=jnp.float32,
    )
    return raw_scores * E ** (-0.5)


def weigh_values(probs_blk, kv_pair):
    mixed_out = jnp.einsum(
        "shnm,smhe->snhe",
        probs_blk.astype(jnp.bfloat16),
        head_view(kv_pair[..., D:]),
        preferred_element_type=jnp.float32,
    )
    return mixed_out.reshape(mixed_out.shape[0], mixed_out.shape[1], D)


def grad_block(queries, kv_pair, log_sum, grad_att):
    probs_blk = jnp.exp(score_block(queries, kv_pair) - log_sum[..., None])
    grad_prob = jnp.einsum(
        "snhe,smhe->shnm",
        head_view(grad_att),
        head_view(kv_pair[..., D:]),
        preferred_element_type=jnp.float32,
    )
    return (probs_blk, grad_prob)


def key_product(grad_scores, kv_pair):
    result = jnp.einsum(
        "shnm,smhe->snhe",
        grad_scores,
        head_view(kv_pair[..., :D]),
        preferred_element_type=jnp.float32,
    )
    return result.reshape(result.shape[0], result.shape[1], D)


def kv_grads(grad_scores, probs_blk, queries, grad_att):
    grad_keys = jnp.einsum(
        "shnm,snhe->smhe", grad_scores, head_view(queries), preferred_element_type=jnp.float32
    ) * E ** (-0.5)
    grad_vals = jnp.einsum(
        "shnm,snhe->smhe",
        probs_blk.astype(jnp.bfloat16),
        head_view(grad_att),
        preferred_element_type=jnp.float32,
    )
    rows_n = grad_keys.shape[1]
    return jnp.concatenate(
        [
            grad_keys.reshape(grad_keys.shape[0], rows_n, D),
            grad_vals.reshape(grad_vals.shape[0], rows_n, D),
        ],
        axis=-1,
    )


def body(
    hidden,
    labels,
    steps_t,
    live_slots,
    label_table,
    targets,
    cotangent,
    weights,
    weight_momentum,
    weight_average,
    biases,
    bias_momentum,
    bias_average,
):
    n_inner = lax.axis_size("inner")
    n_outer = lax.axis_size("outer")
    blocks = n_inner * n_outer
    slots = hidden.shape[0]
    local_tok = hidden.shape[1]
    moves = Staged() if (n_inner, n_outer) == (4, 4) else Direct()
    p_qkv, p_proj, p_up, p_down, p_ada, p_one, p_two, p_three = split_shard(
        weights.astype(LOW), mat_shapes(), blocks
    )
    bias_low = biases.astype(LOW)
    condition = label_table[labels].astype(jnp.float32) + time_embed(steps_t)
    cond_act, silu_cond = jax.vjp(jax.nn.silu, condition)
    cond_low = cond_act.astype(LOW)
    packed = jnp.concatenate([cond_low.reshape(-1), bias_low])
    packed_all = moves.gather_slots(packed)
    cond_all = packed_all[:, : slots * D].reshape(blocks * slots, D)
    bias_all = moves.rows_in_order(packed_all[:, slots * D :])
    b_q, b_v, b_proj, b_up, b_down, b_ada, c_one, c_two, c_three = unpack_rows(
        bias_all.astype(jnp.float32), bias_shapes()
    )
    rows_d = D // blocks
    cond_own = lax.dynamic_slice_in_dim(cond_all, moves.own_row * rows_d, rows_d, 1)
    half_ada = 3 * D
    ada_half = lax.dynamic_slice_in_dim(p_ada, moves.core * half_ada, half_ada, 1)
    mod_part = matmul(cond_own, ada_half).reshape(blocks, slots, half_ada)
    mod_half = moves.reduce_slots(mod_part)
    mod_mate = lax.ppermute(mod_half, "blk", SWAP)
    modulation = (
        jnp.concatenate(
            [
                jnp.where(moves.core == 0, mod_half, mod_mate),
                jnp.where(moves.core == 0, mod_mate, mod_half),
            ],
            axis=1,
        )
        + b_ada
    )
    w_qkv, w_proj, w_up, w_down, w_one, w_two, w_three = [
        moves.gather_rows(p) for p in (p_qkv, p_proj, p_up, p_down, p_one, p_two, p_three)
    ]
    shift_a, scale_a, gate_a, shift_m, scale_m, gate_m = [
        modulation[:, part_idx * D : (part_idx + 1) * D] for part_idx in range(6)
    ]
    hidden_f = hidden.astype(jnp.float32)
    mixed_a, pull_a = jax.vjp(modulate, hidden_f, scale_a, shift_a)
    mixed_a_low = mixed_a.astype(LOW)
    left_qkv = moves.share_left(mixed_a_low)
    qkv_bias = jnp.concatenate([b_q, jnp.zeros((D,), jnp.float32), b_v])
    qkv_low = (matmul(mixed_a_low, w_qkv) + qkv_bias).astype(LOW)
    queries = qkv_low[..., :D]
    near_kv = qkv_low[..., D:]
    far_kv = passed_along(near_kv, "blk", 1)
    near_s = score_block(queries, near_kv)
    far_s = score_block(queries, far_kv)
    row_top = jnp.maximum(jnp.max(near_s, axis=-1), jnp.max(far_s, axis=-1))
    row_total = jnp.sum(jnp.exp(near_s - row_top[..., None]), axis=-1) + jnp.sum(
        jnp.exp(far_s - row_top[..., None]), axis=-1
    )
    log_sum = row_top + jnp.log(row_total)
    attended = weigh_values(jnp.exp(near_s - log_sum[..., None]), near_kv) + weigh_values(
        jnp.exp(far_s - log_sum[..., None]), far_kv
    )
    att_low = attended.astype(LOW)
    left_proj = moves.share_left(att_low)
    branch_a = matmul(att_low, w_proj) + b_proj
    residual = hidden_f + gate_a[:, None, :] * branch_a
    mixed_m, pull_m = jax.vjp(modulate, residual, scale_m, shift_m)
    mixed_m_low = mixed_m.astype(LOW)
    left_up = moves.share_left(mixed_m_low)
    pre_act = matmul(mixed_m_low, w_up) + b_up
    activated, gelu_pull = jax.vjp(gelu_tanh, pre_act)
    act_low = activated.astype(LOW)
    left_down = moves.share_left(act_low)
    branch_m = matmul(act_low, w_down) + b_down
    output = residual + gate_m[:, None, :] * branch_m
    out_low = output.astype(LOW)
    left_one = moves.share_left(out_low)
    hid_one = matmul(out_low, w_one) + c_one
    act_one, silu_one = jax.vjp(jax.nn.silu, hid_one)
    one_low = act_one.astype(LOW)
    left_two = moves.share_left(one_low)
    hid_two = matmul(one_low, w_two) + c_two
    act_two, silu_two = jax.vjp(jax.nn.silu, hid_two)
    two_low = act_two.astype(LOW)
    left_three = moves.share_left(two_low)
    projection = matmul(two_low, w_three) + c_three
    live_f = live_slots.astype(jnp.float32)[:, None, None]
    unit_proj, unit_pull = jax.vjp(rms_unit, projection)
    grad_proj = unit_pull(-LAMBDA_REPA * live_f * rms_unit(targets.astype(jnp.float32)))[0].astype(
        LOW
    )
    grad_pthree = moves.weight_grad(left_three, grad_proj)
    grad_cthree = column_sum(grad_proj)
    grad_htwo = silu_two(matmul_t(grad_proj, w_three))[0].astype(LOW)
    grad_ptwo = moves.weight_grad(left_two, grad_htwo)
    grad_ctwo = column_sum(grad_htwo)
    grad_hone = silu_one(matmul_t(grad_htwo, w_two))[0].astype(LOW)
    grad_pone = moves.weight_grad(left_one, grad_hone)
    grad_cone = column_sum(grad_hone)
    grad_output = cotangent.astype(jnp.float32) * live_f + matmul_t(grad_hone, w_one)
    grad_gate_m = jnp.sum(grad_output * branch_m, axis=1)
    grad_bm = (gate_m[:, None, :] * grad_output).astype(LOW)
    grad_wdown = moves.weight_grad(left_down, grad_bm)
    grad_bdown = column_sum(grad_bm)
    grad_pre = gelu_pull(matmul_t(grad_bm, w_down))[0].astype(LOW)
    grad_wup = moves.weight_grad(left_up, grad_pre)
    grad_bup = column_sum(grad_pre)
    grad_res_m, grad_scale_m, grad_shift_m = pull_m(matmul_t(grad_pre, w_up))
    grad_residual = grad_output + grad_res_m
    grad_gate_a = jnp.sum(grad_residual * branch_a, axis=1)
    grad_ba = (gate_a[:, None, :] * grad_residual).astype(LOW)
    grad_wproj = moves.weight_grad(left_proj, grad_ba)
    grad_bproj = column_sum(grad_ba)
    grad_att = matmul_t(grad_ba, w_proj).astype(LOW)
    near_p, near_dp = grad_block(queries, near_kv, log_sum, grad_att)
    far_p, far_dp = grad_block(queries, far_kv, log_sum, grad_att)
    row_delta = jnp.sum(near_p * near_dp, axis=-1) + jnp.sum(far_p * far_dp, axis=-1)
    near_ds = (near_p * (near_dp - row_delta[..., None])).astype(LOW)
    far_ds = (far_p * (far_dp - row_delta[..., None])).astype(LOW)
    grad_query = (key_product(near_ds, near_kv) + key_product(far_ds, far_kv)) * E ** (-0.5)
    far_dkv = kv_grads(far_ds, far_p, queries, grad_att)
    home_dkv = passed_along(far_dkv.astype(LOW), "blk", -1).astype(far_dkv.dtype)
    near_dkv = kv_grads(near_ds, near_p, queries, grad_att)
    grad_qkv = jnp.concatenate([grad_query, near_dkv + home_dkv], axis=-1).astype(LOW)
    grad_wqkv = moves.weight_grad(left_qkv, grad_qkv)
    qkv_sums = column_sum(grad_qkv)
    grad_hid_a, grad_scale_a, grad_shift_a = pull_a(matmul_t(grad_qkv, w_qkv))
    grad_input = grad_residual + grad_hid_a
    grad_mod_part = jnp.concatenate(
        [grad_shift_a, grad_scale_a, grad_gate_a, grad_shift_m, grad_scale_m, grad_gate_m], axis=1
    )
    bias_terms = (
        qkv_sums[:D],
        qkv_sums[2 * D :],
        grad_bproj,
        grad_bup,
        grad_bdown,
        grad_cone,
        grad_ctwo,
        grad_cthree,
    )
    bias_grid = jnp.concatenate(
        [segment.reshape(blocks, -1) for segment in bias_terms], axis=1
    ).reshape(-1)
    grad_small = jnp.concatenate([grad_mod_part.reshape(-1), bias_grid])
    grad_small = (grad_small + lax.ppermute(grad_small, "blk", SWAP)).astype(LOW)
    small_all = moves.gather_slots(grad_small)
    mod_len = slots * 6 * D
    grad_mod = small_all[:, :mod_len].reshape(blocks * slots, 6 * D)
    grad_wada = jnp.einsum("si,sj->ij", cond_own, grad_mod, preferred_element_type=jnp.float32)
    grad_bada = lax.dynamic_index_in_dim(
        jnp.sum(grad_mod.astype(jnp.float32), axis=0).reshape(blocks, -1),
        moves.own_row,
        0,
        keepdims=False,
    )
    bias_own = jnp.sum(
        lax.dynamic_index_in_dim(
            small_all[:, mod_len:].reshape(blocks, blocks, -1), moves.own_row, 1, keepdims=False
        ).astype(jnp.float32),
        axis=0,
    )
    ada_at = (3 * D + FF + D) // blocks
    grad_b_flat = jnp.concatenate([bias_own[:ada_at], grad_bada, bias_own[ada_at:]])
    cond_cols = matmul_t(grad_mod, p_ada).reshape(blocks, slots, rows_d)
    cond_rows = moves.rows_in_order(moves.slots_seen_from(moves.gather_slots(cond_cols)))
    grad_cond = silu_cond(cond_rows.transpose(1, 0, 2).reshape(slots, D))[0]
    grad_w_flat = jnp.concatenate(
        [
            part.reshape(-1)
            for part in (
                grad_wqkv,
                grad_wproj,
                grad_wup,
                grad_wdown,
                grad_wada,
                grad_pone,
                grad_ptwo,
                grad_pthree,
            )
        ]
    )
    images_all = slots * blocks
    tokens_img = local_tok * lax.axis_size("blk")
    rate_w = LR_COEF / math.sqrt(images_all * tokens_img)
    rate_b = BIAS_FACTOR * rate_w
    mom_w = MOMENTUM * weight_momentum + grad_w_flat
    new_w = weights - rate_w * (grad_w_flat + MOMENTUM * mom_w)
    avg_w = AVERAGE * weight_average + (1.0 - AVERAGE) * new_w
    mom_b = MOMENTUM * bias_momentum + grad_b_flat
    new_b = biases - rate_b * (grad_b_flat + MOMENTUM * mom_b)
    avg_b = AVERAGE * bias_average + (1.0 - AVERAGE) * new_b
    return (
        out_low,
        grad_input,
        grad_cond,
        mom_w,
        new_w,
        new_w.astype(LOW),
        avg_w,
        mom_b,
        new_b,
        new_b.astype(LOW),
        avg_b,
    )


def solution(mesh):
    in_specs = (
        P(("inner", "outer"), "blk", None),
        P(("inner", "outer")),
        P(("inner", "outer")),
        P(("inner", "outer")),
        P(),
        P(("inner", "outer"), "blk", None),
        P(("inner", "outer"), "blk", None),
        P(("inner", "outer")),
        P(("inner", "outer")),
        P(("inner", "outer")),
        P(("inner", "outer")),
        P(("inner", "outer")),
        P(("inner", "outer")),
    )
    out_specs = (
        P(("inner", "outer"), "blk", None),
        P(("inner", "outer"), "blk", None),
        P(("inner", "outer"), None),
        P(("inner", "outer")),
        P(("inner", "outer")),
        P(("inner", "outer")),
        P(("inner", "outer")),
        P(("inner", "outer")),
        P(("inner", "outer")),
        P(("inner", "outer")),
        P(("inner", "outer")),
    )
    return jax.shard_map(body, mesh=mesh, in_specs=in_specs, out_specs=out_specs, check_vma=False)
```

```python
import math

import jax
import jax.numpy as jnp
from jax import lax
from jax.experimental import pallas as pl
from jax.experimental.pallas import tpu as pltpu
from jax.sharding import PartitionSpec as P

E = 72
D = 1152
FF = 4608
PH = 2048
ZD = 768


LAMBDA_REPA = 0.5
MOMENTUM = 0.5
AVERAGE = 0.5
LR_COEF = 0.04
BIAS_FACTOR = 4.0
EPS_NORM = 1e-06
GROUP = ("inner", "outer")
EVERY = ("blk", "inner", "outer")
LOW = jnp.bfloat16


def passed_along(block, axis, distance):
    devices = range(lax.axis_size(axis))
    route = [((i - distance) % len(devices), i) for i in devices]
    return lax.ppermute(block, axis, route)


def mat_shapes():
    return [(D, 3 * D), (D, D), (D, FF), (FF, D), (D, 6 * D), (D, PH), (PH, PH), (PH, ZD)]


def bias_shapes():
    return [(D,), (D,), (D,), (FF,), (D,), (6 * D,), (PH,), (PH,), (ZD,)]


def split_shard(flat_vec, shapes, blocks):
    segments = []
    offset = 0
    for shape_now in shapes:
        rows_here = shape_now[0] // blocks
        length = rows_here * math.prod(shape_now[1:])
        segments.append(
            flat_vec[offset : offset + length].reshape((rows_here,) + tuple(shape_now[1:]))
        )
        offset += length
    return segments


def unpack_rows(line_grid, shapes):
    blocks = line_grid.shape[0]
    segments = []
    offset = 0
    for shape_now in shapes:
        length = shape_now[0] // blocks * math.prod(shape_now[1:])
        segments.append(line_grid[:, offset : offset + length].reshape(shape_now))
        offset += length
    return segments


def flat_id(core, z_at, outer_at):
    return (core * 4 + z_at) * 4 + outer_at


def route_z(pairs_core0):
    route = []
    for z_from, z_to in pairs_core0:
        for outer_at in range(4):
            route.append((flat_id(0, z_from, outer_at), flat_id(0, z_to, outer_at)))
            route.append((flat_id(1, 3 - z_from, outer_at), flat_id(1, 3 - z_to, outer_at)))
    return route


def flipped(route):
    return [(target, source) for source, target in route]


def route_xy(step_core0, step_core1):
    route = []
    for z_at in range(4):
        for outer_at in range(4):
            for core, step in ((0, step_core0), (1, step_core1)):
                route.append((flat_id(core, z_at, outer_at), flat_id(core, z_at, outer_at ^ step)))
    return route


STEP_X, STEP_Y = 1, 2
NEAR_FIRST = route_xy(STEP_X, STEP_Y)
NEAR_SECOND = route_xy(STEP_Y, STEP_X)
Z_PAIR = route_z([(0, 1), (1, 0)])
Z_STRAIGHT = route_z([(0, 2), (1, 3)])
Z_CROSS = route_z([(0, 3), (1, 2)])
SWAP = [(0, 1), (1, 0)]
UP = [(0, 1), (1, 2), (2, 3), (3, 0)]
DOWN = [(1, 0), (2, 1), (3, 2), (0, 3)]
ACROSS = [(0, 2), (2, 0), (1, 3), (3, 1)]
OUT_X = [(0, 1), (1, 0), (2, 3), (3, 2)]
OUT_Y = [(0, 2), (2, 0), (1, 3), (3, 1)]


def move_blocks(table, sources, outs, plan, name):
    block = sources[0].shape[1:]

    def kernel(table_ref, *refs):
        source_refs = refs[: len(sources)]
        out_refs = refs[len(sources) : len(sources) + len(outs)]
        held, sems_in, sems_out = refs[len(sources) + len(outs) :]
        arriving, leaving = [], []
        for number, (source_at, index, out_at, out_index) in enumerate(plan):
            from_row = table_ref[number] if index is None else index
            to_row = table_ref[number] if out_index is None else out_index
            arriving.append(
                pltpu.make_async_copy(
                    source_refs[source_at].at[from_row], held.at[number], sems_in.at[number]
                )
            )
            leaving.append(
                pltpu.make_async_copy(
                    held.at[number], out_refs[out_at].at[to_row], sems_out.at[number]
                )
            )
        for copy in arriving:
            copy.start()
        for copy_in, copy_out in zip(arriving, leaving):
            copy_in.wait()
            copy_out.start()
        for copy in leaving:
            copy.wait()

    count = len(plan)
    low = sources[0].dtype
    return pl.pallas_call(
        kernel,
        out_shape=[jax.ShapeDtypeStruct((length,) + block, low) for length in outs],
        grid_spec=pltpu.PrefetchScalarGridSpec(
            num_scalar_prefetch=1,
            grid=(1,),
            in_specs=[pl.BlockSpec(memory_space=pl.ANY)] * len(sources),
            out_specs=[pl.BlockSpec(memory_space=pl.ANY)] * len(outs),
            scratch_shapes=[
                pltpu.VMEM((count,) + block, low),
                pltpu.SemaphoreType.DMA((count,)),
                pltpu.SemaphoreType.DMA((count,)),
            ],
        ),
        compiler_params=pltpu.CompilerParams(vmem_limit_bytes=32 * 1024 * 1024),
        name=name,
    )(table, *sources)


def place_blocks(sources, table, count):
    plan = [
        (source_at, at, 0, None)
        for source_at, source in enumerate(sources)
        for at in range(source.shape[0])
    ]
    return move_blocks(table, sources, [count], plan, "place_blocks")[0]


def pick_blocks(source, table, counts):
    plan = [
        (0, None, out_at, at) for out_at, length in enumerate(counts) for at in range(length)
    ]
    return move_blocks(table, [source], list(counts), plan, "pick_blocks")


class Staged:
    def __init__(self):
        self.core = lax.axis_index("blk")
        self.z_at = lax.axis_index("inner")
        outer_at = lax.axis_index("outer")
        self.y_at = outer_at // 2
        self.x_at = outer_at % 2
        self.own_half = (self.z_at // 2) == self.core
        self.own_row = self.z_at * 4 + outer_at

    def z_pair(self, core):
        low_bit = self.z_at % 2
        return 2 * core + low_bit, 2 * core + 1 - low_bit

    def near_order(self, core, picks):
        found = []
        for far, near in picks:
            first = jnp.where(core == 0, self.x_at, self.y_at) ^ near
            second = jnp.where(core == 0, self.y_at, self.x_at) ^ far
            y_now = jnp.where(core == 0, second, first)
            x_now = jnp.where(core == 0, first, second)
            found.append(y_now * 2 + x_now)
        return found

    def gather_rows(self, own):
        pair = lax.ppermute(own, EVERY, Z_PAIR)
        straight = lax.ppermute(own, EVERY, Z_STRAIGHT)
        cross = lax.ppermute(own, EVERY, Z_CROSS)
        two = jnp.where(
            self.own_half, jnp.stack([own, pair]), jnp.stack([straight, cross])
        )
        four = jnp.concatenate([two, lax.ppermute(two, EVERY, NEAR_FIRST)])
        far_four = lax.ppermute(four, EVERY, NEAR_SECOND)
        mate_four = lax.ppermute(four, "blk", SWAP)
        mate_far = lax.ppermute(far_four, "blk", SWAP)
        table = []
        for core in (self.core, 1 - self.core):
            for outer_at in self.near_order(core, [(0, 0), (0, 1), (1, 0), (1, 1)]):
                for z_now in self.z_pair(core):
                    table.append(z_now * 4 + outer_at)
        full = place_blocks(
            [four, far_four, mate_four, mate_far], jnp.stack(table).astype(jnp.int32), 16
        )
        return full.reshape(-1, own.shape[-1])

    def share_left(self, left):
        half = left.shape[-1] // 2
        tokens = left.reshape(-1, left.shape[-1])
        keep = lax.dynamic_slice_in_dim(tokens, self.core * half, half, 1)
        give = lax.dynamic_slice_in_dim(tokens, (1 - self.core) * half, half, 1)
        return jnp.concatenate([keep, lax.ppermute(give, "blk", SWAP)])

    def weight_grad(self, left, right):
        tokens = right.reshape(-1, right.shape[-1])
        both = jnp.concatenate([tokens, lax.ppermute(tokens, "blk", SWAP)])
        grad = jnp.einsum("ni,nj->ij", left, both, preferred_element_type=jnp.float32)
        blocks = grad.astype(LOW).reshape(8, -1, grad.shape[-1])
        low_bit = self.z_at % 2
        table = []
        for outer_at in self.near_order(self.core, [(1, 1), (1, 0), (0, 1), (0, 0)]):
            for z_now in (low_bit, 1 - low_bit):
                table.append(z_now * 4 + outer_at)
        give, keep = pick_blocks(blocks, jnp.stack(table).astype(jnp.int32), (4, 4))
        came = lax.ppermute(give, EVERY, NEAR_SECOND)
        give = (keep[:2].astype(jnp.float32) + came[:2].astype(jnp.float32)).astype(LOW)
        keep = (keep[2:].astype(jnp.float32) + came[2:].astype(jnp.float32)).astype(LOW)
        came = lax.ppermute(give, EVERY, NEAR_FIRST)
        first = (keep[0].astype(jnp.float32) + came[0].astype(jnp.float32)).astype(LOW)
        second = (keep[1].astype(jnp.float32) + came[1].astype(jnp.float32)).astype(LOW)
        pair = lax.ppermute(second, EVERY, flipped(Z_PAIR))
        straight = lax.ppermute(first, EVERY, flipped(Z_STRAIGHT))
        cross = lax.ppermute(second, EVERY, flipped(Z_CROSS))
        summed = (
            (first.astype(jnp.float32) + pair.astype(jnp.float32))
            + (straight.astype(jnp.float32) + cross.astype(jnp.float32))
        ).astype(LOW)
        mate = lax.ppermute(summed, "blk", SWAP)
        return jnp.where(self.own_half, summed, mate).astype(jnp.float32)

    def gather_slots(self, own):
        four = jnp.stack(
            [own]
            + [lax.ppermute(own, "inner", route) for route in (UP, DOWN, ACROSS)]
        )
        eight = jnp.stack([four, lax.ppermute(four, "outer", OUT_X)])
        full = jnp.stack([eight, lax.ppermute(eight, "outer", OUT_Y)])
        return full.reshape((16,) + own.shape)

    def reduce_slots(self, parts):
        parts = parts.reshape((2, 2, 4) + parts.shape[1:])
        eight = parts[0] + lax.ppermute(parts[1], "outer", OUT_Y)
        four = eight[0] + lax.ppermute(eight[1], "outer", OUT_X)
        return (
            (four[0] + lax.ppermute(four[1], "inner", DOWN))
            + (lax.ppermute(four[2], "inner", UP) + lax.ppermute(four[3], "inner", ACROSS))
        )

    def slots_seen_from(self, gathered):
        found = []
        for slot in range(16):
            back = (slot // 4) * 4 + (0, 2, 1, 3)[slot % 4]
            found.append(gathered[slot, back])
        return jnp.stack(found)

    def rows_in_order(self, slots):
        table = []
        for z_now in range(4):
            away = (z_now - self.z_at) % 4
            z_slot = jnp.where(away == 0, 0, jnp.where(away == 3, 1, jnp.where(away == 1, 2, 3)))
            for outer_now in range(4):
                flip = jnp.bitwise_xor(outer_now, self.y_at * 2 + self.x_at)
                table.append(flip * 4 + z_slot)
        flat = jnp.take(slots.reshape(16, -1), jnp.stack(table), axis=0)
        return flat.reshape(slots.shape)


def outer_sum(left_arr, right_arr):
    return jnp.einsum("sni,snj->ij", left_arr, right_arr, preferred_element_type=jnp.float32)


class Direct:
    def __init__(self):
        self.core = lax.axis_index("blk")
        self.own_row = lax.axis_index("inner") * lax.axis_size("outer") + lax.axis_index("outer")

    def gather_rows(self, own):
        return lax.all_gather(own, GROUP, axis=0, tiled=True)

    def share_left(self, left):
        return left

    def weight_grad(self, left, right):
        grad = outer_sum(left, right).astype(LOW)
        part = lax.psum_scatter(grad, GROUP, scatter_dimension=0, tiled=True)
        return lax.psum(part, "blk").astype(jnp.float32)

    def gather_slots(self, own):
        return lax.all_gather(own, GROUP, axis=0)

    def reduce_slots(self, parts):
        return lax.psum_scatter(parts, GROUP, scatter_dimension=0, tiled=False)

    def slots_seen_from(self, gathered):
        return lax.dynamic_index_in_dim(gathered, self.own_row, 1, keepdims=False)

    def rows_in_order(self, slots):
        return slots


def time_embed(steps_t):
    half_dim = D // 2
    frequency = jnp.exp(-math.log(10000.0) * jnp.arange(half_dim, dtype=jnp.float32) / half_dim)
    angles = steps_t.astype(jnp.float32)[:, None] * frequency[None, :]
    return jnp.concatenate([jnp.cos(angles), jnp.sin(angles)], axis=1)


def modulate(values, scale_v, shift_v):
    center = values - jnp.mean(values, axis=-1, keepdims=True)
    normed = center * lax.rsqrt(jnp.mean(center * center, axis=-1, keepdims=True) + EPS_NORM)
    return normed * (1.0 + scale_v[:, None, :]) + shift_v[:, None, :]


def gelu_tanh(values):
    return jax.nn.gelu(values, approximate=True)


def rms_unit(values):
    return values * lax.rsqrt(jnp.mean(values * values, axis=-1, keepdims=True) + EPS_NORM)


def matmul(left_arr, right_arr):
    return jnp.einsum("...i,ij->...j", left_arr, right_arr, preferred_element_type=jnp.float32)


def matmul_t(left_arr, right_arr):
    return jnp.einsum("...j,ij->...i", left_arr, right_arr, preferred_element_type=jnp.float32)


def column_sum(tensor):
    return jnp.sum(tensor.astype(jnp.float32), axis=(0, 1))


def head_view(tensor):
    return tensor.reshape(tensor.shape[0], tensor.shape[1], -1, E)


def score_block(queries, kv_pair):
    raw_scores = jnp.einsum(
        "snhe,smhe->shnm",
        head_view(queries),
        head_view(kv_pair[..., :D]),
        preferred_element_type=jnp.float32,
    )
    return raw_scores * E ** (-0.5)


def weigh_values(probs_blk, kv_pair):
    mixed_out = jnp.einsum(
        "shnm,smhe->snhe",
        probs_blk.astype(jnp.bfloat16),
        head_view(kv_pair[..., D:]),
        preferred_element_type=jnp.float32,
    )
    return mixed_out.reshape(mixed_out.shape[0], mixed_out.shape[1], D)


def grad_block(queries, kv_pair, log_sum, grad_att):
    probs_blk = jnp.exp(score_block(queries, kv_pair) - log_sum[..., None])
    grad_prob = jnp.einsum(
        "snhe,smhe->shnm",
        head_view(grad_att),
        head_view(kv_pair[..., D:]),
        preferred_element_type=jnp.float32,
    )
    return (probs_blk, grad_prob)


def key_product(grad_scores, kv_pair):
    result = jnp.einsum(
        "shnm,smhe->snhe",
        grad_scores,
        head_view(kv_pair[..., :D]),
        preferred_element_type=jnp.float32,
    )
    return result.reshape(result.shape[0], result.shape[1], D)


def kv_grads(grad_scores, probs_blk, queries, grad_att):
    grad_keys = jnp.einsum(
        "shnm,snhe->smhe", grad_scores, head_view(queries), preferred_element_type=jnp.float32
    ) * E ** (-0.5)
    grad_vals = jnp.einsum(
        "shnm,snhe->smhe",
        probs_blk.astype(jnp.bfloat16),
        head_view(grad_att),
        preferred_element_type=jnp.float32,
    )
    rows_n = grad_keys.shape[1]
    return jnp.concatenate(
        [
            grad_keys.reshape(grad_keys.shape[0], rows_n, D),
            grad_vals.reshape(grad_vals.shape[0], rows_n, D),
        ],
        axis=-1,
    )


def body(
    hidden,
    labels,
    steps_t,
    live_slots,
    label_table,
    targets,
    cotangent,
    weights,
    weight_momentum,
    weight_average,
    biases,
    bias_momentum,
    bias_average,
):
    n_inner = lax.axis_size("inner")
    n_outer = lax.axis_size("outer")
    blocks = n_inner * n_outer
    slots = hidden.shape[0]
    local_tok = hidden.shape[1]
    moves = Staged() if (n_inner, n_outer) == (4, 4) else Direct()
    p_qkv, p_proj, p_up, p_down, p_ada, p_one, p_two, p_three = split_shard(
        weights.astype(LOW), mat_shapes(), blocks
    )
    bias_low = biases.astype(LOW)
    condition = label_table[labels].astype(jnp.float32) + time_embed(steps_t)
    cond_act, silu_cond = jax.vjp(jax.nn.silu, condition)
    cond_low = cond_act.astype(LOW)
    packed = jnp.concatenate([cond_low.reshape(-1), bias_low])
    packed_all = moves.gather_slots(packed)
    cond_all = packed_all[:, : slots * D].reshape(blocks * slots, D)
    bias_all = moves.rows_in_order(packed_all[:, slots * D :])
    b_q, b_v, b_proj, b_up, b_down, b_ada, c_one, c_two, c_three = unpack_rows(
        bias_all.astype(jnp.float32), bias_shapes()
    )
    rows_d = D // blocks
    cond_own = lax.dynamic_slice_in_dim(cond_all, moves.own_row * rows_d, rows_d, 1)
    half_ada = 3 * D
    ada_half = lax.dynamic_slice_in_dim(p_ada, moves.core * half_ada, half_ada, 1)
    mod_part = matmul(cond_own, ada_half).reshape(blocks, slots, half_ada)
    mod_half = moves.reduce_slots(mod_part)
    mod_mate = lax.ppermute(mod_half, "blk", SWAP)
    modulation = (
        jnp.concatenate(
            [
                jnp.where(moves.core == 0, mod_half, mod_mate),
                jnp.where(moves.core == 0, mod_mate, mod_half),
            ],
            axis=1,
        )
        + b_ada
    )
    w_qkv, w_proj, w_up, w_down, w_one, w_two, w_three = [
        moves.gather_rows(p) for p in (p_qkv, p_proj, p_up, p_down, p_one, p_two, p_three)
    ]
    shift_a, scale_a, gate_a, shift_m, scale_m, gate_m = [
        modulation[:, part_idx * D : (part_idx + 1) * D] for part_idx in range(6)
    ]
    hidden_f = hidden.astype(jnp.float32)
    mixed_a, pull_a = jax.vjp(modulate, hidden_f, scale_a, shift_a)
    mixed_a_low = mixed_a.astype(LOW)
    left_qkv = moves.share_left(mixed_a_low)
    qkv_bias = jnp.concatenate([b_q, jnp.zeros((D,), jnp.float32), b_v])
    qkv_low = (matmul(mixed_a_low, w_qkv) + qkv_bias).astype(LOW)
    queries = qkv_low[..., :D]
    near_kv = qkv_low[..., D:]
    far_kv = passed_along(near_kv, "blk", 1)
    near_s = score_block(queries, near_kv)
    far_s = score_block(queries, far_kv)
    row_top = jnp.maximum(jnp.max(near_s, axis=-1), jnp.max(far_s, axis=-1))
    row_total = jnp.sum(jnp.exp(near_s - row_top[..., None]), axis=-1) + jnp.sum(
        jnp.exp(far_s - row_top[..., None]), axis=-1
    )
    log_sum = row_top + jnp.log(row_total)
    attended = weigh_values(jnp.exp(near_s - log_sum[..., None]), near_kv) + weigh_values(
        jnp.exp(far_s - log_sum[..., None]), far_kv
    )
    att_low = attended.astype(LOW)
    left_proj = moves.share_left(att_low)
    branch_a = matmul(att_low, w_proj) + b_proj
    residual = hidden_f + gate_a[:, None, :] * branch_a
    mixed_m, pull_m = jax.vjp(modulate, residual, scale_m, shift_m)
    mixed_m_low = mixed_m.astype(LOW)
    left_up = moves.share_left(mixed_m_low)
    pre_act = matmul(mixed_m_low, w_up) + b_up
    activated, gelu_pull = jax.vjp(gelu_tanh, pre_act)
    act_low = activated.astype(LOW)
    left_down = moves.share_left(act_low)
    branch_m = matmul(act_low, w_down) + b_down
    output = residual + gate_m[:, None, :] * branch_m
    out_low = output.astype(LOW)
    left_one = moves.share_left(out_low)
    hid_one = matmul(out_low, w_one) + c_one
    act_one, silu_one = jax.vjp(jax.nn.silu, hid_one)
    one_low = act_one.astype(LOW)
    left_two = moves.share_left(one_low)
    hid_two = matmul(one_low, w_two) + c_two
    act_two, silu_two = jax.vjp(jax.nn.silu, hid_two)
    two_low = act_two.astype(LOW)
    left_three = moves.share_left(two_low)
    projection = matmul(two_low, w_three) + c_three
    live_f = live_slots.astype(jnp.float32)[:, None, None]
    unit_proj, unit_pull = jax.vjp(rms_unit, projection)
    grad_proj = unit_pull(-LAMBDA_REPA * live_f * rms_unit(targets.astype(jnp.float32)))[0].astype(
        LOW
    )
    grad_pthree = moves.weight_grad(left_three, grad_proj)
    grad_cthree = column_sum(grad_proj)
    grad_htwo = silu_two(matmul_t(grad_proj, w_three))[0].astype(LOW)
    grad_ptwo = moves.weight_grad(left_two, grad_htwo)
    grad_ctwo = column_sum(grad_htwo)
    grad_hone = silu_one(matmul_t(grad_htwo, w_two))[0].astype(LOW)
    grad_pone = moves.weight_grad(left_one, grad_hone)
    grad_cone = column_sum(grad_hone)
    grad_output = cotangent.astype(jnp.float32) * live_f + matmul_t(grad_hone, w_one)
    grad_gate_m = jnp.sum(grad_output * branch_m, axis=1)
    grad_bm = (gate_m[:, None, :] * grad_output).astype(LOW)
    grad_wdown = moves.weight_grad(left_down, grad_bm)
    grad_bdown = column_sum(grad_bm)
    grad_pre = gelu_pull(matmul_t(grad_bm, w_down))[0].astype(LOW)
    grad_wup = moves.weight_grad(left_up, grad_pre)
    grad_bup = column_sum(grad_pre)
    grad_res_m, grad_scale_m, grad_shift_m = pull_m(matmul_t(grad_pre, w_up))
    grad_residual = grad_output + grad_res_m
    grad_gate_a = jnp.sum(grad_residual * branch_a, axis=1)
    grad_ba = (gate_a[:, None, :] * grad_residual).astype(LOW)
    grad_wproj = moves.weight_grad(left_proj, grad_ba)
    grad_bproj = column_sum(grad_ba)
    grad_att = matmul_t(grad_ba, w_proj).astype(LOW)
    near_p, near_dp = grad_block(queries, near_kv, log_sum, grad_att)
    far_p, far_dp = grad_block(queries, far_kv, log_sum, grad_att)
    row_delta = jnp.sum(near_p * near_dp, axis=-1) + jnp.sum(far_p * far_dp, axis=-1)
    near_ds = (near_p * (near_dp - row_delta[..., None])).astype(LOW)
    far_ds = (far_p * (far_dp - row_delta[..., None])).astype(LOW)
    grad_query = (key_product(near_ds, near_kv) + key_product(far_ds, far_kv)) * E ** (-0.5)
    far_dkv = kv_grads(far_ds, far_p, queries, grad_att)
    home_dkv = passed_along(far_dkv.astype(LOW), "blk", -1).astype(far_dkv.dtype)
    near_dkv = kv_grads(near_ds, near_p, queries, grad_att)
    grad_qkv = jnp.concatenate([grad_query, near_dkv + home_dkv], axis=-1).astype(LOW)
    grad_wqkv = moves.weight_grad(left_qkv, grad_qkv)
    qkv_sums = column_sum(grad_qkv)
    grad_hid_a, grad_scale_a, grad_shift_a = pull_a(matmul_t(grad_qkv, w_qkv))
    grad_input = grad_residual + grad_hid_a
    grad_mod_part = jnp.concatenate(
        [grad_shift_a, grad_scale_a, grad_gate_a, grad_shift_m, grad_scale_m, grad_gate_m], axis=1
    )
    bias_terms = (
        qkv_sums[:D],
        qkv_sums[2 * D :],
        grad_bproj,
        grad_bup,
        grad_bdown,
        grad_cone,
        grad_ctwo,
        grad_cthree,
    )
    bias_grid = jnp.concatenate(
        [segment.reshape(blocks, -1) for segment in bias_terms], axis=1
    ).reshape(-1)
    grad_small = jnp.concatenate([grad_mod_part.reshape(-1), bias_grid])
    grad_small = (grad_small + lax.ppermute(grad_small, "blk", SWAP)).astype(LOW)
    small_all = moves.gather_slots(grad_small)
    mod_len = slots * 6 * D
    grad_mod = small_all[:, :mod_len].reshape(blocks * slots, 6 * D)
    grad_wada = jnp.einsum("si,sj->ij", cond_own, grad_mod, preferred_element_type=jnp.float32)
    grad_bada = lax.dynamic_index_in_dim(
        jnp.sum(grad_mod.astype(jnp.float32), axis=0).reshape(blocks, -1),
        moves.own_row,
        0,
        keepdims=False,
    )
    bias_own = jnp.sum(
        lax.dynamic_index_in_dim(
            small_all[:, mod_len:].reshape(blocks, blocks, -1), moves.own_row, 1, keepdims=False
        ).astype(jnp.float32),
        axis=0,
    )
    ada_at = (3 * D + FF + D) // blocks
    grad_b_flat = jnp.concatenate([bias_own[:ada_at], grad_bada, bias_own[ada_at:]])
    cond_cols = matmul_t(grad_mod, p_ada).reshape(blocks, slots, rows_d)
    cond_rows = moves.rows_in_order(moves.slots_seen_from(moves.gather_slots(cond_cols)))
    grad_cond = silu_cond(cond_rows.transpose(1, 0, 2).reshape(slots, D))[0]
    grad_w_flat = jnp.concatenate(
        [
            part.reshape(-1)
            for part in (
                grad_wqkv,
                grad_wproj,
                grad_wup,
                grad_wdown,
                grad_wada,
                grad_pone,
                grad_ptwo,
                grad_pthree,
            )
        ]
    )
    images_all = slots * blocks
    tokens_img = local_tok * lax.axis_size("blk")
    rate_w = LR_COEF / math.sqrt(images_all * tokens_img)
    rate_b = BIAS_FACTOR * rate_w
    mom_w = MOMENTUM * weight_momentum + grad_w_flat
    new_w = weights - rate_w * (grad_w_flat + MOMENTUM * mom_w)
    avg_w = AVERAGE * weight_average + (1.0 - AVERAGE) * new_w
    mom_b = MOMENTUM * bias_momentum + grad_b_flat
    new_b = biases - rate_b * (grad_b_flat + MOMENTUM * mom_b)
    avg_b = AVERAGE * bias_average + (1.0 - AVERAGE) * new_b
    return (
        out_low,
        grad_input,
        grad_cond,
        mom_w,
        new_w,
        new_w.astype(LOW),
        avg_w,
        mom_b,
        new_b,
        new_b.astype(LOW),
        avg_b,
    )


def solution(mesh):
    in_specs = (
        P(("inner", "outer"), "blk", None),
        P(("inner", "outer")),
        P(("inner", "outer")),
        P(("inner", "outer")),
        P(),
        P(("inner", "outer"), "blk", None),
        P(("inner", "outer"), "blk", None),
        P(("inner", "outer")),
        P(("inner", "outer")),
        P(("inner", "outer")),
        P(("inner", "outer")),
        P(("inner", "outer")),
        P(("inner", "outer")),
    )
    out_specs = (
        P(("inner", "outer"), "blk", None),
        P(("inner", "outer"), "blk", None),
        P(("inner", "outer"), None),
        P(("inner", "outer")),
        P(("inner", "outer")),
        P(("inner", "outer")),
        P(("inner", "outer")),
        P(("inner", "outer")),
        P(("inner", "outer")),
        P(("inner", "outer")),
        P(("inner", "outer")),
    )
    return jax.shard_map(body, mesh=mesh, in_specs=in_specs, out_specs=out_specs, check_vma=False)
```

```python
import functools
import math

import jax
import jax.numpy as jnp
from jax import lax
from jax.experimental import pallas as pl
from jax.experimental.pallas import tpu as pltpu
from jax.sharding import PartitionSpec as P

E = 72
D = 1152
FF = 4608
PH = 2048
ZD = 768


LAMBDA_REPA = 0.5
MOMENTUM = 0.5
AVERAGE = 0.5
LR_COEF = 0.04
BIAS_FACTOR = 4.0
EPS_NORM = 1e-06
GROUP = ("inner", "outer")
EVERY = ("blk", "inner", "outer")
LOW = jnp.bfloat16


def passed_along(block, axis, distance):
    devices = range(lax.axis_size(axis))
    route = [((i - distance) % len(devices), i) for i in devices]
    return lax.ppermute(block, axis, route)


def mat_shapes():
    return [(D, 3 * D), (D, D), (D, FF), (FF, D), (D, 6 * D), (D, PH), (PH, PH), (PH, ZD)]


def bias_shapes():
    return [(D,), (D,), (D,), (FF,), (D,), (6 * D,), (PH,), (PH,), (ZD,)]


def split_shard(flat_vec, shapes, blocks):
    segments = []
    offset = 0
    for shape_now in shapes:
        rows_here = shape_now[0] // blocks
        length = rows_here * math.prod(shape_now[1:])
        segments.append(
            flat_vec[offset : offset + length].reshape((rows_here,) + tuple(shape_now[1:]))
        )
        offset += length
    return segments


def unpack_rows(line_grid, shapes):
    blocks = line_grid.shape[0]
    segments = []
    offset = 0
    for shape_now in shapes:
        length = shape_now[0] // blocks * math.prod(shape_now[1:])
        segments.append(line_grid[:, offset : offset + length].reshape(shape_now))
        offset += length
    return segments


def flat_id(core, z_at, outer_at):
    return (core * 4 + z_at) * 4 + outer_at


def route_z(pairs_core0):
    route = []
    for z_from, z_to in pairs_core0:
        for outer_at in range(4):
            route.append((flat_id(0, z_from, outer_at), flat_id(0, z_to, outer_at)))
            route.append((flat_id(1, 3 - z_from, outer_at), flat_id(1, 3 - z_to, outer_at)))
    return route


def flipped(route):
    return [(target, source) for source, target in route]


def route_xy(step_core0, step_core1):
    route = []
    for z_at in range(4):
        for outer_at in range(4):
            for core, step in ((0, step_core0), (1, step_core1)):
                route.append((flat_id(core, z_at, outer_at), flat_id(core, z_at, outer_at ^ step)))
    return route


STEP_X, STEP_Y = 1, 2
NEAR_FIRST = route_xy(STEP_X, STEP_Y)
NEAR_SECOND = route_xy(STEP_Y, STEP_X)
Z_PAIR = [(0, 1), (1, 0), (2, 3), (3, 2)]
Z_STRAIGHT = route_z([(0, 2), (1, 3)])
SWAP = [(0, 1), (1, 0)]
UP = [(0, 1), (1, 2), (2, 3), (3, 0)]
DOWN = [(1, 0), (2, 1), (3, 2), (0, 3)]
ACROSS = [(0, 2), (2, 0), (1, 3), (3, 1)]
OUT_X = [(0, 1), (1, 0), (2, 3), (3, 2)]
OUT_Y = [(0, 2), (2, 0), (1, 3), (3, 1)]
OUT_XY = [(0, 3), (3, 0), (1, 2), (2, 1)]


def after(value, *others):
    return lax.optimization_barrier((value,) + others)[0]


def columns_of(widths):
    found, start = [], 0
    for width in widths:
        found.append((start, width))
        start += width
    return found


def move_blocks(table, sources, outs, plan, name):
    rows = sources[0].shape[1]
    low = sources[0].dtype
    widths = [columns[1] for _, _, columns, _, _, _ in plan]
    total = sum(widths)

    def kernel(table_ref, *refs):
        source_refs = refs[: len(sources)]
        out_refs = refs[len(sources) : len(sources) + len(outs)]
        held, sems_in, sems_out = refs[len(sources) + len(outs) :]
        arriving, leaving = [], []
        start = 0
        for number, (source_at, index, columns, out_at, out_index, out_columns) in enumerate(plan):
            from_row = table_ref[number] if index is None else index
            to_row = table_ref[number] if out_index is None else out_index
            here = held.at[:, pl.ds(start, columns[1])]
            start += columns[1]
            arriving.append(
                pltpu.make_async_copy(
                    source_refs[source_at].at[from_row, :, pl.ds(*columns)],
                    here,
                    sems_in.at[number],
                )
            )
            leaving.append(
                pltpu.make_async_copy(
                    here,
                    out_refs[out_at].at[to_row, :, pl.ds(*out_columns)],
                    sems_out.at[number],
                )
            )
        for copy in arriving:
            copy.start()
        for copy_in, copy_out in zip(arriving, leaving):
            copy_in.wait()
            copy_out.start()
        for copy in leaving:
            copy.wait()

    count = len(plan)
    return pl.pallas_call(
        kernel,
        out_shape=[jax.ShapeDtypeStruct((length, rows, width), low) for length, width in outs],
        grid_spec=pltpu.PrefetchScalarGridSpec(
            num_scalar_prefetch=1,
            grid=(1,),
            in_specs=[pl.BlockSpec(memory_space=pl.ANY)] * len(sources),
            out_specs=[pl.BlockSpec(memory_space=pl.ANY)] * len(outs),
            scratch_shapes=[
                pltpu.VMEM((rows, total), low),
                pltpu.SemaphoreType.DMA((count,)),
                pltpu.SemaphoreType.DMA((count,)),
            ],
        ),
        compiler_params=pltpu.CompilerParams(vmem_limit_bytes=32 * 1024 * 1024),
        name=name,
    )(table, *sources)


def updated(grad, weight, momentum, average, rate):
    momentum = MOMENTUM * momentum + grad
    weight = weight - rate * (grad + MOMENTUM * momentum)
    return momentum, weight, weight.astype(LOW), AVERAGE * average + (1.0 - AVERAGE) * weight


def update_rows(pieces, state, at, rate, results):
    counts = [grad.shape[0] * width // 128 for grad, _, width in pieces]
    count = sum(counts)
    chunk = 144 if count % 144 == 0 else 128
    total = state[0].shape[0]
    given = [] if results is None else list(results)
    number_of = len(pieces)

    def kernel(*refs):
        grad_refs = refs[:number_of]
        weight_ref, momentum_ref, average_ref = refs[number_of : number_of + 3]
        refs = refs[number_of + 3 + len(given) :]
        outs, arrived = refs[:4], refs[4 : 4 + number_of]
        grad_flat, weight, momentum, average, low, sems = refs[4 + number_of :]
        window = pl.ds(at, count)
        fetched = [
            pltpu.make_async_copy(grad_ref.at[:, pl.ds(start, width)], held, sems.at[3 + number])
            for number, (grad_ref, held, (_, start, width)) in enumerate(
                zip(grad_refs, arrived, pieces)
            )
        ]
        copies = [
            pltpu.make_async_copy(weight_ref.at[window], weight, sems.at[0]),
            pltpu.make_async_copy(momentum_ref.at[window], momentum, sems.at[1]),
            pltpu.make_async_copy(average_ref.at[window], average, sems.at[2]),
        ]
        for copy in fetched + copies:
            copy.start()
        offset = 0
        for copy, held, (grad, _, width) in zip(fetched, arrived, pieces):
            copy.wait()
            rows, per_row = grad.shape[0], width // 128
            for at_now in range(per_row):
                grad_flat[pl.ds(offset + at_now, rows, stride=per_row), :] = held[
                    :, pl.ds(at_now * 128, 128)
                ].astype(jnp.float32)
            offset += rows * per_row
        for copy in copies:
            copy.wait()

        def step(number, carry):
            here = pl.ds(pl.multiple_of(number * chunk, 16), chunk)
            momentum[here], weight[here], low[here], average[here] = updated(
                grad_flat[here], weight[here], momentum[here], average[here], rate
            )
            return carry

        lax.fori_loop(0, count // chunk, step, 0)
        copies = [
            pltpu.make_async_copy(held, out.at[window], sems.at[number])
            for number, (held, out) in enumerate(zip((momentum, weight, low, average), outs))
        ]
        for copy in copies:
            copy.start()
        for copy in copies:
            copy.wait()

    flat = pltpu.VMEM((count, 128), jnp.float32)
    return pl.pallas_call(
        kernel,
        in_specs=[pl.BlockSpec(memory_space=pl.ANY)] * number_of
        + [pl.BlockSpec(memory_space=pltpu.HBM)] * (3 + len(given)),
        out_specs=[pl.BlockSpec(memory_space=pltpu.HBM)] * 4,
        out_shape=[
            jax.ShapeDtypeStruct((total, 128), kind)
            for kind in (jnp.float32, jnp.float32, LOW, jnp.float32)
        ],
        input_output_aliases={number_of + 3 + number: number for number in range(len(given))},
        scratch_shapes=[
            pltpu.VMEM((grad.shape[0], width), grad.dtype) for grad, _, width in pieces
        ]
        + [flat, flat, flat, flat, pltpu.VMEM((count, 128), LOW)]
        + [pltpu.SemaphoreType.DMA((3 + max(number_of, 1),))],
        compiler_params=pltpu.CompilerParams(vmem_limit_bytes=57 * 1024 * 1024),
        name="update_rows",
    )(*[grad for grad, _, _ in pieces], *state, *given)


def place_blocks(sources, table, widths):
    plan, places = [], []
    for out_at, columns in enumerate(columns_of(widths)):
        number = 0
        for source_at, source in enumerate(sources):
            for at in range(source.shape[0]):
                plan.append((source_at, at, columns, out_at, None, (0, columns[1])))
                places.append(table[number])
                number += 1
    outs = [(16, width) for width in widths]
    return move_blocks(jnp.stack(places).astype(jnp.int32), sources, outs, plan, "place_blocks")


def pick_blocks(sources, table):
    widths = [source.shape[-1] for source in sources]
    plan, places = [], []
    for number in range(8):
        for source_at, columns in enumerate(columns_of(widths)):
            plan.append(
                (source_at, None, (0, columns[1]), number // 4, number % 4, columns)
            )
            places.append(table[number])
    outs = [(4, sum(widths)), (4, sum(widths))]
    return move_blocks(jnp.stack(places).astype(jnp.int32), sources, outs, plan, "pick_blocks")


class Staged:
    def __init__(self):
        self.core = lax.axis_index("blk")
        self.z_at = lax.axis_index("inner")
        outer_at = lax.axis_index("outer")
        self.y_at = outer_at // 2
        self.x_at = outer_at % 2
        self.own_half = (self.z_at // 2) == self.core
        self.own_row = self.z_at * 4 + outer_at

    def z_pair(self, core):
        low_bit = self.z_at % 2
        return 2 * core + low_bit, 2 * core + 1 - low_bit

    def near_order(self, core, picks):
        found = []
        for far, near in picks:
            first = jnp.where(core == 0, self.x_at, self.y_at) ^ near
            second = jnp.where(core == 0, self.y_at, self.x_at) ^ far
            y_now = jnp.where(core == 0, second, first)
            x_now = jnp.where(core == 0, first, second)
            found.append(y_now * 2 + x_now)
        return found

    def gather_groups(self, groups, gates, early):
        packed = [
            group[0] if len(group) == 1 else jnp.concatenate(group, axis=1) for group in groups
        ]
        table = []
        for core in (self.core, 1 - self.core):
            for outer_at in self.near_order(core, [(0, 0), (0, 1), (1, 0), (1, 1)]):
                for z_now in self.z_pair(core):
                    table.append(z_now * 4 + outer_at)
        last = len(groups) - 1
        held, others, twos, fours, tokens = {}, {}, {}, {}, {}

        def first_stage(k, gates, late):
            own = after(packed[k], *gates)
            came = after(lax.ppermute(own, EVERY, Z_STRAIGHT), *late)
            held[k] = jnp.where(self.own_half, own, came)
            others[k] = lax.ppermute(held[k], "inner", Z_PAIR)

        def second_stage(k, late):
            twos[k] = jnp.stack([held[k], after(others[k], *late)])

        def third_stage(k, late):
            came = after(lax.ppermute(twos[k], EVERY, NEAR_FIRST), *late)
            fours[k] = jnp.concatenate([twos[k], came])

        first_stage(0, (), early[0]())
        second_stage(0, early[1]())
        first_stage(1, (held[0],), (twos[0],))
        third_stage(0, early[2](twos[0]))
        second_stage(1, (fours[0],))
        for k in range(len(groups)):
            if k + 1 < last:
                first_stage(k + 2, (twos[k + 1],), ())
            far_four = lax.ppermute(fours[k], EVERY, NEAR_SECOND)
            mate_four = lax.ppermute(fours[k], "blk", SWAP)
            if k < last:
                far_four = after(far_four, twos[k + 1])
            else:
                far_four = after(far_four, tokens[k - 1])
            if k < last:
                third_stage(k + 1, (far_four,))
            mate_far = lax.ppermute(far_four, "blk", SWAP)
            if k < last:
                mate_far = after(mate_far, fours[k + 1])
            sources = [fours[k], far_four, mate_four, mate_far]
            widths = [part.shape[1] for part in groups[k]]
            tokens[k] = gates[k](
                [part.reshape(-1, part.shape[-1]) for part in place_blocks(sources, table, widths)]
            )
            if k + 1 < last:
                second_stage(k + 2, (tokens[k],))

    def share_left(self, left):
        half = left.shape[-1] // 2
        tokens = left.reshape(-1, left.shape[-1])
        keep = lax.dynamic_slice_in_dim(tokens, self.core * half, half, 1)
        give = lax.dynamic_slice_in_dim(tokens, (1 - self.core) * half, half, 1)
        return jnp.concatenate([keep, lax.ppermute(give, "blk", SWAP)])

    def share_right(self, right):
        tokens = right.reshape(-1, right.shape[-1])
        return jnp.concatenate([tokens, lax.ppermute(tokens, "blk", SWAP)])

    def start_grads(self, pairs):
        return StagedGrads(self, pairs)

    def update(self, state, rate, parts):
        lanes = [array.reshape(-1, 128) for array in state]
        sizes = [rows * cols // (16 * 128) for rows, cols in mat_shapes()]
        results = None
        for entries in parts:
            if isinstance(entries[0][0], StagedGrads) and entries[0][0].stage == 3:
                entries[0][0].add(results[0])
            pieces = []
            for part, start, number in entries:
                grad = part.both if isinstance(part, StagedGrads) else part
                pieces.append((grad, start, mat_shapes()[number][1]))
            first = entries[0][2]
            results = update_rows(pieces, lanes, sum(sizes[:first]), rate, results)
        return [result.reshape(-1) for result in results]

    def gather_slots(self, own, between=None):
        four = jnp.concatenate(
            [own] + [lax.ppermute(own, "inner", route) for route in (UP, DOWN, ACROSS)]
        )
        self.token = four
        if between is not None:
            four = after(four, between())
        return jnp.concatenate(
            [four] + [lax.ppermute(four, "outer", route) for route in (OUT_X, OUT_Y, OUT_XY)]
        )

    def swap_slots(self, parts, between):
        parts = parts.reshape((4, 4) + parts.shape[1:])
        four = jnp.stack(
            [parts[0]]
            + [
                lax.ppermute(parts[1 + at], "outer", route)
                for at, route in enumerate((OUT_X, OUT_Y, OUT_XY))
            ]
        )
        four = after(four, between())
        return jnp.stack(
            [four[:, 0]]
            + [
                lax.ppermute(four[:, 1 + at], "inner", route)
                for at, route in enumerate((DOWN, UP, ACROSS))
            ],
        )

    def reduce_slots(self, parts, late):
        parts = parts.reshape((4, 4) + parts.shape[1:])
        four = parts[0]
        for at, route in enumerate((OUT_X, OUT_Y, OUT_XY)):
            four = four + after(lax.ppermute(parts[1 + at], "outer", route), late)
        self.token = four
        total = four[0]
        for at, route in enumerate((DOWN, UP, ACROSS)):
            total = total + lax.ppermute(four[1 + at], "inner", route)
        return total

    def slot_rows(self):
        found = []
        for z_now in range(4):
            away = (z_now - self.z_at) % 4
            z_slot = jnp.where(away == 0, 0, jnp.where(away == 3, 1, jnp.where(away == 1, 2, 3)))
            for outer_now in range(4):
                flip = jnp.bitwise_xor(outer_now, self.y_at * 2 + self.x_at)
                found.append((flip, z_slot))
        return found

    def rows_in_order(self, slots):
        table = [flip * 4 + z_slot for flip, z_slot in self.slot_rows()]
        return jnp.take(slots, jnp.stack(table), axis=0)

    def swapped_in_order(self, came):
        table = []
        for flip, z_slot in self.slot_rows():
            came_at = jnp.where(z_slot == 1, 2, jnp.where(z_slot == 2, 1, z_slot))
            table.append(came_at * 4 + flip)
        return jnp.take(came.reshape(16, -1), jnp.stack(table), axis=0)


class StagedGrads:
    def __init__(self, moves, pairs):
        self.moves = moves
        self.widths = [right.shape[-1] for _, right in pairs]
        blocks = []
        for left, right in pairs:
            grad = jnp.einsum("ni,nj->ij", left, right, preferred_element_type=jnp.float32)
            blocks.append(grad.astype(LOW).reshape(8, -1, grad.shape[-1]))
        low_bit = moves.z_at % 2
        table = []
        for outer_at in moves.near_order(moves.core, [(1, 1), (1, 0), (0, 1), (0, 0)]):
            for z_now in (low_bit, 1 - low_bit):
                table.append(z_now * 4 + outer_at)
        self.give, self.keep = pick_blocks(blocks, table)
        self.token = self.give
        self.stage = 0

    def send(self, *gates):
        self.give = after(self.give, *gates) if gates else self.give
        axes, route = (
            (EVERY, NEAR_SECOND),
            (EVERY, NEAR_FIRST),
            ("inner", Z_PAIR),
            (EVERY, flipped(Z_STRAIGHT)),
        )[self.stage]
        self.came = lax.ppermute(self.give, axes, route)

    def add(self, *late):
        came = after(self.came, *late) if late else self.came
        total = self.keep.astype(jnp.float32) + came.astype(jnp.float32)
        if self.stage == 0:
            self.give = total[:2].astype(LOW)
            self.keep = total[2:].astype(LOW)
        elif self.stage == 1:
            self.give = total[1].astype(LOW)
            self.keep = total[0].astype(LOW)
        else:
            self.give = self.keep = total.astype(LOW)
        if self.stage == 3:
            mate = lax.ppermute(self.give, "blk", SWAP)
            self.both = jnp.where(self.moves.own_half, self.give, mate)
        self.token = self.give
        self.stage += 1


def outer_sum(left_arr, right_arr):
    return jnp.einsum("sni,snj->ij", left_arr, right_arr, preferred_element_type=jnp.float32)


class DirectGrads:
    def __init__(self, pairs):
        self.parts = [outer_sum(left, right).astype(LOW) for left, right in pairs]
        self.token = self.parts[0]

    def send(self, *gates):
        pass

    def add(self, *late):
        pass

    @functools.cached_property
    def result(self):
        found = []
        for grad in self.parts:
            part = lax.psum_scatter(grad, GROUP, scatter_dimension=0, tiled=True)
            found.append(lax.psum(part, "blk").astype(jnp.float32))
        return found


class Direct:
    def __init__(self):
        self.core = lax.axis_index("blk")
        self.own_row = lax.axis_index("inner") * lax.axis_size("outer") + lax.axis_index("outer")

    def gather_groups(self, groups, gates, early):
        early[0]()
        early[1]()
        early[2](groups[0][0])
        for group, gate in zip(groups, gates):
            gate([lax.all_gather(part, GROUP, axis=0, tiled=True) for part in group])

    def share_left(self, left):
        return left

    def share_right(self, right):
        return right

    def start_grads(self, pairs):
        return DirectGrads(pairs)

    def update(self, state, rate, parts):
        found = {}
        for part, start, number in sum(parts, []):
            whole = jnp.concatenate(part.result, axis=1) if isinstance(part, DirectGrads) else part
            found[number] = whole[:, start : start + mat_shapes()[number][1]]
        grad = jnp.concatenate([found[number].reshape(-1) for number in sorted(found)])
        return updated(grad, *state, rate)

    def gather_slots(self, own, between=None):
        self.token = own
        if between is not None:
            between()
        return lax.all_gather(own, GROUP, axis=0, tiled=True)

    def reduce_slots(self, parts, late):
        self.token = parts
        return lax.psum_scatter(parts, GROUP, scatter_dimension=0, tiled=False)

    def swap_slots(self, parts, between):
        between()
        return lax.all_gather(parts, GROUP, axis=0)

    def rows_in_order(self, slots):
        return slots

    def swapped_in_order(self, came):
        mine = lax.dynamic_index_in_dim(came, self.own_row, 1, keepdims=False)
        return mine.reshape(mine.shape[0], -1)


def time_embed(steps_t):
    half_dim = D // 2
    frequency = jnp.exp(-math.log(10000.0) * jnp.arange(half_dim, dtype=jnp.float32) / half_dim)
    angles = steps_t.astype(jnp.float32)[:, None] * frequency[None, :]
    return jnp.concatenate([jnp.cos(angles), jnp.sin(angles)], axis=1)


def modulate(values, scale_v, shift_v):
    center = values - jnp.mean(values, axis=-1, keepdims=True)
    normed = center * lax.rsqrt(jnp.mean(center * center, axis=-1, keepdims=True) + EPS_NORM)
    return normed * (1.0 + scale_v[:, None, :]) + shift_v[:, None, :]


def gelu_tanh(values):
    return jax.nn.gelu(values, approximate=True)


def rms_unit(values):
    return values * lax.rsqrt(jnp.mean(values * values, axis=-1, keepdims=True) + EPS_NORM)


def matmul(left_arr, right_arr):
    return jnp.einsum("...i,ij->...j", left_arr, right_arr, preferred_element_type=jnp.float32)


def matmul_t(left_arr, right_arr):
    return jnp.einsum("...j,ij->...i", left_arr, right_arr, preferred_element_type=jnp.float32)


def column_sum(tensor):
    return jnp.sum(tensor.astype(jnp.float32), axis=(0, 1))


def attention(queries, near_kv, far_kv):
    images, rows, _ = queries.shape
    heads = D // E

    def kernel(q_ref, near_ref, far_ref, out_ref):
        for head in range(heads):
            own = pl.ds(head * E, E)
            other = pl.ds(D + head * E, E)
            q_now = q_ref[0, :, own]
            keys = jnp.concatenate([near_ref[0, :, own], far_ref[0, :, own]], axis=0)
            values = jnp.concatenate([near_ref[0, :, other], far_ref[0, :, other]], axis=0)
            scores = dot_nt(keys, q_now) * E ** (-0.5)
            top = jnp.max(scores, axis=0, keepdims=True)
            weight = jnp.exp(scores - top)
            probs = weight * (1.0 / jnp.sum(weight, axis=0, keepdims=True))
            out_ref[0, :, own] = dot_tn(probs.astype(LOW), values).astype(LOW)

    block = pl.BlockSpec((1, rows, D), lambda i: (i, 0, 0))
    block_kv = pl.BlockSpec((1, rows, 2 * D), lambda i: (i, 0, 0))
    return pl.pallas_call(
        kernel,
        grid=(images,),
        in_specs=[block, block_kv, block_kv],
        out_specs=block,
        out_shape=jax.ShapeDtypeStruct(queries.shape, LOW),
        compiler_params=pltpu.CompilerParams(vmem_limit_bytes=32 * 1024 * 1024),
        name="attention",
    )(queries, near_kv, far_kv)


def attention_grads(queries, near_kv, far_kv, grad_att):
    images, rows, _ = queries.shape
    heads = D // E

    def kernel(q_ref, near_ref, far_ref, grad_ref, dq_ref, dnear_ref, dfar_ref):
        for head in range(heads):
            own = pl.ds(head * E, E)
            other = pl.ds(D + head * E, E)
            q_now = q_ref[0, :, own]
            g_now = grad_ref[0, :, own]
            keys = jnp.concatenate([near_ref[0, :, own], far_ref[0, :, own]], axis=0)
            values = jnp.concatenate([near_ref[0, :, other], far_ref[0, :, other]], axis=0)
            scores = dot_nt(keys, q_now) * E ** (-0.5)
            top = jnp.max(scores, axis=0, keepdims=True)
            weight = jnp.exp(scores - top)
            probs = weight * (1.0 / jnp.sum(weight, axis=0, keepdims=True))
            grad_probs = dot_nt(values, g_now)
            delta = jnp.sum(probs * grad_probs, axis=0, keepdims=True)
            grad_scores = (probs * (grad_probs - delta)).astype(LOW)
            dq_ref[0, :, own] = (dot_tn(grad_scores, keys) * E ** (-0.5)).astype(LOW)
            grad_keys = dot_nn(grad_scores, q_now) * E ** (-0.5)
            grad_values = dot_nn(probs.astype(LOW), g_now)
            dnear_ref[0, :, own] = grad_keys[:rows]
            dnear_ref[0, :, other] = grad_values[:rows]
            dfar_ref[0, :, own] = grad_keys[rows:].astype(LOW)
            dfar_ref[0, :, other] = grad_values[rows:].astype(LOW)

    block = pl.BlockSpec((1, rows, D), lambda i: (i, 0, 0))
    block_kv = pl.BlockSpec((1, rows, 2 * D), lambda i: (i, 0, 0))
    return pl.pallas_call(
        kernel,
        grid=(images,),
        in_specs=[block, block_kv, block_kv, block],
        out_specs=[block, block_kv, block_kv],
        out_shape=[
            jax.ShapeDtypeStruct(queries.shape, LOW),
            jax.ShapeDtypeStruct(near_kv.shape, jnp.float32),
            jax.ShapeDtypeStruct(far_kv.shape, LOW),
        ],
        compiler_params=pltpu.CompilerParams(vmem_limit_bytes=32 * 1024 * 1024),
        name="attention_grads",
    )(queries, near_kv, far_kv, grad_att)


def dot_nn(left, right):
    return lax.dot_general(
        left, right, (((1,), (0,)), ((), ())), preferred_element_type=jnp.float32
    )


def dot_nt(left, right):
    return lax.dot_general(
        left, right, (((1,), (1,)), ((), ())), preferred_element_type=jnp.float32
    )


def dot_tn(left, right):
    return lax.dot_general(
        left, right, (((0,), (0,)), ((), ())), preferred_element_type=jnp.float32
    )


def body(
    hidden,
    labels,
    steps_t,
    live_slots,
    label_table,
    targets,
    cotangent,
    weights,
    weight_momentum,
    weight_average,
    biases,
    bias_momentum,
    bias_average,
):
    n_inner = lax.axis_size("inner")
    n_outer = lax.axis_size("outer")
    blocks = n_inner * n_outer
    slots = hidden.shape[0]
    local_tok = hidden.shape[1]
    moves = Staged() if (n_inner, n_outer) == (4, 4) else Direct()
    p_qkv, p_proj, p_up, p_down, p_ada, p_one, p_two, p_three = split_shard(
        weights.astype(LOW), mat_shapes(), blocks
    )
    bias_low = biases.astype(LOW)
    condition = label_table[labels].astype(jnp.float32) + time_embed(steps_t)
    cond_act, silu_cond = jax.vjp(jax.nn.silu, condition)
    cond_low = cond_act.astype(LOW)
    kept = {}
    rows_d = D // blocks
    half_ada = 3 * D

    def early_gather():
        packed = jnp.concatenate([cond_low, bias_low.reshape(slots, -1)], axis=1)
        kept["packed"] = moves.gather_slots(packed)
        return (moves.token,)

    def early_product():
        packed_all = kept["packed"]
        cond_own = lax.dynamic_slice_in_dim(
            packed_all[:, :D], moves.own_row * rows_d, rows_d, 1
        )
        ada_half = lax.dynamic_slice_in_dim(p_ada, moves.core * half_ada, half_ada, 1)
        mod_part = matmul(cond_own, ada_half).reshape(blocks, slots, half_ada)
        kept.update(cond_own=cond_own, mod_part=mod_part)
        return (mod_part,)

    def early_modulation(gate):
        mod_half = moves.reduce_slots(kept["mod_part"], gate)
        late = moves.token
        mod_mate = lax.ppermute(mod_half, "blk", SWAP)
        bias_all = moves.rows_in_order(kept["packed"][:, D:].reshape(blocks, -1))
        biases_now = unpack_rows(bias_all.astype(jnp.float32), bias_shapes())
        b_ada = biases_now[5]
        kept["biases"] = biases_now
        modulation = (
            jnp.concatenate(
                [
                    jnp.where(moves.core == 0, mod_half, mod_mate),
                    jnp.where(moves.core == 0, mod_mate, mod_half),
                ],
                axis=1,
            )
            + b_ada
        )
        shift_a, scale_a, gate_a, shift_m, scale_m, gate_m = [
            modulation[:, part_idx * D : (part_idx + 1) * D] for part_idx in range(6)
        ]
        hidden_f = hidden.astype(jnp.float32)
        mixed_a, pull_a = jax.vjp(modulate, hidden_f, scale_a, shift_a)
        mixed_a_low = mixed_a.astype(LOW)
        left_qkv = moves.share_left(mixed_a_low)
        kept.update(
            gates=(gate_a, gate_m), scale_m=scale_m, shift_m=shift_m, hidden_f=hidden_f,
            mixed_a_low=mixed_a_low, pull_a=pull_a, left_qkv=left_qkv,
        )
        return (late,)

    def use_first(arrived):
        b_q, b_v = kept["biases"][:2]
        (w_qkv,) = arrived
        qkv_bias = jnp.concatenate([b_q, jnp.zeros((D,), jnp.float32), b_v])
        qkv_low = (matmul(kept["mixed_a_low"], w_qkv) + qkv_bias).astype(LOW)
        near_kv = qkv_low[..., D:]
        far_kv = passed_along(near_kv, "blk", 1)
        kept.update(w_qkv=w_qkv, queries=qkv_low[..., :D], near_kv=near_kv, far_kv=far_kv)
        return far_kv
    def use_second(arrived):
        w_proj, w_one = arrived
        b_proj = kept["biases"][2]
        queries, near_kv, far_kv = kept["queries"], kept["near_kv"], kept["far_kv"]
        queries = after(queries, w_proj)
        att_low = attention(queries, near_kv, far_kv)
        left_proj = moves.share_left(att_low)
        branch_a = matmul(att_low, w_proj) + b_proj
        residual = kept["hidden_f"] + kept["gates"][0][:, None, :] * branch_a
        mixed_m, pull_m = jax.vjp(modulate, residual, kept["scale_m"], kept["shift_m"])
        mixed_m_low = mixed_m.astype(LOW)
        left_up = moves.share_left(mixed_m_low)
        kept.update(
            w_proj=w_proj, w_one=w_one, left_proj=left_proj,
            branch_a=branch_a, residual=residual, pull_m=pull_m, left_up=left_up,
            mixed_m_low=mixed_m_low,
        )
        return mixed_m_low

    def use_third(arrived):
        (w_up,) = arrived
        b_up = kept["biases"][3]
        pre_act = matmul(kept["mixed_m_low"], w_up) + b_up
        activated, gelu_pull = jax.vjp(gelu_tanh, pre_act)
        act_low = activated.astype(LOW)
        left_down = moves.share_left(act_low)
        kept.update(w_up=w_up, gelu_pull=gelu_pull, act_low=act_low, left_down=left_down)
        return act_low

    def use_fourth(arrived):
        (w_down,) = arrived
        b_down, c_one = kept["biases"][4], kept["biases"][6]
        branch_m = matmul(kept["act_low"], w_down) + b_down
        output = kept["residual"] + kept["gates"][1][:, None, :] * branch_m
        out_low = output.astype(LOW)
        left_one = moves.share_left(out_low)
        hid_one = matmul(out_low, kept["w_one"]) + c_one
        act_one, silu_one = jax.vjp(jax.nn.silu, hid_one)
        one_low = act_one.astype(LOW)
        left_two = moves.share_left(one_low)
        kept.update(
            w_down=w_down, branch_m=branch_m, out_low=out_low, left_one=left_one,
            silu_one=silu_one, one_low=one_low, left_two=left_two,
        )
        return one_low

    def use_fifth(arrived):
        w_two, w_three = arrived
        c_two, c_three = kept["biases"][7:]
        hid_two = matmul(kept["one_low"], w_two) + c_two
        act_two, silu_two = jax.vjp(jax.nn.silu, hid_two)
        two_low = act_two.astype(LOW)
        left_three = moves.share_left(two_low)
        projection = matmul(two_low, w_three) + c_three
        kept.update(
            w_two=w_two, w_three=w_three, silu_two=silu_two, left_three=left_three,
            projection=projection,
        )

    moves.gather_groups(
        [[p_qkv], [p_proj, p_one], [p_up], [p_down], [p_two, p_three]],
        [use_first, use_second, use_third, use_fourth, use_fifth],
        [early_gather, early_product, early_modulation],
    )
    w_qkv, w_proj, w_up, w_down, w_one, w_two, w_three = [
        kept[name] for name in ("w_qkv", "w_proj", "w_up", "w_down", "w_one", "w_two", "w_three")
    ]
    gate_a, gate_m = kept["gates"]
    cond_own = kept["cond_own"]
    pull_a, left_qkv = kept["pull_a"], kept["left_qkv"]
    queries, near_kv, far_kv = [kept[name] for name in ("queries", "near_kv", "far_kv")]
    branch_a, branch_m, out_low, projection = [
        kept[name] for name in ("branch_a", "branch_m", "out_low", "projection")
    ]
    pull_m, gelu_pull, silu_one, silu_two = [
        kept[name] for name in ("pull_m", "gelu_pull", "silu_one", "silu_two")
    ]
    live_f = live_slots.astype(jnp.float32)[:, None, None]
    unit_proj, unit_pull = jax.vjp(rms_unit, projection)
    grad_proj = unit_pull(-LAMBDA_REPA * live_f * rms_unit(targets.astype(jnp.float32)))[0].astype(
        LOW
    )
    right_three = moves.share_right(grad_proj)
    grad_cthree = column_sum(grad_proj)
    grad_htwo = silu_two(matmul_t(grad_proj, w_three))[0].astype(LOW)
    right_two = moves.share_right(grad_htwo)
    grad_ctwo = column_sum(grad_htwo)
    grad_hone = silu_one(matmul_t(grad_htwo, w_two))[0].astype(LOW)
    right_one = moves.share_right(grad_hone)
    grads_fourth = moves.start_grads(
        [(kept["left_two"], right_two), (kept["left_three"], right_three)]
    )
    grad_cone = column_sum(grad_hone)
    grads_fourth.send()
    right_one = after(right_one, grads_fourth.token)
    grads_one = moves.start_grads([(kept["left_one"], right_one)])
    grads_one.send()
    grad_hone = after(grad_hone, grads_one.token)
    grad_output = cotangent.astype(jnp.float32) * live_f + matmul_t(grad_hone, w_one)
    grad_gate_m = jnp.sum(grad_output * branch_m, axis=1)
    grad_bm = (gate_m[:, None, :] * grad_output).astype(LOW)
    right_down = moves.share_right(grad_bm)
    grad_bdown = column_sum(grad_bm)
    grad_pre = gelu_pull(matmul_t(grad_bm, w_down))[0].astype(LOW)
    right_up = moves.share_right(grad_pre)
    grads_down = moves.start_grads([(kept["left_down"], right_down)])
    grad_bup = column_sum(grad_pre)
    grads_down.send()
    grads_fourth.add(grads_down.token)
    grads_fourth.send()
    grad_pre = after(grad_pre, grads_down.token, grads_fourth.token)
    grad_res_m, grad_scale_m, grad_shift_m = pull_m(matmul_t(grad_pre, w_up))
    grad_residual = grad_output + grad_res_m
    grad_gate_a = jnp.sum(grad_residual * branch_a, axis=1)
    grad_ba = (gate_a[:, None, :] * grad_residual).astype(LOW)
    right_proj = moves.share_right(grad_ba)
    grad_bproj = column_sum(grad_ba)
    grad_att = matmul_t(grad_ba, w_proj).astype(LOW)
    grads_one.add(grad_att)
    grads_one.send()
    grads_fourth.add(grad_att)
    grads_fourth.send()
    right_up = after(right_up, grads_fourth.token, grads_one.token)
    grads_up = moves.start_grads([(kept["left_up"], right_up), (kept["left_proj"], right_proj)])
    grads_up.send()
    grads_down.add(grads_up.token)
    grads_down.send()
    grads_one.add(grads_up.token)
    grads_one.send()
    grad_att = after(grad_att, grads_up.token, grads_down.token, grads_one.token)
    grad_query, near_dkv, far_dkv = attention_grads(queries, near_kv, far_kv, grad_att)
    home_dkv = passed_along(far_dkv, "blk", -1)
    grads_down.add(grad_query)
    grads_down.send()
    grads_fourth.add(grad_query)
    grads_fourth.send()
    grads_one.add(grad_query)
    grads_one.send()
    home_dkv = after(home_dkv, grads_down.token, grads_one.token, grads_fourth.token)
    grad_kv = (near_dkv + home_dkv.astype(jnp.float32)).astype(LOW)
    grad_qkv = jnp.concatenate([grad_query, grad_kv], axis=-1)
    grads_up.add(grad_kv)
    grads_up.send()
    right_qkv = after(moves.share_right(grad_qkv), grads_up.token)
    grads_first = moves.start_grads([(left_qkv, right_qkv)])
    qkv_sums = column_sum(grad_qkv)
    grads_first.send()
    grads_up.add(grads_first.token)
    grads_up.send()
    grads_down.add(grads_first.token)
    grads_down.send()
    grads_fourth.add(grads_first.token)
    grads_one.add(grads_first.token)
    grad_qkv = after(
        grad_qkv, grads_up.token, grads_down.token, grads_fourth.token, grads_one.token
    )
    grad_hid_a, grad_scale_a, grad_shift_a = pull_a(matmul_t(grad_qkv, w_qkv))
    grad_input = grad_residual + grad_hid_a
    grad_mod_part = jnp.concatenate(
        [grad_shift_a, grad_scale_a, grad_gate_a, grad_shift_m, grad_scale_m, grad_gate_m], axis=1
    )
    bias_terms = (
        qkv_sums[:D],
        qkv_sums[2 * D :],
        grad_bproj,
        grad_bup,
        grad_bdown,
        grad_cone,
        grad_ctwo,
        grad_cthree,
    )
    bias_grid = jnp.concatenate(
        [segment.reshape(blocks, -1) for segment in bias_terms], axis=1
    ).reshape(slots, -1)
    grad_small = jnp.concatenate([grad_mod_part, bias_grid], axis=1)
    small_came = lax.ppermute(grad_small, "blk", SWAP)
    grads_first.add(grad_small)
    grads_first.send()
    grad_small = (grad_small + after(small_came, grads_first.token)).astype(LOW)

    def between_levels():
        grads_up.add(grad_small)
        grads_up.send()
        grads_first.add(moves.token)
        grads_first.send()
        return lax.optimization_barrier((grads_first.token, grads_up.token))[0]

    def between_swaps():
        grads_up.add()
        return grads_up.token

    small_all = moves.gather_slots(grad_small, between_levels)
    grads_first.add()
    grads_first.send()
    small_all = after(small_all, grads_first.token)
    grad_mod = small_all[:, : 6 * D]
    cond_cols = matmul_t(grad_mod, p_ada).reshape(blocks, slots, rows_d)
    cond_rows = moves.swapped_in_order(moves.swap_slots(cond_cols, between_swaps))
    grad_cond = silu_cond(
        cond_rows.reshape(blocks, slots, rows_d).transpose(1, 0, 2).reshape(slots, D)
    )[0]
    grad_wada = jnp.einsum("si,sj->ij", cond_own, grad_mod, preferred_element_type=jnp.float32)
    grad_bada = lax.dynamic_index_in_dim(
        jnp.sum(grad_mod.astype(jnp.float32), axis=0).reshape(blocks, -1),
        moves.own_row,
        0,
        keepdims=False,
    )
    bias_sums = jnp.sum(
        small_all[:, 6 * D :].astype(jnp.float32).reshape(blocks, slots, -1), axis=0
    )
    bias_own = lax.dynamic_index_in_dim(
        bias_sums.reshape(blocks, -1), moves.own_row, 0, keepdims=False
    )
    ada_at = (3 * D + FF + D) // blocks
    grad_b_flat = jnp.concatenate([bias_own[:ada_at], grad_bada, bias_own[ada_at:]])
    grads_down.add(grad_mod_part)
    images_all = slots * blocks
    tokens_img = local_tok * lax.axis_size("blk")
    rate_w = LR_COEF / math.sqrt(images_all * tokens_img)
    rate_b = BIAS_FACTOR * rate_w
    mom_w, new_w, low_w, avg_w = moves.update(
        (weights, weight_momentum, weight_average),
        rate_w,
        [
            [(grads_fourth, 0, 6)],
            [(grads_fourth, PH, 7)],
            [(grads_one, 0, 5)],
            [(grads_down, 0, 3)],
            [(grad_wada, 0, 4)],
            [(grads_up, 0, 2)],
            [(grads_first, 0, 0), (grads_up, FF, 1)],
        ],
    )
    mom_b = MOMENTUM * bias_momentum + grad_b_flat
    new_b = biases - rate_b * (grad_b_flat + MOMENTUM * mom_b)
    avg_b = AVERAGE * bias_average + (1.0 - AVERAGE) * new_b
    return (
        out_low,
        grad_input,
        grad_cond,
        mom_w,
        new_w,
        low_w,
        avg_w,
        mom_b,
        new_b,
        new_b.astype(LOW),
        avg_b,
    )


def solution(mesh):
    in_specs = (
        P(("inner", "outer"), "blk", None),
        P(("inner", "outer")),
        P(("inner", "outer")),
        P(("inner", "outer")),
        P(),
        P(("inner", "outer"), "blk", None),
        P(("inner", "outer"), "blk", None),
        P(("inner", "outer")),
        P(("inner", "outer")),
        P(("inner", "outer")),
        P(("inner", "outer")),
        P(("inner", "outer")),
        P(("inner", "outer")),
    )
    out_specs = (
        P(("inner", "outer"), "blk", None),
        P(("inner", "outer"), "blk", None),
        P(("inner", "outer"), None),
        P(("inner", "outer")),
        P(("inner", "outer")),
        P(("inner", "outer")),
        P(("inner", "outer")),
        P(("inner", "outer")),
        P(("inner", "outer")),
        P(("inner", "outer")),
        P(("inner", "outer")),
    )
    return jax.shard_map(body, mesh=mesh, in_specs=in_specs, out_specs=out_specs, check_vma=False)
```

```python
import functools
import math

import jax
import jax.numpy as jnp
from jax import lax
from jax.experimental import pallas as pl
from jax.experimental.pallas import tpu as pltpu
from jax.sharding import PartitionSpec as P

E = 72
D = 1152
FF = 4608
PH = 2048
ZD = 768


LAMBDA_REPA = 0.5
MOMENTUM = 0.5
AVERAGE = 0.5
LR_COEF = 0.04
BIAS_FACTOR = 4.0
EPS_NORM = 1e-06
GROUP = ("inner", "outer")
EVERY = ("blk", "inner", "outer")
LOW = jnp.bfloat16


def passed_along(block, axis, distance):
    devices = range(lax.axis_size(axis))
    route = [((i - distance) % len(devices), i) for i in devices]
    return lax.ppermute(block, axis, route)


def mat_shapes():
    return [(D, 3 * D), (D, D), (D, FF), (FF, D), (D, 6 * D), (D, PH), (PH, PH), (PH, ZD)]


def bias_shapes():
    return [(D,), (D,), (D,), (FF,), (D,), (6 * D,), (PH,), (PH,), (ZD,)]


def split_shard(flat_vec, shapes, blocks):
    segments = []
    offset = 0
    for shape_now in shapes:
        rows_here = shape_now[0] // blocks
        length = rows_here * math.prod(shape_now[1:])
        segments.append(
            flat_vec[offset : offset + length].reshape((rows_here,) + tuple(shape_now[1:]))
        )
        offset += length
    return segments


def unpack_rows(line_grid, shapes):
    blocks = line_grid.shape[0]
    segments = []
    offset = 0
    for shape_now in shapes:
        length = shape_now[0] // blocks * math.prod(shape_now[1:])
        segments.append(line_grid[:, offset : offset + length].reshape(shape_now))
        offset += length
    return segments


def flat_id(core, z_at, outer_at):
    return (core * 4 + z_at) * 4 + outer_at


def route_z(pairs_core0):
    route = []
    for z_from, z_to in pairs_core0:
        for outer_at in range(4):
            route.append((flat_id(0, z_from, outer_at), flat_id(0, z_to, outer_at)))
            route.append((flat_id(1, 3 - z_from, outer_at), flat_id(1, 3 - z_to, outer_at)))
    return route


def flipped(route):
    return [(target, source) for source, target in route]


def route_xy(step_core0, step_core1):
    route = []
    for z_at in range(4):
        for outer_at in range(4):
            for core, step in ((0, step_core0), (1, step_core1)):
                route.append((flat_id(core, z_at, outer_at), flat_id(core, z_at, outer_at ^ step)))
    return route


STEP_X, STEP_Y = 1, 2
NEAR_FIRST = route_xy(STEP_X, STEP_Y)
NEAR_SECOND = route_xy(STEP_Y, STEP_X)
Z_PAIR = [(0, 1), (1, 0), (2, 3), (3, 2)]
Z_STRAIGHT = route_z([(0, 2), (1, 3)])
SWAP = [(0, 1), (1, 0)]
UP = [(0, 1), (1, 2), (2, 3), (3, 0)]
DOWN = [(1, 0), (2, 1), (3, 2), (0, 3)]
ACROSS = [(0, 2), (2, 0), (1, 3), (3, 1)]
OUT_X = [(0, 1), (1, 0), (2, 3), (3, 2)]
OUT_Y = [(0, 2), (2, 0), (1, 3), (3, 1)]
OUT_XY = [(0, 3), (3, 0), (1, 2), (2, 1)]


def after(value, *others):
    return lax.optimization_barrier((value,) + others)[0]


def after_all(values, *others):
    return lax.optimization_barrier(tuple(values) + others)[: len(values)]


def about(micros):
    return pl.CostEstimate(flops=0, transcendentals=0, bytes_accessed=int(micros * 3.3e6))


def columns_of(widths):
    found, start = [], 0
    for width in widths:
        found.append((start, width))
        start += width
    return found


def move_blocks(table, sources, outs, plan, name):
    rows = sources[0].shape[1]
    low = sources[0].dtype
    widths = [columns[1] for _, _, columns, _, _, _ in plan]
    total = sum(widths)

    def kernel(table_ref, *refs):
        source_refs = refs[: len(sources)]
        out_refs = refs[len(sources) : len(sources) + len(outs)]
        held, sems_in, sems_out = refs[len(sources) + len(outs) :]
        arriving, leaving = [], []
        start = 0
        for number, (source_at, index, columns, out_at, out_index, out_columns) in enumerate(plan):
            from_row = table_ref[number] if index is None else index
            to_row = table_ref[number] if out_index is None else out_index
            here = held.at[:, pl.ds(start, columns[1])]
            start += columns[1]
            arriving.append(
                pltpu.make_async_copy(
                    source_refs[source_at].at[from_row, :, pl.ds(*columns)],
                    here,
                    sems_in.at[number],
                )
            )
            leaving.append(
                pltpu.make_async_copy(
                    here,
                    out_refs[out_at].at[to_row, :, pl.ds(*out_columns)],
                    sems_out.at[number],
                )
            )
        for copy in arriving:
            copy.start()
        for copy_in, copy_out in zip(arriving, leaving):
            copy_in.wait()
            copy_out.start()
        for copy in leaving:
            copy.wait()

    count = len(plan)
    return pl.pallas_call(
        kernel,
        out_shape=[jax.ShapeDtypeStruct((length, rows, width), low) for length, width in outs],
        grid_spec=pltpu.PrefetchScalarGridSpec(
            num_scalar_prefetch=1,
            grid=(1,),
            in_specs=[pl.BlockSpec(memory_space=pl.ANY)] * len(sources),
            out_specs=[pl.BlockSpec(memory_space=pl.ANY)] * len(outs),
            scratch_shapes=[
                pltpu.VMEM((rows, total), low),
                pltpu.SemaphoreType.DMA((count,)),
                pltpu.SemaphoreType.DMA((count,)),
            ],
        ),
        compiler_params=pltpu.CompilerParams(vmem_limit_bytes=32 * 1024 * 1024),
        cost_estimate=about(1 + 5e-7 * count * rows * total / len(plan)),
        name=name,
    )(table, *sources)


def updated(grad, weight, momentum, average, rate):
    momentum = MOMENTUM * momentum + grad
    weight = weight - rate * (grad + MOMENTUM * momentum)
    return momentum, weight, weight.astype(LOW), AVERAGE * average + (1.0 - AVERAGE) * weight


def update_rows(pieces, state, at, rate, results):
    counts = [grad.shape[0] * width // 128 for grad, _, width in pieces]
    count = sum(counts)
    chunk = 144 if count % 144 == 0 else 128
    total = state[0].shape[0]
    given = [] if results is None else list(results)
    number_of = len(pieces)

    def kernel(*refs):
        grad_refs = refs[:number_of]
        weight_ref, momentum_ref, average_ref = refs[number_of : number_of + 3]
        refs = refs[number_of + 3 + len(given) :]
        outs, arrived = refs[:4], refs[4 : 4 + number_of]
        grad_flat, weight, momentum, average, low, sems = refs[4 + number_of :]
        window = pl.ds(at, count)
        fetched = [
            pltpu.make_async_copy(grad_ref.at[:, pl.ds(start, width)], held, sems.at[3 + number])
            for number, (grad_ref, held, (_, start, width)) in enumerate(
                zip(grad_refs, arrived, pieces)
            )
        ]
        copies = [
            pltpu.make_async_copy(weight_ref.at[window], weight, sems.at[0]),
            pltpu.make_async_copy(momentum_ref.at[window], momentum, sems.at[1]),
            pltpu.make_async_copy(average_ref.at[window], average, sems.at[2]),
        ]
        for copy in fetched + copies:
            copy.start()
        offset = 0
        for copy, held, (grad, _, width) in zip(fetched, arrived, pieces):
            copy.wait()
            rows, per_row = grad.shape[0], width // 128
            for at_now in range(per_row):
                grad_flat[pl.ds(offset + at_now, rows, stride=per_row), :] = held[
                    :, pl.ds(at_now * 128, 128)
                ].astype(jnp.float32)
            offset += rows * per_row
        for copy in copies:
            copy.wait()

        def step(number, carry):
            here = pl.ds(pl.multiple_of(number * chunk, 16), chunk)
            momentum[here], weight[here], low[here], average[here] = updated(
                grad_flat[here], weight[here], momentum[here], average[here], rate
            )
            return carry

        lax.fori_loop(0, count // chunk, step, 0)
        copies = [
            pltpu.make_async_copy(held, out.at[window], sems.at[number])
            for number, (held, out) in enumerate(zip((momentum, weight, low, average), outs))
        ]
        for copy in copies:
            copy.start()
        for copy in copies:
            copy.wait()

    flat = pltpu.VMEM((count, 128), jnp.float32)
    return pl.pallas_call(
        kernel,
        in_specs=[pl.BlockSpec(memory_space=pl.ANY)] * number_of
        + [pl.BlockSpec(memory_space=pltpu.HBM)] * (3 + len(given)),
        out_specs=[pl.BlockSpec(memory_space=pltpu.HBM)] * 4,
        out_shape=[
            jax.ShapeDtypeStruct((total, 128), kind)
            for kind in (jnp.float32, jnp.float32, LOW, jnp.float32)
        ],
        input_output_aliases={number_of + 3 + number: number for number in range(len(given))},
        scratch_shapes=[
            pltpu.VMEM((grad.shape[0], width), grad.dtype) for grad, _, width in pieces
        ]
        + [flat, flat, flat, flat, pltpu.VMEM((count, 128), LOW)]
        + [pltpu.SemaphoreType.DMA((3 + max(number_of, 1),))],
        compiler_params=pltpu.CompilerParams(vmem_limit_bytes=57 * 1024 * 1024),
        cost_estimate=about(1 + count * 0.0016),
        name="update_rows",
    )(*[grad for grad, _, _ in pieces], *state, *given)


def place_blocks(sources, table, widths):
    plan, places = [], []
    for out_at, columns in enumerate(columns_of(widths)):
        number = 0
        for source_at, source in enumerate(sources):
            for at in range(source.shape[0]):
                plan.append((source_at, at, columns, out_at, None, (0, columns[1])))
                places.append(table[number])
                number += 1
    outs = [(16, width) for width in widths]
    return move_blocks(jnp.stack(places).astype(jnp.int32), sources, outs, plan, "place_blocks")


def half_grads(table, left, right, start, total, given):
    tokens, features = left[0].shape
    width = right[0].shape[-1]
    half = features // 2
    rows = half // 8
    tile = next(t for t in (1152, 768, 512, 384, 256) if width % t == 0 and start % t == 0)
    if half > 1152:
        tile = 384
    given = [] if given is None else list(given)

    def kernel(table_ref, own_left, mate_left, own_right, mate_right, *refs):
        give_ref, keep_ref, total_ref = refs[len(given) :]
        for core in range(2):

            @pl.when(table_ref[0] == core)
            def _():
                mine = pl.ds(core * half, half)
                total_ref[...] = dot_tn(own_left[:, mine], own_right[...]) + dot_tn(
                    mate_left[:, mine], mate_right[...]
                )

        for number in range(8):
            block = total_ref[pl.ds(pl.multiple_of(table_ref[1 + number] * rows, 8), rows), :]
            (give_ref, keep_ref)[number // 4][number % 4] = block.astype(LOW)

    first = start // tile
    whole = pl.BlockSpec((tokens, features), lambda i, table: (0, 0))
    part = pl.BlockSpec((tokens, tile), lambda i, table: (0, i))
    out = pl.BlockSpec((4, rows, tile), lambda i, table: (0, 0, first + i))
    return pl.pallas_call(
        kernel,
        grid_spec=pltpu.PrefetchScalarGridSpec(
            num_scalar_prefetch=1,
            grid=(width // tile,),
            in_specs=[whole, whole, part, part]
            + [pl.BlockSpec(memory_space=pl.ANY)] * len(given),
            out_specs=[out, out],
            scratch_shapes=[pltpu.VMEM((half, tile), jnp.float32)],
        ),
        out_shape=[jax.ShapeDtypeStruct((4, rows, total), LOW)] * 2,
        input_output_aliases={5 + number: number for number in range(len(given))},
        compiler_params=pltpu.CompilerParams(vmem_limit_bytes=48 * 1024 * 1024),
        cost_estimate=about(3 + 1.6e-6 * features * width),
        name="half_grads",
    )(table, *left, *right, *given)


class Staged:
    def __init__(self):
        self.core = lax.axis_index("blk")
        self.z_at = lax.axis_index("inner")
        outer_at = lax.axis_index("outer")
        self.y_at = outer_at // 2
        self.x_at = outer_at % 2
        self.own_half = (self.z_at // 2) == self.core
        self.own_row = self.z_at * 4 + outer_at

    def z_pair(self, core):
        low_bit = self.z_at % 2
        return 2 * core + low_bit, 2 * core + 1 - low_bit

    def near_order(self, core, picks):
        found = []
        for far, near in picks:
            first = jnp.where(core == 0, self.x_at, self.y_at) ^ near
            second = jnp.where(core == 0, self.y_at, self.x_at) ^ far
            y_now = jnp.where(core == 0, second, first)
            x_now = jnp.where(core == 0, first, second)
            found.append(y_now * 2 + x_now)
        return found

    def gather_groups(self, groups, gates, early):
        packed = [
            group[0] if len(group) == 1 else jnp.concatenate(group, axis=1) for group in groups
        ]
        table = []
        for core in (self.core, 1 - self.core):
            for outer_at in self.near_order(core, [(0, 0), (0, 1), (1, 0), (1, 1)]):
                for z_now in self.z_pair(core):
                    table.append(z_now * 4 + outer_at)
        last = len(groups) - 1
        held, others, twos, fours, tokens = {}, {}, {}, {}, {}

        def first_stage(k, gates, late):
            own = after(packed[k], *gates)
            came = after(lax.ppermute(own, EVERY, Z_STRAIGHT), *late)
            held[k] = jnp.where(self.own_half, own, came)
            others[k] = lax.ppermute(held[k], "inner", Z_PAIR)

        def second_stage(k, late):
            twos[k] = jnp.stack([held[k], after(others[k], *late)])

        def third_stage(k, late):
            came = after(lax.ppermute(twos[k], EVERY, NEAR_FIRST), *late)
            fours[k] = jnp.concatenate([twos[k], came])

        first_stage(0, (), early[0]())
        second_stage(0, early[1]())
        first_stage(1, (held[0],), (twos[0],))
        third_stage(0, early[2](twos[0]))
        second_stage(1, (fours[0],))
        for k in range(len(groups)):
            if k + 1 < last:
                first_stage(k + 2, (twos[k + 1],), ())
            far_four = lax.ppermute(fours[k], EVERY, NEAR_SECOND)
            mate_four = lax.ppermute(fours[k], "blk", SWAP)
            if k < last:
                far_four = after(far_four, twos[k + 1])
            else:
                far_four = after(far_four, tokens[k - 1])
            if k < last:
                third_stage(k + 1, (far_four,))
            mate_far = lax.ppermute(far_four, "blk", SWAP)
            if k < last:
                mate_far = after(mate_far, fours[k + 1])
            sources = [fours[k], far_four, mate_four, mate_far]
            widths = [part.shape[1] for part in groups[k]]
            tokens[k] = gates[k](
                [part.reshape(-1, part.shape[-1]) for part in place_blocks(sources, table, widths)]
            )
            if k + 1 < last:
                second_stage(k + 2, (tokens[k],))

    def share(self, value):
        tokens = value.reshape(-1, value.shape[-1])
        return tokens, lax.ppermute(tokens, "blk", SWAP)

    def start_grads(self, pairs):
        return StagedGrads(self, pairs)

    def update(self, state, rate, parts):
        lanes = [array.reshape(-1, 128) for array in state]
        sizes = [rows * cols // (16 * 128) for rows, cols in mat_shapes()]
        results = None
        for entries in parts:
            if isinstance(entries[0][0], StagedGrads) and entries[0][0].stage == 3:
                entries[0][0].add(results[0])
            pieces = []
            for part, start, number in entries:
                grad = part.both if isinstance(part, StagedGrads) else part
                pieces.append((grad, start, mat_shapes()[number][1]))
            first = entries[0][2]
            results = update_rows(pieces, lanes, sum(sizes[:first]), rate, results)
        return [result.reshape(-1) for result in results]

    def gather_slots(self, own, between=None):
        four = jnp.concatenate(
            [own] + [lax.ppermute(own, "inner", route) for route in (UP, DOWN, ACROSS)]
        )
        self.token = four
        if between is not None:
            four = after(four, between())
        return jnp.concatenate(
            [four] + [lax.ppermute(four, "outer", route) for route in (OUT_X, OUT_Y, OUT_XY)]
        )

    def swap_slots(self, parts, between):
        parts = parts.reshape((4, 4) + parts.shape[1:])
        four = jnp.stack(
            [parts[0]]
            + [
                lax.ppermute(parts[1 + at], "outer", route)
                for at, route in enumerate((OUT_X, OUT_Y, OUT_XY))
            ]
        )
        four = after(four, between())
        return jnp.stack(
            [four[:, 0]]
            + [
                lax.ppermute(four[:, 1 + at], "inner", route)
                for at, route in enumerate((DOWN, UP, ACROSS))
            ],
        )

    def reduce_slots(self, parts, late):
        parts = parts.reshape((4, 4) + parts.shape[1:])
        four = parts[0]
        for at, route in enumerate((OUT_X, OUT_Y, OUT_XY)):
            four = four + after(lax.ppermute(parts[1 + at], "outer", route), late)
        self.token = four
        total = four[0]
        for at, route in enumerate((DOWN, UP, ACROSS)):
            total = total + lax.ppermute(four[1 + at], "inner", route)
        return total

    def slot_rows(self):
        found = []
        for z_now in range(4):
            away = (z_now - self.z_at) % 4
            z_slot = jnp.where(away == 0, 0, jnp.where(away == 3, 1, jnp.where(away == 1, 2, 3)))
            for outer_now in range(4):
                flip = jnp.bitwise_xor(outer_now, self.y_at * 2 + self.x_at)
                found.append((flip, z_slot))
        return found

    def rows_in_order(self, slots):
        table = [flip * 4 + z_slot for flip, z_slot in self.slot_rows()]
        return jnp.take(slots, jnp.stack(table), axis=0)

    def swapped_in_order(self, came):
        table = []
        for flip, z_slot in self.slot_rows():
            came_at = jnp.where(z_slot == 1, 2, jnp.where(z_slot == 2, 1, z_slot))
            table.append(came_at * 4 + flip)
        return jnp.take(came.reshape(16, -1), jnp.stack(table), axis=0)


class StagedGrads:
    def __init__(self, moves, pairs):
        self.moves = moves
        low_bit = moves.z_at % 2
        table = [moves.core]
        for outer_at in moves.near_order(moves.core, [(1, 1), (1, 0), (0, 1), (0, 0)]):
            for z_now in (low_bit, 1 - low_bit):
                table.append(z_now * 4 + outer_at)
        table = jnp.stack(table).astype(jnp.int32)
        total = sum(right[0].shape[-1] for _, right in pairs)
        start, found = 0, None
        for left, right in pairs:
            found = half_grads(table, left, right, start, total, found)
            start += right[0].shape[-1]
        self.give, self.keep = found
        self.token = self.give
        self.stage = 0

    def send(self, *gates):
        self.give = after(self.give, *gates) if gates else self.give
        axes, route = (
            (EVERY, NEAR_SECOND),
            (EVERY, NEAR_FIRST),
            ("inner", Z_PAIR),
            (EVERY, flipped(Z_STRAIGHT)),
        )[self.stage]
        self.came = lax.ppermute(self.give, axes, route)

    def add(self, *late):
        came = after(self.came, *late) if late else self.came
        total = self.keep.astype(jnp.float32) + came.astype(jnp.float32)
        if self.stage == 0:
            self.give = total[:2].astype(LOW)
            self.keep = total[2:].astype(LOW)
        elif self.stage == 1:
            self.give = total[1].astype(LOW)
            self.keep = total[0].astype(LOW)
        else:
            self.give = self.keep = total.astype(LOW)
        if self.stage == 3:
            mate = lax.ppermute(self.give, "blk", SWAP)
            self.both = jnp.where(self.moves.own_half, self.give, mate)
        self.token = self.give
        self.stage += 1


def outer_sum(left_arr, right_arr):
    return jnp.einsum("sni,snj->ij", left_arr, right_arr, preferred_element_type=jnp.float32)


class DirectGrads:
    def __init__(self, pairs):
        self.parts = [outer_sum(left[0], right[0]).astype(LOW) for left, right in pairs]
        self.token = self.parts[0]

    def send(self, *gates):
        pass

    def add(self, *late):
        pass

    @functools.cached_property
    def result(self):
        found = []
        for grad in self.parts:
            part = lax.psum_scatter(grad, GROUP, scatter_dimension=0, tiled=True)
            found.append(lax.psum(part, "blk").astype(jnp.float32))
        return found


class Direct:
    def __init__(self):
        self.core = lax.axis_index("blk")
        self.own_row = lax.axis_index("inner") * lax.axis_size("outer") + lax.axis_index("outer")

    def gather_groups(self, groups, gates, early):
        early[0]()
        early[1]()
        early[2](groups[0][0])
        for group, gate in zip(groups, gates):
            gate([lax.all_gather(part, GROUP, axis=0, tiled=True) for part in group])

    def share(self, value):
        return (value,)

    def start_grads(self, pairs):
        return DirectGrads(pairs)

    def update(self, state, rate, parts):
        found = {}
        for part, start, number in sum(parts, []):
            whole = jnp.concatenate(part.result, axis=1) if isinstance(part, DirectGrads) else part
            found[number] = whole[:, start : start + mat_shapes()[number][1]]
        grad = jnp.concatenate([found[number].reshape(-1) for number in sorted(found)])
        return updated(grad, *state, rate)

    def gather_slots(self, own, between=None):
        self.token = own
        if between is not None:
            between()
        return lax.all_gather(own, GROUP, axis=0, tiled=True)

    def reduce_slots(self, parts, late):
        self.token = parts
        return lax.psum_scatter(parts, GROUP, scatter_dimension=0, tiled=False)

    def swap_slots(self, parts, between):
        between()
        return lax.all_gather(parts, GROUP, axis=0)

    def rows_in_order(self, slots):
        return slots

    def swapped_in_order(self, came):
        mine = lax.dynamic_index_in_dim(came, self.own_row, 1, keepdims=False)
        return mine.reshape(mine.shape[0], -1)


def time_embed(steps_t):
    half_dim = D // 2
    frequency = jnp.exp(-math.log(10000.0) * jnp.arange(half_dim, dtype=jnp.float32) / half_dim)
    angles = steps_t.astype(jnp.float32)[:, None] * frequency[None, :]
    return jnp.concatenate([jnp.cos(angles), jnp.sin(angles)], axis=1)


def modulate(values, scale_v, shift_v):
    center = values - jnp.mean(values, axis=-1, keepdims=True)
    normed = center * lax.rsqrt(jnp.mean(center * center, axis=-1, keepdims=True) + EPS_NORM)
    return normed * (1.0 + scale_v[:, None, :]) + shift_v[:, None, :]


def gelu_tanh(values):
    return jax.nn.gelu(values, approximate=True)


def rms_unit(values):
    return values * lax.rsqrt(jnp.mean(values * values, axis=-1, keepdims=True) + EPS_NORM)


def matmul(left_arr, right_arr):
    return jnp.einsum("...i,ij->...j", left_arr, right_arr, preferred_element_type=jnp.float32)


def matmul_t(left_arr, right_arr):
    return jnp.einsum("...j,ij->...i", left_arr, right_arr, preferred_element_type=jnp.float32)


def column_sum(tensor):
    return jnp.sum(tensor.astype(jnp.float32), axis=(0, 1))


def attention(queries, near_kv, far_kv):
    images, rows, _ = queries.shape
    heads = D // E

    def kernel(q_ref, near_ref, far_ref, out_ref):
        for head in range(heads):
            own = pl.ds(head * E, E)
            other = pl.ds(D + head * E, E)
            q_now = q_ref[0, :, own]
            keys = jnp.concatenate([near_ref[0, :, own], far_ref[0, :, own]], axis=0)
            values = jnp.concatenate([near_ref[0, :, other], far_ref[0, :, other]], axis=0)
            scores = dot_nt(keys, q_now) * E ** (-0.5)
            top = jnp.max(scores, axis=0, keepdims=True)
            weight = jnp.exp(scores - top)
            probs = weight * (1.0 / jnp.sum(weight, axis=0, keepdims=True))
            out_ref[0, :, own] = dot_tn(probs.astype(LOW), values).astype(LOW)

    block = pl.BlockSpec((1, rows, D), lambda i: (i, 0, 0))
    block_kv = pl.BlockSpec((1, rows, 2 * D), lambda i: (i, 0, 0))
    return pl.pallas_call(
        kernel,
        grid=(images,),
        in_specs=[block, block_kv, block_kv],
        out_specs=block,
        out_shape=jax.ShapeDtypeStruct(queries.shape, LOW),
        compiler_params=pltpu.CompilerParams(vmem_limit_bytes=32 * 1024 * 1024),
        cost_estimate=about(14 * images / 4),
        name="attention",
    )(queries, near_kv, far_kv)


def attention_grads(queries, near_kv, far_kv, grad_att):
    images, rows, _ = queries.shape
    heads = D // E

    def kernel(q_ref, near_ref, far_ref, grad_ref, dq_ref, dnear_ref, dfar_ref):
        for head in range(heads):
            own = pl.ds(head * E, E)
            other = pl.ds(D + head * E, E)
            q_now = q_ref[0, :, own]
            g_now = grad_ref[0, :, own]
            keys = jnp.concatenate([near_ref[0, :, own], far_ref[0, :, own]], axis=0)
            values = jnp.concatenate([near_ref[0, :, other], far_ref[0, :, other]], axis=0)
            scores = dot_nt(keys, q_now) * E ** (-0.5)
            top = jnp.max(scores, axis=0, keepdims=True)
            weight = jnp.exp(scores - top)
            probs = weight * (1.0 / jnp.sum(weight, axis=0, keepdims=True))
            grad_probs = dot_nt(values, g_now)
            delta = jnp.sum(probs * grad_probs, axis=0, keepdims=True)
            grad_scores = (probs * (grad_probs - delta)).astype(LOW)
            dq_ref[0, :, own] = (dot_tn(grad_scores, keys) * E ** (-0.5)).astype(LOW)
            grad_keys = dot_nn(grad_scores, q_now) * E ** (-0.5)
            grad_values = dot_nn(probs.astype(LOW), g_now)
            dnear_ref[0, :, own] = grad_keys[:rows]
            dnear_ref[0, :, other] = grad_values[:rows]
            dfar_ref[0, :, own] = grad_keys[rows:].astype(LOW)
            dfar_ref[0, :, other] = grad_values[rows:].astype(LOW)

    block = pl.BlockSpec((1, rows, D), lambda i: (i, 0, 0))
    block_kv = pl.BlockSpec((1, rows, 2 * D), lambda i: (i, 0, 0))
    return pl.pallas_call(
        kernel,
        grid=(images,),
        in_specs=[block, block_kv, block_kv, block],
        out_specs=[block, block_kv, block_kv],
        out_shape=[
            jax.ShapeDtypeStruct(queries.shape, LOW),
            jax.ShapeDtypeStruct(near_kv.shape, jnp.float32),
            jax.ShapeDtypeStruct(far_kv.shape, LOW),
        ],
        compiler_params=pltpu.CompilerParams(vmem_limit_bytes=32 * 1024 * 1024),
        cost_estimate=about(21 * images / 4),
        name="attention_grads",
    )(queries, near_kv, far_kv, grad_att)


def dot_nn(left, right):
    return lax.dot_general(
        left, right, (((1,), (0,)), ((), ())), preferred_element_type=jnp.float32
    )


def dot_nt(left, right):
    return lax.dot_general(
        left, right, (((1,), (1,)), ((), ())), preferred_element_type=jnp.float32
    )


def dot_tn(left, right):
    return lax.dot_general(
        left, right, (((0,), (0,)), ((), ())), preferred_element_type=jnp.float32
    )


def body(
    hidden,
    labels,
    steps_t,
    live_slots,
    label_table,
    targets,
    cotangent,
    weights,
    weight_momentum,
    weight_average,
    biases,
    bias_momentum,
    bias_average,
):
    n_inner = lax.axis_size("inner")
    n_outer = lax.axis_size("outer")
    blocks = n_inner * n_outer
    slots = hidden.shape[0]
    local_tok = hidden.shape[1]
    moves = Staged() if (n_inner, n_outer) == (4, 4) else Direct()
    p_qkv, p_proj, p_up, p_down, p_ada, p_one, p_two, p_three = split_shard(
        weights.astype(LOW), mat_shapes(), blocks
    )
    bias_low = biases.astype(LOW)
    condition = label_table[labels].astype(jnp.float32) + time_embed(steps_t)
    cond_act, silu_cond = jax.vjp(jax.nn.silu, condition)
    cond_low = cond_act.astype(LOW)
    kept = {}
    rows_d = D // blocks
    half_ada = 3 * D

    def early_gather():
        packed = jnp.concatenate([cond_low, bias_low.reshape(slots, -1)], axis=1)
        kept["packed"] = moves.gather_slots(packed)
        return (moves.token,)

    def early_product():
        packed_all = kept["packed"]
        cond_own = lax.dynamic_slice_in_dim(
            packed_all[:, :D], moves.own_row * rows_d, rows_d, 1
        )
        ada_half = lax.dynamic_slice_in_dim(p_ada, moves.core * half_ada, half_ada, 1)
        mod_part = matmul(cond_own, ada_half).reshape(blocks, slots, half_ada)
        kept.update(cond_own=cond_own, mod_part=mod_part)
        return (mod_part,)

    def early_modulation(gate):
        mod_half = moves.reduce_slots(kept["mod_part"], gate)
        late = moves.token
        mod_mate = lax.ppermute(mod_half, "blk", SWAP)
        bias_all = moves.rows_in_order(kept["packed"][:, D:].reshape(blocks, -1))
        biases_now = unpack_rows(bias_all.astype(jnp.float32), bias_shapes())
        b_ada = biases_now[5]
        kept["biases"] = biases_now
        modulation = (
            jnp.concatenate(
                [
                    jnp.where(moves.core == 0, mod_half, mod_mate),
                    jnp.where(moves.core == 0, mod_mate, mod_half),
                ],
                axis=1,
            )
            + b_ada
        )
        shift_a, scale_a, gate_a, shift_m, scale_m, gate_m = [
            modulation[:, part_idx * D : (part_idx + 1) * D] for part_idx in range(6)
        ]
        hidden_f = hidden.astype(jnp.float32)
        mixed_a, pull_a = jax.vjp(modulate, hidden_f, scale_a, shift_a)
        mixed_a_low = mixed_a.astype(LOW)
        left_qkv = moves.share(mixed_a_low)
        kept.update(
            gates=(gate_a, gate_m), scale_m=scale_m, shift_m=shift_m, hidden_f=hidden_f,
            mixed_a_low=mixed_a_low, pull_a=pull_a, left_qkv=left_qkv,
        )
        return (late,)

    def use_first(arrived):
        b_q, b_v = kept["biases"][:2]
        (w_qkv,) = arrived
        qkv_bias = jnp.concatenate([b_q, jnp.zeros((D,), jnp.float32), b_v])
        qkv_low = (matmul(kept["mixed_a_low"], w_qkv) + qkv_bias).astype(LOW)
        near_kv = qkv_low[..., D:]
        far_kv = passed_along(near_kv, "blk", 1)
        kept.update(w_qkv=w_qkv, queries=qkv_low[..., :D], near_kv=near_kv, far_kv=far_kv)
        return far_kv
    def use_second(arrived):
        w_proj, w_one = arrived
        b_proj = kept["biases"][2]
        queries, near_kv, far_kv = kept["queries"], kept["near_kv"], kept["far_kv"]
        queries = after(queries, w_proj)
        att_low = attention(queries, near_kv, far_kv)
        left_proj = moves.share(att_low)
        branch_a = matmul(att_low, w_proj) + b_proj
        residual = kept["hidden_f"] + kept["gates"][0][:, None, :] * branch_a
        mixed_m, pull_m = jax.vjp(modulate, residual, kept["scale_m"], kept["shift_m"])
        mixed_m_low = mixed_m.astype(LOW)
        left_up = moves.share(mixed_m_low)
        kept.update(
            w_proj=w_proj, w_one=w_one, left_proj=left_proj,
            branch_a=branch_a, residual=residual, pull_m=pull_m, left_up=left_up,
            mixed_m_low=mixed_m_low,
        )
        return mixed_m_low

    def use_third(arrived):
        (w_up,) = arrived
        b_up = kept["biases"][3]
        pre_act = matmul(kept["mixed_m_low"], w_up) + b_up
        activated, gelu_pull = jax.vjp(gelu_tanh, pre_act)
        act_low = activated.astype(LOW)
        gelu_slope = gelu_pull(jnp.ones_like(pre_act))[0]
        left_down = moves.share(act_low)
        act_low, gelu_slope = lax.optimization_barrier((act_low, gelu_slope))
        kept.update(w_up=w_up, gelu_slope=gelu_slope, act_low=act_low, left_down=left_down)
        return act_low

    def use_fourth(arrived):
        (w_down,) = arrived
        b_down, c_one = kept["biases"][4], kept["biases"][6]
        branch_m = matmul(kept["act_low"], w_down) + b_down
        output = kept["residual"] + kept["gates"][1][:, None, :] * branch_m
        out_low = output.astype(LOW)
        left_one = moves.share(out_low)
        hid_one = matmul(out_low, kept["w_one"]) + c_one
        act_one, silu_one = jax.vjp(jax.nn.silu, hid_one)
        one_low = act_one.astype(LOW)
        left_two = moves.share(one_low)
        kept.update(
            w_down=w_down, branch_m=branch_m, out_low=out_low, left_one=left_one,
            silu_one=silu_one, one_low=one_low, left_two=left_two,
        )
        return one_low

    def use_fifth(arrived):
        w_two, w_three = arrived
        c_two, c_three = kept["biases"][7:]
        hid_two = matmul(kept["one_low"], w_two) + c_two
        act_two, silu_two = jax.vjp(jax.nn.silu, hid_two)
        two_low = act_two.astype(LOW)
        left_three = moves.share(two_low)
        projection = matmul(two_low, w_three) + c_three
        kept.update(
            w_two=w_two, w_three=w_three, silu_two=silu_two, left_three=left_three,
            projection=projection,
        )

    moves.gather_groups(
        [[p_qkv], [p_proj, p_one], [p_up], [p_down], [p_two, p_three]],
        [use_first, use_second, use_third, use_fourth, use_fifth],
        [early_gather, early_product, early_modulation],
    )
    w_qkv, w_proj, w_up, w_down, w_one, w_two, w_three = [
        kept[name] for name in ("w_qkv", "w_proj", "w_up", "w_down", "w_one", "w_two", "w_three")
    ]
    gate_a, gate_m = kept["gates"]
    cond_own = kept["cond_own"]
    pull_a, left_qkv = kept["pull_a"], kept["left_qkv"]
    queries, near_kv, far_kv = [kept[name] for name in ("queries", "near_kv", "far_kv")]
    branch_a, branch_m, out_low, projection = [
        kept[name] for name in ("branch_a", "branch_m", "out_low", "projection")
    ]
    pull_m, gelu_slope, silu_one, silu_two = [
        kept[name] for name in ("pull_m", "gelu_slope", "silu_one", "silu_two")
    ]
    live_f = live_slots.astype(jnp.float32)[:, None, None]
    unit_proj, unit_pull = jax.vjp(rms_unit, projection)
    grad_proj = unit_pull(-LAMBDA_REPA * live_f * rms_unit(targets.astype(jnp.float32)))[0].astype(
        LOW
    )
    right_three = moves.share(grad_proj)
    grad_cthree = column_sum(grad_proj)
    grad_htwo = silu_two(matmul_t(grad_proj, w_three))[0].astype(LOW)
    right_two = moves.share(grad_htwo)
    grad_ctwo = column_sum(grad_htwo)
    grad_hone = silu_one(matmul_t(grad_htwo, w_two))[0].astype(LOW)
    right_one = moves.share(grad_hone)
    grads_fourth = moves.start_grads(
        [(kept["left_two"], right_two), (kept["left_three"], right_three)]
    )
    grad_cone = column_sum(grad_hone)
    grads_fourth.send()
    right_one = after_all(right_one, grads_fourth.token)
    grads_one = moves.start_grads([(kept["left_one"], right_one)])
    grads_one.send()
    grad_hone = after(grad_hone, grads_one.token)
    grad_output = cotangent.astype(jnp.float32) * live_f + matmul_t(grad_hone, w_one)
    grad_gate_m = jnp.sum(grad_output * branch_m, axis=1)
    grad_bm = (gate_m[:, None, :] * grad_output).astype(LOW)
    right_down = moves.share(grad_bm)
    grad_bdown = column_sum(grad_bm)
    grad_pre = (matmul_t(grad_bm, w_down) * gelu_slope).astype(LOW)
    right_up = moves.share(grad_pre)
    grads_down = moves.start_grads([(kept["left_down"], right_down)])
    grad_bup = column_sum(grad_pre)
    grads_down.send()
    grads_fourth.add(grads_down.token)
    grads_fourth.send()
    grad_pre = after(grad_pre, grads_down.token, grads_fourth.token)
    grad_res_m, grad_scale_m, grad_shift_m = pull_m(matmul_t(grad_pre, w_up))
    grad_residual = grad_output + grad_res_m
    grad_gate_a = jnp.sum(grad_residual * branch_a, axis=1)
    grad_ba = (gate_a[:, None, :] * grad_residual).astype(LOW)
    right_proj = moves.share(grad_ba)
    grad_bproj = column_sum(grad_ba)
    grad_att = matmul_t(grad_ba, w_proj).astype(LOW)
    grads_one.add(grad_att)
    grads_one.send()
    grads_fourth.add(grad_att)
    grads_fourth.send()
    right_up = after_all(right_up, grads_fourth.token, grads_one.token)
    grads_up = moves.start_grads([(kept["left_up"], right_up), (kept["left_proj"], right_proj)])
    grads_up.send()
    grads_down.add(grads_up.token)
    grads_down.send()
    grads_one.add(grads_up.token)
    grads_one.send()
    grads_fourth.add(grads_up.token)
    grads_fourth.send()
    grad_att = after(
        grad_att, grads_up.token, grads_down.token, grads_one.token, grads_fourth.token
    )
    grad_query, near_dkv, far_dkv = attention_grads(queries, near_kv, far_kv, grad_att)
    home_dkv = passed_along(far_dkv, "blk", -1)
    grads_down.add(grad_query)
    grads_down.send()
    grads_fourth.add(grad_query)
    grads_one.add(grad_query)
    grads_one.send()
    home_dkv = after(home_dkv, grads_down.token, grads_one.token, grads_fourth.token)
    grad_kv = (near_dkv + home_dkv.astype(jnp.float32)).astype(LOW)
    grad_qkv = jnp.concatenate([grad_query, grad_kv], axis=-1)
    grads_first = moves.start_grads([(left_qkv, moves.share(grad_qkv))])
    qkv_sums = column_sum(grad_qkv)
    grads_first.send()
    grads_down.add(grads_first.token)
    grads_down.send()
    grads_one.add(grads_first.token)
    grad_qkv = after(grad_qkv, grads_first.token, grads_down.token, grads_one.token)
    grad_hid_a, grad_scale_a, grad_shift_a = pull_a(matmul_t(grad_qkv, w_qkv))
    grad_input = grad_residual + grad_hid_a
    grad_mod_part = jnp.concatenate(
        [grad_shift_a, grad_scale_a, grad_gate_a, grad_shift_m, grad_scale_m, grad_gate_m], axis=1
    )
    bias_terms = (
        qkv_sums[:D],
        qkv_sums[2 * D :],
        grad_bproj,
        grad_bup,
        grad_bdown,
        grad_cone,
        grad_ctwo,
        grad_cthree,
    )
    bias_grid = jnp.concatenate(
        [segment.reshape(blocks, -1) for segment in bias_terms], axis=1
    ).reshape(slots, -1)
    grad_small = jnp.concatenate([grad_mod_part, bias_grid], axis=1)
    small_came = lax.ppermute(grad_small, "blk", SWAP)
    grads_up.add(grad_small)
    grads_up.send()
    grads_first.add(grads_up.token)
    grads_first.send()
    small_came = after(small_came, grads_up.token, grads_first.token)
    grad_small = (grad_small + small_came).astype(LOW)
    small_all = moves.gather_slots(grad_small)
    grads_first.add(small_all)
    grads_first.send()
    grads_up.add(small_all)
    grads_up.send()
    small_all = after(small_all, grads_first.token, grads_up.token)

    def between_swaps():
        grads_first.add()
        grads_first.send()
        grads_up.add()
        grads_up.send()
        return lax.optimization_barrier((grads_up.token, grads_first.token))[0]

    grad_mod = small_all[:, : 6 * D]
    cond_cols = matmul_t(grad_mod, p_ada).reshape(blocks, slots, rows_d)
    cond_rows = moves.swapped_in_order(moves.swap_slots(cond_cols, between_swaps))
    grad_cond = silu_cond(
        cond_rows.reshape(blocks, slots, rows_d).transpose(1, 0, 2).reshape(slots, D)
    )[0]
    grad_wada = jnp.einsum("si,sj->ij", cond_own, grad_mod, preferred_element_type=jnp.float32)
    grad_bada = lax.dynamic_index_in_dim(
        jnp.sum(grad_mod.astype(jnp.float32), axis=0).reshape(blocks, -1),
        moves.own_row,
        0,
        keepdims=False,
    )
    bias_sums = jnp.sum(
        small_all[:, 6 * D :].astype(jnp.float32).reshape(blocks, slots, -1), axis=0
    )
    bias_own = lax.dynamic_index_in_dim(
        bias_sums.reshape(blocks, -1), moves.own_row, 0, keepdims=False
    )
    ada_at = (3 * D + FF + D) // blocks
    grad_b_flat = jnp.concatenate([bias_own[:ada_at], grad_bada, bias_own[ada_at:]])
    grads_down.add(grad_mod_part)
    grads_up.add()
    images_all = slots * blocks
    tokens_img = local_tok * lax.axis_size("blk")
    rate_w = LR_COEF / math.sqrt(images_all * tokens_img)
    rate_b = BIAS_FACTOR * rate_w
    mom_w, new_w, low_w, avg_w = moves.update(
        (weights, weight_momentum, weight_average),
        rate_w,
        [
            [(grads_fourth, 0, 6)],
            [(grads_fourth, PH, 7)],
            [(grads_one, 0, 5)],
            [(grads_down, 0, 3)],
            [(grads_up, 0, 2)],
            [(grad_wada, 0, 4)],
            [(grads_first, 0, 0), (grads_up, FF, 1)],
        ],
    )
    mom_b = MOMENTUM * bias_momentum + grad_b_flat
    new_b = biases - rate_b * (grad_b_flat + MOMENTUM * mom_b)
    avg_b = AVERAGE * bias_average + (1.0 - AVERAGE) * new_b
    return (
        out_low,
        grad_input,
        grad_cond,
        mom_w,
        new_w,
        low_w,
        avg_w,
        mom_b,
        new_b,
        new_b.astype(LOW),
        avg_b,
    )


def solution(mesh):
    in_specs = (
        P(("inner", "outer"), "blk", None),
        P(("inner", "outer")),
        P(("inner", "outer")),
        P(("inner", "outer")),
        P(),
        P(("inner", "outer"), "blk", None),
        P(("inner", "outer"), "blk", None),
        P(("inner", "outer")),
        P(("inner", "outer")),
        P(("inner", "outer")),
        P(("inner", "outer")),
        P(("inner", "outer")),
        P(("inner", "outer")),
    )
    out_specs = (
        P(("inner", "outer"), "blk", None),
        P(("inner", "outer"), "blk", None),
        P(("inner", "outer"), None),
        P(("inner", "outer")),
        P(("inner", "outer")),
        P(("inner", "outer")),
        P(("inner", "outer")),
        P(("inner", "outer")),
        P(("inner", "outer")),
        P(("inner", "outer")),
        P(("inner", "outer")),
    )
    return jax.shard_map(body, mesh=mesh, in_specs=in_specs, out_specs=out_specs, check_vma=False)
```

```python
import functools
import math

import jax
import jax.numpy as jnp
from jax import lax
from jax.experimental import pallas as pl
from jax.experimental.pallas import tpu as pltpu
from jax.sharding import PartitionSpec as P

E = 72
D = 1152
FF = 4608
PH = 2048
ZD = 768


LAMBDA_REPA = 0.5
MOMENTUM = 0.5
AVERAGE = 0.5
LR_COEF = 0.04
BIAS_FACTOR = 4.0
EPS_NORM = 1e-06
GROUP = ("inner", "outer")
EVERY = ("blk", "inner", "outer")
LOW = jnp.bfloat16


def passed_along(block, axis, distance):
    devices = range(lax.axis_size(axis))
    route = [((i - distance) % len(devices), i) for i in devices]
    return lax.ppermute(block, axis, route)


def mat_shapes():
    return [(D, 3 * D), (D, D), (D, FF), (FF, D), (D, 6 * D), (D, PH), (PH, PH), (PH, ZD)]


def bias_shapes():
    return [(D,), (D,), (D,), (FF,), (D,), (6 * D,), (PH,), (PH,), (ZD,)]


def split_shard(flat_vec, shapes, blocks):
    segments = []
    offset = 0
    for shape_now in shapes:
        rows_here = shape_now[0] // blocks
        length = rows_here * math.prod(shape_now[1:])
        segments.append(
            flat_vec[offset : offset + length].reshape((rows_here,) + tuple(shape_now[1:]))
        )
        offset += length
    return segments


def unpack_rows(line_grid, shapes):
    blocks = line_grid.shape[0]
    segments = []
    offset = 0
    for shape_now in shapes:
        length = shape_now[0] // blocks * math.prod(shape_now[1:])
        segments.append(line_grid[:, offset : offset + length].reshape(shape_now))
        offset += length
    return segments


def flat_id(core, z_at, outer_at):
    return (core * 4 + z_at) * 4 + outer_at


def route_z(pairs_core0):
    route = []
    for z_from, z_to in pairs_core0:
        for outer_at in range(4):
            route.append((flat_id(0, z_from, outer_at), flat_id(0, z_to, outer_at)))
            route.append((flat_id(1, 3 - z_from, outer_at), flat_id(1, 3 - z_to, outer_at)))
    return route


def flipped(route):
    return [(target, source) for source, target in route]


def route_xy(step_core0, step_core1):
    route = []
    for z_at in range(4):
        for outer_at in range(4):
            for core, step in ((0, step_core0), (1, step_core1)):
                route.append((flat_id(core, z_at, outer_at), flat_id(core, z_at, outer_at ^ step)))
    return route


STEP_X, STEP_Y = 1, 2
NEAR_FIRST = route_xy(STEP_X, STEP_Y)
NEAR_SECOND = route_xy(STEP_Y, STEP_X)
Z_PAIR = [(0, 1), (1, 0), (2, 3), (3, 2)]
Z_STRAIGHT = route_z([(0, 2), (1, 3)])
SWAP = [(0, 1), (1, 0)]
UP = [(0, 1), (1, 2), (2, 3), (3, 0)]
DOWN = [(1, 0), (2, 1), (3, 2), (0, 3)]
ACROSS = [(0, 2), (2, 0), (1, 3), (3, 1)]
OUT_X = [(0, 1), (1, 0), (2, 3), (3, 2)]
OUT_Y = [(0, 2), (2, 0), (1, 3), (3, 1)]
OUT_XY = [(0, 3), (3, 0), (1, 2), (2, 1)]


def after(value, *others):
    return lax.optimization_barrier((value,) + others)[0]


def after_all(values, *others):
    return lax.optimization_barrier(tuple(values) + others)[: len(values)]


def about(micros):
    return pl.CostEstimate(flops=0, transcendentals=0, bytes_accessed=int(micros * 3.3e6))


def columns_of(widths):
    found, start = [], 0
    for width in widths:
        found.append((start, width))
        start += width
    return found


def move_blocks(table, sources, outs, plan, name):
    rows = sources[0].shape[1]
    low = sources[0].dtype
    widths = [columns[1] for _, _, columns, _, _, _ in plan]
    total = sum(widths)

    def kernel(table_ref, *refs):
        source_refs = refs[: len(sources)]
        out_refs = refs[len(sources) : len(sources) + len(outs)]
        held, sems_in, sems_out = refs[len(sources) + len(outs) :]
        arriving, leaving = [], []
        start = 0
        for number, (source_at, index, columns, out_at, out_index, out_columns) in enumerate(plan):
            from_row = table_ref[number] if index is None else index
            to_row = table_ref[number] if out_index is None else out_index
            here = held.at[:, pl.ds(start, columns[1])]
            start += columns[1]
            arriving.append(
                pltpu.make_async_copy(
                    source_refs[source_at].at[from_row, :, pl.ds(*columns)],
                    here,
                    sems_in.at[number],
                )
            )
            leaving.append(
                pltpu.make_async_copy(
                    here,
                    out_refs[out_at].at[to_row, :, pl.ds(*out_columns)],
                    sems_out.at[number],
                )
            )
        for copy in arriving:
            copy.start()
        for copy_in, copy_out in zip(arriving, leaving):
            copy_in.wait()
            copy_out.start()
        for copy in leaving:
            copy.wait()

    count = len(plan)
    return pl.pallas_call(
        kernel,
        out_shape=[jax.ShapeDtypeStruct((length, rows, width), low) for length, width in outs],
        grid_spec=pltpu.PrefetchScalarGridSpec(
            num_scalar_prefetch=1,
            grid=(1,),
            in_specs=[pl.BlockSpec(memory_space=pl.ANY)] * len(sources),
            out_specs=[pl.BlockSpec(memory_space=pl.ANY)] * len(outs),
            scratch_shapes=[
                pltpu.VMEM((rows, total), low),
                pltpu.SemaphoreType.DMA((count,)),
                pltpu.SemaphoreType.DMA((count,)),
            ],
        ),
        compiler_params=pltpu.CompilerParams(vmem_limit_bytes=32 * 1024 * 1024),
        cost_estimate=about(1 + 5e-7 * count * rows * total / len(plan)),
        name=name,
    )(table, *sources)


def updated(grad, weight, momentum, average, rate):
    momentum = MOMENTUM * momentum + grad
    weight = weight - rate * (grad + MOMENTUM * momentum)
    return momentum, weight, weight.astype(LOW), AVERAGE * average + (1.0 - AVERAGE) * weight


def update_rows(pieces, state, at, rate, results):
    counts = [grad.shape[0] * width // 128 for grad, _, width in pieces]
    count = sum(counts)
    chunk = 144 if count % 144 == 0 else 128
    total = state[0].shape[0]
    given = [] if results is None else list(results)
    number_of = len(pieces)

    def kernel(*refs):
        grad_refs = refs[:number_of]
        weight_ref, momentum_ref, average_ref = refs[number_of : number_of + 3]
        refs = refs[number_of + 3 + len(given) :]
        outs, arrived = refs[:4], refs[4 : 4 + number_of]
        grad_flat, weight, momentum, average, low, sems = refs[4 + number_of :]
        window = pl.ds(at, count)
        fetched = [
            pltpu.make_async_copy(grad_ref.at[:, pl.ds(start, width)], held, sems.at[3 + number])
            for number, (grad_ref, held, (_, start, width)) in enumerate(
                zip(grad_refs, arrived, pieces)
            )
        ]
        copies = [
            pltpu.make_async_copy(weight_ref.at[window], weight, sems.at[0]),
            pltpu.make_async_copy(momentum_ref.at[window], momentum, sems.at[1]),
            pltpu.make_async_copy(average_ref.at[window], average, sems.at[2]),
        ]
        for copy in fetched + copies:
            copy.start()
        offset = 0
        for copy, held, (grad, _, width) in zip(fetched, arrived, pieces):
            copy.wait()
            rows, per_row = grad.shape[0], width // 128
            for at_now in range(per_row):
                grad_flat[pl.ds(offset + at_now, rows, stride=per_row), :] = held[
                    :, pl.ds(at_now * 128, 128)
                ].astype(jnp.float32)
            offset += rows * per_row
        for copy in copies:
            copy.wait()

        def step(number, carry):
            here = pl.ds(pl.multiple_of(number * chunk, 16), chunk)
            momentum[here], weight[here], low[here], average[here] = updated(
                grad_flat[here], weight[here], momentum[here], average[here], rate
            )
            return carry

        lax.fori_loop(0, count // chunk, step, 0)
        copies = [
            pltpu.make_async_copy(held, out.at[window], sems.at[number])
            for number, (held, out) in enumerate(zip((momentum, weight, low, average), outs))
        ]
        for copy in copies:
            copy.start()
        for copy in copies:
            copy.wait()

    flat = pltpu.VMEM((count, 128), jnp.float32)
    return pl.pallas_call(
        kernel,
        in_specs=[pl.BlockSpec(memory_space=pl.ANY)] * number_of
        + [pl.BlockSpec(memory_space=pltpu.HBM)] * (3 + len(given)),
        out_specs=[pl.BlockSpec(memory_space=pltpu.HBM)] * 4,
        out_shape=[
            jax.ShapeDtypeStruct((total, 128), kind)
            for kind in (jnp.float32, jnp.float32, LOW, jnp.float32)
        ],
        input_output_aliases={number_of + 3 + number: number for number in range(len(given))},
        scratch_shapes=[
            pltpu.VMEM((grad.shape[0], width), grad.dtype) for grad, _, width in pieces
        ]
        + [flat, flat, flat, flat, pltpu.VMEM((count, 128), LOW)]
        + [pltpu.SemaphoreType.DMA((3 + max(number_of, 1),))],
        compiler_params=pltpu.CompilerParams(vmem_limit_bytes=57 * 1024 * 1024),
        cost_estimate=about(1 + count * 0.0016),
        name="update_rows",
    )(*[grad for grad, _, _ in pieces], *state, *given)


def place_blocks(sources, table, widths):
    plan, places = [], []
    for out_at, columns in enumerate(columns_of(widths)):
        number = 0
        for source_at, source in enumerate(sources):
            for at in range(source.shape[0]):
                plan.append((source_at, at, columns, out_at, None, (0, columns[1])))
                places.append(table[number])
                number += 1
    outs = [(16, width) for width in widths]
    return move_blocks(jnp.stack(places).astype(jnp.int32), sources, outs, plan, "place_blocks")


def half_grads(table, left, right, start, total, given):
    tokens, features = left[0].shape
    width = right[0].shape[-1]
    half = features // 2
    rows = half // 8
    tile = next(t for t in (1152, 768, 512, 384, 256) if width % t == 0 and start % t == 0)
    if half > 1152:
        tile = 384
    given = [] if given is None else list(given)

    def kernel(table_ref, own_left, mate_left, own_right, mate_right, *refs):
        give_ref, keep_ref, total_ref = refs[len(given) :]
        for core in range(2):

            @pl.when(table_ref[0] == core)
            def _():
                mine = pl.ds(core * half, half)
                total_ref[...] = dot_tn(own_left[:, mine], own_right[...]) + dot_tn(
                    mate_left[:, mine], mate_right[...]
                )

        for number in range(8):
            block = total_ref[pl.ds(pl.multiple_of(table_ref[1 + number] * rows, 8), rows), :]
            (give_ref, keep_ref)[number // 4][number % 4] = block.astype(LOW)

    first = start // tile
    whole = pl.BlockSpec((tokens, features), lambda i, table: (0, 0))
    part = pl.BlockSpec((tokens, tile), lambda i, table: (0, i))
    out = pl.BlockSpec((4, rows, tile), lambda i, table: (0, 0, first + i))
    return pl.pallas_call(
        kernel,
        grid_spec=pltpu.PrefetchScalarGridSpec(
            num_scalar_prefetch=1,
            grid=(width // tile,),
            in_specs=[whole, whole, part, part]
            + [pl.BlockSpec(memory_space=pl.ANY)] * len(given),
            out_specs=[out, out],
            scratch_shapes=[pltpu.VMEM((half, tile), jnp.float32)],
        ),
        out_shape=[jax.ShapeDtypeStruct((4, rows, total), LOW)] * 2,
        input_output_aliases={5 + number: number for number in range(len(given))},
        compiler_params=pltpu.CompilerParams(vmem_limit_bytes=48 * 1024 * 1024),
        cost_estimate=about(3 + 1.6e-6 * features * width),
        name="half_grads",
    )(table, *left, *right, *given)


class Staged:
    def __init__(self):
        self.core = lax.axis_index("blk")
        self.z_at = lax.axis_index("inner")
        outer_at = lax.axis_index("outer")
        self.y_at = outer_at // 2
        self.x_at = outer_at % 2
        self.own_half = (self.z_at // 2) == self.core
        self.own_row = self.z_at * 4 + outer_at

    def z_pair(self, core):
        low_bit = self.z_at % 2
        return 2 * core + low_bit, 2 * core + 1 - low_bit

    def near_order(self, core, picks):
        found = []
        for far, near in picks:
            first = jnp.where(core == 0, self.x_at, self.y_at) ^ near
            second = jnp.where(core == 0, self.y_at, self.x_at) ^ far
            y_now = jnp.where(core == 0, second, first)
            x_now = jnp.where(core == 0, first, second)
            found.append(y_now * 2 + x_now)
        return found

    def gather_groups(self, groups, gates, early):
        packed = [
            group[0] if len(group) == 1 else jnp.concatenate(group, axis=1) for group in groups
        ]
        table = []
        for core in (self.core, 1 - self.core):
            for outer_at in self.near_order(core, [(0, 0), (0, 1), (1, 0), (1, 1)]):
                for z_now in self.z_pair(core):
                    table.append(z_now * 4 + outer_at)
        last = len(groups) - 1
        held, others, twos, fours, tokens = {}, {}, {}, {}, {}

        def first_stage(k, gates, late):
            own = after(packed[k], *gates)
            came = after(lax.ppermute(own, EVERY, Z_STRAIGHT), *late)
            held[k] = jnp.where(self.own_half, own, came)
            others[k] = lax.ppermute(held[k], "inner", Z_PAIR)

        def second_stage(k, late):
            twos[k] = jnp.stack([held[k], after(others[k], *late)])

        def third_stage(k, late):
            came = after(lax.ppermute(twos[k], EVERY, NEAR_FIRST), *late)
            fours[k] = jnp.concatenate([twos[k], came])

        first_stage(0, (), early[0]())
        second_stage(0, early[1](held[0]))
        first_stage(1, (held[0],), (twos[0],))
        third_stage(0, early[2](twos[0]))
        second_stage(1, (fours[0],))
        for k in range(len(groups)):
            if k + 1 < last:
                first_stage(k + 2, (twos[k + 1],), ())
            far_four = lax.ppermute(fours[k], EVERY, NEAR_SECOND)
            mate_four = lax.ppermute(fours[k], "blk", SWAP)
            if k < last:
                far_four = after(far_four, twos[k + 1])
            else:
                far_four = after(far_four, tokens[k - 1])
            if k < last:
                third_stage(k + 1, (far_four,))
            mate_far = lax.ppermute(far_four, "blk", SWAP)
            if k < last:
                mate_far = after(mate_far, fours[k + 1])
            sources = [fours[k], far_four, mate_four, mate_far]
            widths = [part.shape[1] for part in groups[k]]
            tokens[k] = gates[k](
                [part.reshape(-1, part.shape[-1]) for part in place_blocks(sources, table, widths)]
            )
            if k + 1 < last:
                second_stage(k + 2, (tokens[k],))

    def share(self, value):
        tokens = value.reshape(-1, value.shape[-1])
        return tokens, lax.ppermute(tokens, "blk", SWAP)

    def start_grads(self, pairs):
        return StagedGrads(self, pairs)

    def update(self, state, rate, parts):
        lanes = [array.reshape(-1, 128) for array in state]
        sizes = [rows * cols // (16 * 128) for rows, cols in mat_shapes()]
        results = None
        for entries in parts:
            if isinstance(entries[0][0], StagedGrads) and entries[0][0].stage == 3:
                for part, _, _ in sum(parts, []):
                    if isinstance(part, StagedGrads) and part.stage == 3:
                        part.add(results[0])
            pieces = []
            for part, start, number in entries:
                grad = part.both if isinstance(part, StagedGrads) else part
                pieces.append((grad, start, mat_shapes()[number][1]))
            first = entries[0][2]
            results = update_rows(pieces, lanes, sum(sizes[:first]), rate, results)
        return [result.reshape(-1) for result in results]

    def gather_slots(self, own, between=None):
        four = jnp.concatenate(
            [own] + [lax.ppermute(own, "inner", route) for route in (UP, DOWN, ACROSS)]
        )
        self.token = four
        if between is not None:
            four = after(four, between())
        return jnp.concatenate(
            [four] + [lax.ppermute(four, "outer", route) for route in (OUT_X, OUT_Y, OUT_XY)]
        )

    def swap_slots(self, parts, between):
        parts = parts.reshape((4, 4) + parts.shape[1:])
        four = jnp.stack(
            [parts[0]]
            + [
                lax.ppermute(parts[1 + at], "outer", route)
                for at, route in enumerate((OUT_X, OUT_Y, OUT_XY))
            ]
        )
        four = after(four, between())
        return jnp.stack(
            [four[:, 0]]
            + [
                lax.ppermute(four[:, 1 + at], "inner", route)
                for at, route in enumerate((DOWN, UP, ACROSS))
            ],
        )

    def reduce_slots(self, parts, late):
        parts = parts.reshape((4, 4) + parts.shape[1:])
        four = parts[0]
        for at, route in enumerate((OUT_X, OUT_Y, OUT_XY)):
            four = four + after(lax.ppermute(parts[1 + at], "outer", route), late)
        self.token = four
        total = four[0]
        for at, route in enumerate((DOWN, UP, ACROSS)):
            total = total + lax.ppermute(four[1 + at], "inner", route)
        return total

    def slot_rows(self):
        found = []
        for z_now in range(4):
            away = (z_now - self.z_at) % 4
            z_slot = jnp.where(away == 0, 0, jnp.where(away == 3, 1, jnp.where(away == 1, 2, 3)))
            for outer_now in range(4):
                flip = jnp.bitwise_xor(outer_now, self.y_at * 2 + self.x_at)
                found.append((flip, z_slot))
        return found

    def rows_in_order(self, slots):
        table = [flip * 4 + z_slot for flip, z_slot in self.slot_rows()]
        return jnp.take(slots, jnp.stack(table), axis=0)

    def swapped_in_order(self, came):
        table = []
        for flip, z_slot in self.slot_rows():
            came_at = jnp.where(z_slot == 1, 2, jnp.where(z_slot == 2, 1, z_slot))
            table.append(came_at * 4 + flip)
        return jnp.take(came.reshape(16, -1), jnp.stack(table), axis=0)


class StagedGrads:
    def __init__(self, moves, pairs):
        self.moves = moves
        low_bit = moves.z_at % 2
        table = [moves.core]
        for outer_at in moves.near_order(moves.core, [(1, 1), (1, 0), (0, 1), (0, 0)]):
            for z_now in (low_bit, 1 - low_bit):
                table.append(z_now * 4 + outer_at)
        table = jnp.stack(table).astype(jnp.int32)
        total = sum(right[0].shape[-1] for _, right in pairs)
        start, found = 0, None
        for left, right in pairs:
            found = half_grads(table, left, right, start, total, found)
            start += right[0].shape[-1]
        self.give, self.keep = found
        self.token = self.give
        self.stage = 0

    def send(self, *gates):
        self.give = after(self.give, *gates) if gates else self.give
        axes, route = (
            (EVERY, NEAR_SECOND),
            (EVERY, NEAR_FIRST),
            ("inner", Z_PAIR),
            (EVERY, flipped(Z_STRAIGHT)),
        )[self.stage]
        self.came = lax.ppermute(self.give, axes, route)

    def add(self, *late):
        came = after(self.came, *late) if late else self.came
        total = self.keep.astype(jnp.float32) + came.astype(jnp.float32)
        if self.stage == 0:
            self.give = total[:2].astype(LOW)
            self.keep = total[2:].astype(LOW)
        elif self.stage == 1:
            self.give = total[1].astype(LOW)
            self.keep = total[0].astype(LOW)
        else:
            self.give = self.keep = total.astype(LOW)
        if self.stage == 3:
            mate = lax.ppermute(self.give, "blk", SWAP)
            self.both = jnp.where(self.moves.own_half, self.give, mate)
        self.token = self.give
        self.stage += 1


def outer_sum(left_arr, right_arr):
    return jnp.einsum("sni,snj->ij", left_arr, right_arr, preferred_element_type=jnp.float32)


class DirectGrads:
    def __init__(self, pairs):
        self.parts = [outer_sum(left[0], right[0]).astype(LOW) for left, right in pairs]
        self.token = self.parts[0]

    def send(self, *gates):
        pass

    def add(self, *late):
        pass

    @functools.cached_property
    def result(self):
        found = []
        for grad in self.parts:
            part = lax.psum_scatter(grad, GROUP, scatter_dimension=0, tiled=True)
            found.append(lax.psum(part, "blk").astype(jnp.float32))
        return found


class Direct:
    def __init__(self):
        self.core = lax.axis_index("blk")
        self.own_row = lax.axis_index("inner") * lax.axis_size("outer") + lax.axis_index("outer")

    def gather_groups(self, groups, gates, early):
        early[0]()
        early[1](groups[0][0])
        early[2](groups[0][0])
        for group, gate in zip(groups, gates):
            gate([lax.all_gather(part, GROUP, axis=0, tiled=True) for part in group])

    def share(self, value):
        return (value,)

    def start_grads(self, pairs):
        return DirectGrads(pairs)

    def update(self, state, rate, parts):
        found = {}
        for part, start, number in sum(parts, []):
            whole = jnp.concatenate(part.result, axis=1) if isinstance(part, DirectGrads) else part
            found[number] = whole[:, start : start + mat_shapes()[number][1]]
        grad = jnp.concatenate([found[number].reshape(-1) for number in sorted(found)])
        return updated(grad, *state, rate)

    def gather_slots(self, own, between=None):
        self.token = own
        if between is not None:
            between()
        return lax.all_gather(own, GROUP, axis=0, tiled=True)

    def reduce_slots(self, parts, late):
        self.token = parts
        return lax.psum_scatter(parts, GROUP, scatter_dimension=0, tiled=False)

    def swap_slots(self, parts, between):
        between()
        return lax.all_gather(parts, GROUP, axis=0)

    def rows_in_order(self, slots):
        return slots

    def swapped_in_order(self, came):
        mine = lax.dynamic_index_in_dim(came, self.own_row, 1, keepdims=False)
        return mine.reshape(mine.shape[0], -1)


def time_embed(steps_t):
    half_dim = D // 2
    frequency = jnp.exp(-math.log(10000.0) * jnp.arange(half_dim, dtype=jnp.float32) / half_dim)
    angles = steps_t.astype(jnp.float32)[:, None] * frequency[None, :]
    return jnp.concatenate([jnp.cos(angles), jnp.sin(angles)], axis=1)


def modulate(values, scale_v, shift_v):
    center = values - jnp.mean(values, axis=-1, keepdims=True)
    normed = center * lax.rsqrt(jnp.mean(center * center, axis=-1, keepdims=True) + EPS_NORM)
    return normed * (1.0 + scale_v[:, None, :]) + shift_v[:, None, :]


def gelu_tanh(values):
    return jax.nn.gelu(values, approximate=True)


def rms_unit(values):
    return values * lax.rsqrt(jnp.mean(values * values, axis=-1, keepdims=True) + EPS_NORM)


def matmul(left_arr, right_arr):
    return jnp.einsum("...i,ij->...j", left_arr, right_arr, preferred_element_type=jnp.float32)


def matmul_t(left_arr, right_arr):
    return jnp.einsum("...j,ij->...i", left_arr, right_arr, preferred_element_type=jnp.float32)


def column_sum(tensor):
    return jnp.sum(tensor.astype(jnp.float32), axis=(0, 1))


def attention(queries, near_kv, far_kv):
    images, rows, _ = queries.shape
    heads = D // E

    def kernel(q_ref, near_ref, far_ref, out_ref):
        for head in range(heads):
            own = pl.ds(head * E, E)
            other = pl.ds(D + head * E, E)
            q_now = q_ref[0, :, own]
            keys = jnp.concatenate([near_ref[0, :, own], far_ref[0, :, own]], axis=0)
            values = jnp.concatenate([near_ref[0, :, other], far_ref[0, :, other]], axis=0)
            scores = dot_nt(keys, q_now) * E ** (-0.5)
            top = jnp.max(scores, axis=0, keepdims=True)
            weight = jnp.exp(scores - top)
            probs = weight * (1.0 / jnp.sum(weight, axis=0, keepdims=True))
            out_ref[0, :, own] = dot_tn(probs.astype(LOW), values).astype(LOW)

    block = pl.BlockSpec((1, rows, D), lambda i: (i, 0, 0))
    block_kv = pl.BlockSpec((1, rows, 2 * D), lambda i: (i, 0, 0))
    return pl.pallas_call(
        kernel,
        grid=(images,),
        in_specs=[block, block_kv, block_kv],
        out_specs=block,
        out_shape=jax.ShapeDtypeStruct(queries.shape, LOW),
        compiler_params=pltpu.CompilerParams(vmem_limit_bytes=32 * 1024 * 1024),
        cost_estimate=about(14 * images / 4),
        name="attention",
    )(queries, near_kv, far_kv)


def attention_grads(queries, near_kv, far_kv, grad_att):
    images, rows, _ = queries.shape
    heads = D // E

    def kernel(q_ref, near_ref, far_ref, grad_ref, dq_ref, dnear_ref, dfar_ref):
        for head in range(heads):
            own = pl.ds(head * E, E)
            other = pl.ds(D + head * E, E)
            q_now = q_ref[0, :, own]
            g_now = grad_ref[0, :, own]
            keys = jnp.concatenate([near_ref[0, :, own], far_ref[0, :, own]], axis=0)
            values = jnp.concatenate([near_ref[0, :, other], far_ref[0, :, other]], axis=0)
            scores = dot_nt(keys, q_now) * E ** (-0.5)
            top = jnp.max(scores, axis=0, keepdims=True)
            weight = jnp.exp(scores - top)
            probs = weight * (1.0 / jnp.sum(weight, axis=0, keepdims=True))
            grad_probs = dot_nt(values, g_now)
            delta = jnp.sum(probs * grad_probs, axis=0, keepdims=True)
            grad_scores = (probs * (grad_probs - delta)).astype(LOW)
            dq_ref[0, :, own] = (dot_tn(grad_scores, keys) * E ** (-0.5)).astype(LOW)
            grad_keys = dot_nn(grad_scores, q_now) * E ** (-0.5)
            grad_values = dot_nn(probs.astype(LOW), g_now)
            dnear_ref[0, :, own] = grad_keys[:rows]
            dnear_ref[0, :, other] = grad_values[:rows]
            dfar_ref[0, :, own] = grad_keys[rows:].astype(LOW)
            dfar_ref[0, :, other] = grad_values[rows:].astype(LOW)

    block = pl.BlockSpec((1, rows, D), lambda i: (i, 0, 0))
    block_kv = pl.BlockSpec((1, rows, 2 * D), lambda i: (i, 0, 0))
    return pl.pallas_call(
        kernel,
        grid=(images,),
        in_specs=[block, block_kv, block_kv, block],
        out_specs=[block, block_kv, block_kv],
        out_shape=[
            jax.ShapeDtypeStruct(queries.shape, LOW),
            jax.ShapeDtypeStruct(near_kv.shape, jnp.float32),
            jax.ShapeDtypeStruct(far_kv.shape, LOW),
        ],
        compiler_params=pltpu.CompilerParams(vmem_limit_bytes=32 * 1024 * 1024),
        cost_estimate=about(21 * images / 4),
        name="attention_grads",
    )(queries, near_kv, far_kv, grad_att)


def dot_nn(left, right):
    return lax.dot_general(
        left, right, (((1,), (0,)), ((), ())), preferred_element_type=jnp.float32
    )


def dot_nt(left, right):
    return lax.dot_general(
        left, right, (((1,), (1,)), ((), ())), preferred_element_type=jnp.float32
    )


def dot_tn(left, right):
    return lax.dot_general(
        left, right, (((0,), (0,)), ((), ())), preferred_element_type=jnp.float32
    )


def body(
    hidden,
    labels,
    steps_t,
    live_slots,
    label_table,
    targets,
    cotangent,
    weights,
    weight_momentum,
    weight_average,
    biases,
    bias_momentum,
    bias_average,
):
    n_inner = lax.axis_size("inner")
    n_outer = lax.axis_size("outer")
    blocks = n_inner * n_outer
    slots = hidden.shape[0]
    local_tok = hidden.shape[1]
    moves = Staged() if (n_inner, n_outer) == (4, 4) else Direct()
    p_qkv, p_proj, p_up, p_down, p_ada, p_one, p_two, p_three = split_shard(
        weights.astype(LOW), mat_shapes(), blocks
    )
    bias_low = biases.astype(LOW)
    condition = label_table[labels].astype(jnp.float32) + time_embed(steps_t)
    cond_act, silu_cond = jax.vjp(jax.nn.silu, condition)
    cond_low = cond_act.astype(LOW)
    kept = {}
    rows_d = D // blocks
    half_ada = 3 * D

    def early_gather():
        packed = jnp.concatenate([cond_low, bias_low.reshape(slots, -1)], axis=1)
        kept["packed"] = moves.gather_slots(packed)
        return (moves.token,)

    def early_product(gate):
        packed_all = after(kept["packed"], gate)
        cond_own = lax.dynamic_slice_in_dim(
            packed_all[:, :D], moves.own_row * rows_d, rows_d, 1
        )
        ada_half = lax.dynamic_slice_in_dim(p_ada, moves.core * half_ada, half_ada, 1)
        mod_part = matmul(cond_own, ada_half).reshape(blocks, slots, half_ada)
        kept.update(cond_own=cond_own, mod_part=mod_part)
        return (mod_part,)

    def early_modulation(gate):
        mod_half = moves.reduce_slots(kept["mod_part"], gate)
        late = moves.token
        mod_mate = lax.ppermute(mod_half, "blk", SWAP)
        bias_all = moves.rows_in_order(kept["packed"][:, D:].reshape(blocks, -1))
        biases_now = unpack_rows(bias_all.astype(jnp.float32), bias_shapes())
        b_ada = biases_now[5]
        kept["biases"] = biases_now
        modulation = (
            jnp.concatenate(
                [
                    jnp.where(moves.core == 0, mod_half, mod_mate),
                    jnp.where(moves.core == 0, mod_mate, mod_half),
                ],
                axis=1,
            )
            + b_ada
        )
        shift_a, scale_a, gate_a, shift_m, scale_m, gate_m = [
            modulation[:, part_idx * D : (part_idx + 1) * D] for part_idx in range(6)
        ]
        hidden_f = hidden.astype(jnp.float32)
        mixed_a, pull_a = jax.vjp(modulate, hidden_f, scale_a, shift_a)
        mixed_a_low = mixed_a.astype(LOW)
        left_qkv = moves.share(mixed_a_low)
        kept.update(
            gates=(gate_a, gate_m), scale_m=scale_m, shift_m=shift_m, hidden_f=hidden_f,
            mixed_a_low=mixed_a_low, pull_a=pull_a, left_qkv=left_qkv,
        )
        return (late,)

    def use_first(arrived):
        b_q, b_v = kept["biases"][:2]
        (w_qkv,) = arrived
        qkv_bias = jnp.concatenate([b_q, jnp.zeros((D,), jnp.float32), b_v])
        qkv_low = (matmul(kept["mixed_a_low"], w_qkv) + qkv_bias).astype(LOW)
        near_kv = qkv_low[..., D:]
        far_kv = passed_along(near_kv, "blk", 1)
        kept.update(w_qkv=w_qkv, queries=qkv_low[..., :D], near_kv=near_kv, far_kv=far_kv)
        return far_kv
    def use_second(arrived):
        w_proj, w_one = arrived
        b_proj = kept["biases"][2]
        queries, near_kv, far_kv = kept["queries"], kept["near_kv"], kept["far_kv"]
        queries = after(queries, w_proj)
        att_low = attention(queries, near_kv, far_kv)
        left_proj = moves.share(att_low)
        branch_a = matmul(att_low, w_proj) + b_proj
        residual = kept["hidden_f"] + kept["gates"][0][:, None, :] * branch_a
        mixed_m, pull_m = jax.vjp(modulate, residual, kept["scale_m"], kept["shift_m"])
        mixed_m_low = mixed_m.astype(LOW)
        left_up = moves.share(mixed_m_low)
        kept.update(
            w_proj=w_proj, w_one=w_one, left_proj=left_proj,
            branch_a=branch_a, residual=residual, pull_m=pull_m, left_up=left_up,
            mixed_m_low=mixed_m_low,
        )
        return mixed_m_low

    def use_third(arrived):
        (w_up,) = arrived
        b_up = kept["biases"][3]
        pre_act = matmul(kept["mixed_m_low"], w_up) + b_up
        activated, gelu_pull = jax.vjp(gelu_tanh, pre_act)
        act_low = activated.astype(LOW)
        gelu_slope = gelu_pull(jnp.ones_like(pre_act))[0]
        left_down = moves.share(act_low)
        act_low, gelu_slope = lax.optimization_barrier((act_low, gelu_slope))
        kept.update(w_up=w_up, gelu_slope=gelu_slope, act_low=act_low, left_down=left_down)
        return act_low

    def use_fourth(arrived):
        (w_down,) = arrived
        b_down, c_one = kept["biases"][4], kept["biases"][6]
        branch_m = matmul(kept["act_low"], w_down) + b_down
        output = kept["residual"] + kept["gates"][1][:, None, :] * branch_m
        out_low = output.astype(LOW)
        left_one = moves.share(out_low)
        hid_one = matmul(out_low, kept["w_one"]) + c_one
        act_one, silu_one = jax.vjp(jax.nn.silu, hid_one)
        one_low = act_one.astype(LOW)
        left_two = moves.share(one_low)
        kept.update(
            w_down=w_down, branch_m=branch_m, out_low=out_low, left_one=left_one,
            silu_one=silu_one, one_low=one_low, left_two=left_two,
        )
        return one_low

    def use_fifth(arrived):
        w_two, w_three = arrived
        c_two, c_three = kept["biases"][7:]
        hid_two = matmul(kept["one_low"], w_two) + c_two
        act_two, silu_two = jax.vjp(jax.nn.silu, hid_two)
        two_low = act_two.astype(LOW)
        left_three = moves.share(two_low)
        projection = matmul(two_low, w_three) + c_three
        kept.update(
            w_two=w_two, w_three=w_three, silu_two=silu_two, left_three=left_three,
            projection=projection,
        )

    moves.gather_groups(
        [[p_qkv], [p_proj, p_one], [p_up], [p_down], [p_two, p_three]],
        [use_first, use_second, use_third, use_fourth, use_fifth],
        [early_gather, early_product, early_modulation],
    )
    w_qkv, w_proj, w_up, w_down, w_one, w_two, w_three = [
        kept[name] for name in ("w_qkv", "w_proj", "w_up", "w_down", "w_one", "w_two", "w_three")
    ]
    gate_a, gate_m = kept["gates"]
    cond_own = kept["cond_own"]
    pull_a, left_qkv = kept["pull_a"], kept["left_qkv"]
    queries, near_kv, far_kv = [kept[name] for name in ("queries", "near_kv", "far_kv")]
    branch_a, branch_m, out_low, projection = [
        kept[name] for name in ("branch_a", "branch_m", "out_low", "projection")
    ]
    pull_m, gelu_slope, silu_one, silu_two = [
        kept[name] for name in ("pull_m", "gelu_slope", "silu_one", "silu_two")
    ]
    live_f = live_slots.astype(jnp.float32)[:, None, None]
    unit_proj, unit_pull = jax.vjp(rms_unit, projection)
    grad_proj = unit_pull(-LAMBDA_REPA * live_f * rms_unit(targets.astype(jnp.float32)))[0].astype(
        LOW
    )
    right_three = moves.share(grad_proj)
    grad_cthree = column_sum(grad_proj)
    grad_htwo = silu_two(matmul_t(grad_proj, w_three))[0].astype(LOW)
    right_two = moves.share(grad_htwo)
    grad_ctwo = column_sum(grad_htwo)
    grad_hone = silu_one(matmul_t(grad_htwo, w_two))[0].astype(LOW)
    right_one = moves.share(grad_hone)
    grads_fourth = moves.start_grads(
        [(kept["left_two"], right_two), (kept["left_three"], right_three)]
    )
    grad_cone = column_sum(grad_hone)
    grads_fourth.send()
    right_one = after_all(right_one, grads_fourth.token)
    grads_one = moves.start_grads([(kept["left_one"], right_one)])
    grads_one.send()
    grad_hone = after(grad_hone, grads_one.token)
    grad_output = cotangent.astype(jnp.float32) * live_f + matmul_t(grad_hone, w_one)
    grad_gate_m = jnp.sum(grad_output * branch_m, axis=1)
    grad_bm = (gate_m[:, None, :] * grad_output).astype(LOW)
    right_down = moves.share(grad_bm)
    grad_bdown = column_sum(grad_bm)
    grad_pre = (matmul_t(grad_bm, w_down) * gelu_slope).astype(LOW)
    right_up = moves.share(grad_pre)
    grads_down = moves.start_grads([(kept["left_down"], right_down)])
    grad_bup = column_sum(grad_pre)
    grads_down.send()
    grads_fourth.add(grads_down.token)
    grads_fourth.send()
    grad_pre = after(grad_pre, grads_down.token, grads_fourth.token)
    grad_res_m, grad_scale_m, grad_shift_m = pull_m(matmul_t(grad_pre, w_up))
    grad_residual = grad_output + grad_res_m
    grad_gate_a = jnp.sum(grad_residual * branch_a, axis=1)
    grad_ba = (gate_a[:, None, :] * grad_residual).astype(LOW)
    right_proj = moves.share(grad_ba)
    grad_bproj = column_sum(grad_ba)
    grad_att = matmul_t(grad_ba, w_proj).astype(LOW)
    grads_one.add(grad_att)
    grads_one.send()
    grads_fourth.add(grad_att)
    grads_fourth.send()
    right_up = after_all(right_up, grads_fourth.token, grads_one.token)
    grads_up = moves.start_grads([(kept["left_up"], right_up), (kept["left_proj"], right_proj)])
    grads_up.send()
    grads_down.add(grads_up.token)
    grads_down.send()
    grads_one.add(grads_up.token)
    grads_one.send()
    grads_fourth.add(grads_up.token)
    grads_fourth.send()
    grad_att = after(
        grad_att, grads_up.token, grads_down.token, grads_one.token, grads_fourth.token
    )
    grad_query, near_dkv, far_dkv = attention_grads(queries, near_kv, far_kv, grad_att)
    home_dkv = passed_along(far_dkv, "blk", -1)
    grads_down.add(grad_query)
    grads_down.send()
    grads_fourth.add(grad_query)
    grads_one.add(grad_query)
    grads_one.send()
    home_dkv = after(home_dkv, grads_down.token, grads_one.token, grads_fourth.token)
    grad_kv = (near_dkv + home_dkv.astype(jnp.float32)).astype(LOW)
    grad_qkv = jnp.concatenate([grad_query, grad_kv], axis=-1)
    grads_first = moves.start_grads([(left_qkv, moves.share(grad_qkv))])
    qkv_sums = column_sum(grad_qkv)
    grads_first.send()
    grads_down.add(grads_first.token)
    grads_down.send()
    grads_one.add(grads_first.token)
    grad_qkv = after(grad_qkv, grads_first.token, grads_down.token, grads_one.token)
    grad_hid_a, grad_scale_a, grad_shift_a = pull_a(matmul_t(grad_qkv, w_qkv))
    grad_input = grad_residual + grad_hid_a
    grad_mod_part = jnp.concatenate(
        [grad_shift_a, grad_scale_a, grad_gate_a, grad_shift_m, grad_scale_m, grad_gate_m], axis=1
    )
    bias_terms = (
        qkv_sums[:D],
        qkv_sums[2 * D :],
        grad_bproj,
        grad_bup,
        grad_bdown,
        grad_cone,
        grad_ctwo,
        grad_cthree,
    )
    bias_grid = jnp.concatenate(
        [segment.reshape(blocks, -1) for segment in bias_terms], axis=1
    ).reshape(slots, -1)
    grad_small = jnp.concatenate([grad_mod_part, bias_grid], axis=1)
    small_came = lax.ppermute(grad_small, "blk", SWAP)
    grads_up.add(grad_small)
    grads_up.send()
    grads_first.add(grads_up.token)
    grads_first.send()
    small_came = after(small_came, grads_up.token, grads_first.token)
    grad_small = (grad_small + small_came).astype(LOW)
    small_all = moves.gather_slots(grad_small)
    grads_first.add(small_all)
    grads_first.send()
    grads_up.add(small_all)
    grads_up.send()
    small_all = after(small_all, grads_first.token, grads_up.token)

    def between_swaps():
        grads_first.add()
        grads_first.send()
        grads_up.add()
        grads_up.send()
        return lax.optimization_barrier((grads_up.token, grads_first.token))[0]

    grad_mod = small_all[:, : 6 * D]
    cond_cols = matmul_t(grad_mod, p_ada).reshape(blocks, slots, rows_d)
    cond_rows = moves.swapped_in_order(moves.swap_slots(cond_cols, between_swaps))
    grad_cond = silu_cond(
        cond_rows.reshape(blocks, slots, rows_d).transpose(1, 0, 2).reshape(slots, D)
    )[0]
    grad_wada = jnp.einsum("si,sj->ij", cond_own, grad_mod, preferred_element_type=jnp.float32)
    grad_bada = lax.dynamic_index_in_dim(
        jnp.sum(grad_mod.astype(jnp.float32), axis=0).reshape(blocks, -1),
        moves.own_row,
        0,
        keepdims=False,
    )
    bias_sums = jnp.sum(
        small_all[:, 6 * D :].astype(jnp.float32).reshape(blocks, slots, -1), axis=0
    )
    bias_own = lax.dynamic_index_in_dim(
        bias_sums.reshape(blocks, -1), moves.own_row, 0, keepdims=False
    )
    ada_at = (3 * D + FF + D) // blocks
    grad_b_flat = jnp.concatenate([bias_own[:ada_at], grad_bada, bias_own[ada_at:]])
    grads_down.add(grad_mod_part)
    images_all = slots * blocks
    tokens_img = local_tok * lax.axis_size("blk")
    rate_w = LR_COEF / math.sqrt(images_all * tokens_img)
    rate_b = BIAS_FACTOR * rate_w
    mom_w, new_w, low_w, avg_w = moves.update(
        (weights, weight_momentum, weight_average),
        rate_w,
        [
            [(grads_fourth, 0, 6)],
            [(grads_fourth, PH, 7)],
            [(grads_one, 0, 5)],
            [(grads_down, 0, 3)],
            [(grad_wada, 0, 4)],
            [(grads_up, 0, 2)],
            [(grads_first, 0, 0), (grads_up, FF, 1)],
        ],
    )
    mom_b = MOMENTUM * bias_momentum + grad_b_flat
    new_b = biases - rate_b * (grad_b_flat + MOMENTUM * mom_b)
    avg_b = AVERAGE * bias_average + (1.0 - AVERAGE) * new_b
    return (
        out_low,
        grad_input,
        grad_cond,
        mom_w,
        new_w,
        low_w,
        avg_w,
        mom_b,
        new_b,
        new_b.astype(LOW),
        avg_b,
    )


def solution(mesh):
    in_specs = (
        P(("inner", "outer"), "blk", None),
        P(("inner", "outer")),
        P(("inner", "outer")),
        P(("inner", "outer")),
        P(),
        P(("inner", "outer"), "blk", None),
        P(("inner", "outer"), "blk", None),
        P(("inner", "outer")),
        P(("inner", "outer")),
        P(("inner", "outer")),
        P(("inner", "outer")),
        P(("inner", "outer")),
        P(("inner", "outer")),
    )
    out_specs = (
        P(("inner", "outer"), "blk", None),
        P(("inner", "outer"), "blk", None),
        P(("inner", "outer"), None),
        P(("inner", "outer")),
        P(("inner", "outer")),
        P(("inner", "outer")),
        P(("inner", "outer")),
        P(("inner", "outer")),
        P(("inner", "outer")),
        P(("inner", "outer")),
        P(("inner", "outer")),
    )
    return jax.shard_map(body, mesh=mesh, in_specs=in_specs, out_specs=out_specs, check_vma=False)
```

```python
import functools
import math

import jax
import jax.numpy as jnp
from jax import lax
from jax.experimental import pallas as pl
from jax.experimental.pallas import tpu as pltpu
from jax.sharding import PartitionSpec as P

E = 72
D = 1152
FF = 4608
PH = 2048
ZD = 768


LAMBDA_REPA = 0.5
MOMENTUM = 0.5
AVERAGE = 0.5
LR_COEF = 0.04
BIAS_FACTOR = 4.0
EPS_NORM = 1e-06
GROUP = ("inner", "outer")
EVERY = ("blk", "inner", "outer")
LOW = jnp.bfloat16


def passed_along(block, axis, distance):
    devices = range(lax.axis_size(axis))
    route = [((i - distance) % len(devices), i) for i in devices]
    return lax.ppermute(block, axis, route)


def mat_shapes():
    return [(D, 3 * D), (D, D), (D, FF), (FF, D), (D, 6 * D), (D, PH), (PH, PH), (PH, ZD)]


def bias_shapes():
    return [(D,), (D,), (D,), (FF,), (D,), (6 * D,), (PH,), (PH,), (ZD,)]


def split_shard(flat_vec, shapes, blocks):
    segments = []
    offset = 0
    for shape_now in shapes:
        rows_here = shape_now[0] // blocks
        length = rows_here * math.prod(shape_now[1:])
        segments.append(
            flat_vec[offset : offset + length].reshape((rows_here,) + tuple(shape_now[1:]))
        )
        offset += length
    return segments


def unpack_rows(line_grid, shapes):
    blocks = line_grid.shape[0]
    segments = []
    offset = 0
    for shape_now in shapes:
        length = shape_now[0] // blocks * math.prod(shape_now[1:])
        segments.append(line_grid[:, offset : offset + length].reshape(shape_now))
        offset += length
    return segments


def flat_id(core, z_at, outer_at):
    return (core * 4 + z_at) * 4 + outer_at


def route_z(pairs_core0):
    route = []
    for z_from, z_to in pairs_core0:
        for outer_at in range(4):
            route.append((flat_id(0, z_from, outer_at), flat_id(0, z_to, outer_at)))
            route.append((flat_id(1, 3 - z_from, outer_at), flat_id(1, 3 - z_to, outer_at)))
    return route


def flipped(route):
    return [(target, source) for source, target in route]


def route_xy(step_core0, step_core1):
    route = []
    for z_at in range(4):
        for outer_at in range(4):
            for core, step in ((0, step_core0), (1, step_core1)):
                route.append((flat_id(core, z_at, outer_at), flat_id(core, z_at, outer_at ^ step)))
    return route


STEP_X, STEP_Y = 1, 2
NEAR_FIRST = route_xy(STEP_X, STEP_Y)
NEAR_SECOND = route_xy(STEP_Y, STEP_X)
Z_PAIR = [(0, 1), (1, 0), (2, 3), (3, 2)]
Z_STRAIGHT = route_z([(0, 2), (1, 3)])
SWAP = [(0, 1), (1, 0)]
UP = [(0, 1), (1, 2), (2, 3), (3, 0)]
DOWN = [(1, 0), (2, 1), (3, 2), (0, 3)]
ACROSS = [(0, 2), (2, 0), (1, 3), (3, 1)]
OUT_X = [(0, 1), (1, 0), (2, 3), (3, 2)]
OUT_Y = [(0, 2), (2, 0), (1, 3), (3, 1)]
OUT_XY = [(0, 3), (3, 0), (1, 2), (2, 1)]


def after(value, *others):
    return lax.optimization_barrier((value,) + others)[0]


def after_all(values, *others):
    return lax.optimization_barrier(tuple(values) + others)[: len(values)]


def about(micros):
    return pl.CostEstimate(flops=0, transcendentals=0, bytes_accessed=int(micros * 3.3e6))


def columns_of(widths):
    found, start = [], 0
    for width in widths:
        found.append((start, width))
        start += width
    return found


def move_blocks(table, sources, outs, plan, name):
    rows = sources[0].shape[1]
    low = sources[0].dtype
    widths = [columns[1] for _, _, columns, _, _, _ in plan]
    total = sum(widths)

    def kernel(table_ref, *refs):
        source_refs = refs[: len(sources)]
        out_refs = refs[len(sources) : len(sources) + len(outs)]
        held, sems_in, sems_out = refs[len(sources) + len(outs) :]
        arriving, leaving = [], []
        start = 0
        for number, (source_at, index, columns, out_at, out_index, out_columns) in enumerate(plan):
            from_row = table_ref[number] if index is None else index
            to_row = table_ref[number] if out_index is None else out_index
            here = held.at[:, pl.ds(start, columns[1])]
            start += columns[1]
            arriving.append(
                pltpu.make_async_copy(
                    source_refs[source_at].at[from_row, :, pl.ds(*columns)],
                    here,
                    sems_in.at[number],
                )
            )
            leaving.append(
                pltpu.make_async_copy(
                    here,
                    out_refs[out_at].at[to_row, :, pl.ds(*out_columns)],
                    sems_out.at[number],
                )
            )
        for copy in arriving:
            copy.start()
        for copy_in, copy_out in zip(arriving, leaving):
            copy_in.wait()
            copy_out.start()
        for copy in leaving:
            copy.wait()

    count = len(plan)
    return pl.pallas_call(
        kernel,
        out_shape=[jax.ShapeDtypeStruct((length, rows, width), low) for length, width in outs],
        grid_spec=pltpu.PrefetchScalarGridSpec(
            num_scalar_prefetch=1,
            grid=(1,),
            in_specs=[pl.BlockSpec(memory_space=pl.ANY)] * len(sources),
            out_specs=[pl.BlockSpec(memory_space=pl.ANY)] * len(outs),
            scratch_shapes=[
                pltpu.VMEM((rows, total), low),
                pltpu.SemaphoreType.DMA((count,)),
                pltpu.SemaphoreType.DMA((count,)),
            ],
        ),
        compiler_params=pltpu.CompilerParams(vmem_limit_bytes=32 * 1024 * 1024),
        cost_estimate=about(1 + 5e-7 * count * rows * total / len(plan)),
        name=name,
    )(table, *sources)


def updated(grad, weight, momentum, average, rate):
    momentum = MOMENTUM * momentum + grad
    weight = weight - rate * (grad + MOMENTUM * momentum)
    return momentum, weight, weight.astype(LOW), AVERAGE * average + (1.0 - AVERAGE) * weight


def update_rows(pieces, state, at, rate, results):
    counts = [grad.shape[0] * width // 128 for grad, _, width in pieces]
    count = sum(counts)
    chunk = 144 if count % 144 == 0 else 128
    total = state[0].shape[0]
    given = [] if results is None else list(results)
    number_of = len(pieces)

    def kernel(*refs):
        grad_refs = refs[:number_of]
        weight_ref, momentum_ref, average_ref = refs[number_of : number_of + 3]
        refs = refs[number_of + 3 + len(given) :]
        outs, arrived = refs[:4], refs[4 : 4 + number_of]
        grad_flat, weight, momentum, average, low, sems = refs[4 + number_of :]
        window = pl.ds(at, count)
        fetched = [
            pltpu.make_async_copy(grad_ref.at[:, pl.ds(start, width)], held, sems.at[3 + number])
            for number, (grad_ref, held, (_, start, width)) in enumerate(
                zip(grad_refs, arrived, pieces)
            )
        ]
        copies = [
            pltpu.make_async_copy(weight_ref.at[window], weight, sems.at[0]),
            pltpu.make_async_copy(momentum_ref.at[window], momentum, sems.at[1]),
            pltpu.make_async_copy(average_ref.at[window], average, sems.at[2]),
        ]
        for copy in fetched + copies:
            copy.start()
        offset = 0
        for copy, held, (grad, _, width) in zip(fetched, arrived, pieces):
            copy.wait()
            rows, per_row = grad.shape[0], width // 128
            for at_now in range(per_row):
                grad_flat[pl.ds(offset + at_now, rows, stride=per_row), :] = held[
                    :, pl.ds(at_now * 128, 128)
                ].astype(jnp.float32)
            offset += rows * per_row
        for copy in copies:
            copy.wait()

        def step(number, carry):
            here = pl.ds(pl.multiple_of(number * chunk, 16), chunk)
            momentum[here], weight[here], low[here], average[here] = updated(
                grad_flat[here], weight[here], momentum[here], average[here], rate
            )
            return carry

        lax.fori_loop(0, count // chunk, step, 0)
        copies = [
            pltpu.make_async_copy(held, out.at[window], sems.at[number])
            for number, (held, out) in enumerate(zip((momentum, weight, low, average), outs))
        ]
        for copy in copies:
            copy.start()
        for copy in copies:
            copy.wait()

    flat = pltpu.VMEM((count, 128), jnp.float32)
    return pl.pallas_call(
        kernel,
        in_specs=[pl.BlockSpec(memory_space=pl.ANY)] * number_of
        + [pl.BlockSpec(memory_space=pltpu.HBM)] * (3 + len(given)),
        out_specs=[pl.BlockSpec(memory_space=pltpu.HBM)] * 4,
        out_shape=[
            jax.ShapeDtypeStruct((total, 128), kind)
            for kind in (jnp.float32, jnp.float32, LOW, jnp.float32)
        ],
        input_output_aliases={number_of + 3 + number: number for number in range(len(given))},
        scratch_shapes=[
            pltpu.VMEM((grad.shape[0], width), grad.dtype) for grad, _, width in pieces
        ]
        + [flat, flat, flat, flat, pltpu.VMEM((count, 128), LOW)]
        + [pltpu.SemaphoreType.DMA((3 + max(number_of, 1),))],
        compiler_params=pltpu.CompilerParams(vmem_limit_bytes=57 * 1024 * 1024),
        cost_estimate=about(1 + count * 0.0016),
        name="update_rows",
    )(*[grad for grad, _, _ in pieces], *state, *given)


def place_blocks(sources, table, widths):
    plan, places = [], []
    for out_at, columns in enumerate(columns_of(widths)):
        number = 0
        for source_at, source in enumerate(sources):
            for at in range(source.shape[0]):
                plan.append((source_at, at, columns, out_at, None, (0, columns[1])))
                places.append(table[number])
                number += 1
    outs = [(16, width) for width in widths]
    return move_blocks(jnp.stack(places).astype(jnp.int32), sources, outs, plan, "place_blocks")


def half_grads(table, left, right, start, total, given):
    tokens, features = left[0].shape
    width = right[0].shape[-1]
    half = features // 2
    rows = half // 8
    tile = next(t for t in (1152, 768, 512, 384, 256) if width % t == 0 and start % t == 0)
    if half > 1152:
        tile = 384
    given = [] if given is None else list(given)

    def kernel(table_ref, own_left, mate_left, own_right, mate_right, *refs):
        give_ref, keep_ref, total_ref = refs[len(given) :]
        for core in range(2):

            @pl.when(table_ref[0] == core)
            def _():
                mine = pl.ds(core * half, half)
                total_ref[...] = dot_tn(own_left[:, mine], own_right[...]) + dot_tn(
                    mate_left[:, mine], mate_right[...]
                )

        for number in range(8):
            block = total_ref[pl.ds(pl.multiple_of(table_ref[1 + number] * rows, 8), rows), :]
            (give_ref, keep_ref)[number // 4][number % 4] = block.astype(LOW)

    first = start // tile
    whole = pl.BlockSpec((tokens, features), lambda i, table: (0, 0))
    part = pl.BlockSpec((tokens, tile), lambda i, table: (0, i))
    out = pl.BlockSpec((4, rows, tile), lambda i, table: (0, 0, first + i))
    return pl.pallas_call(
        kernel,
        grid_spec=pltpu.PrefetchScalarGridSpec(
            num_scalar_prefetch=1,
            grid=(width // tile,),
            in_specs=[whole, whole, part, part]
            + [pl.BlockSpec(memory_space=pl.ANY)] * len(given),
            out_specs=[out, out],
            scratch_shapes=[pltpu.VMEM((half, tile), jnp.float32)],
        ),
        out_shape=[jax.ShapeDtypeStruct((4, rows, total), LOW)] * 2,
        input_output_aliases={5 + number: number for number in range(len(given))},
        compiler_params=pltpu.CompilerParams(vmem_limit_bytes=48 * 1024 * 1024),
        cost_estimate=about(3 + 1.6e-6 * features * width),
        name="half_grads",
    )(table, *left, *right, *given)


class Staged:
    def __init__(self):
        self.core = lax.axis_index("blk")
        self.z_at = lax.axis_index("inner")
        outer_at = lax.axis_index("outer")
        self.y_at = outer_at // 2
        self.x_at = outer_at % 2
        self.own_half = (self.z_at // 2) == self.core
        self.own_row = self.z_at * 4 + outer_at

    def z_pair(self, core):
        low_bit = self.z_at % 2
        return 2 * core + low_bit, 2 * core + 1 - low_bit

    def near_order(self, core, picks):
        found = []
        for far, near in picks:
            first = jnp.where(core == 0, self.x_at, self.y_at) ^ near
            second = jnp.where(core == 0, self.y_at, self.x_at) ^ far
            y_now = jnp.where(core == 0, second, first)
            x_now = jnp.where(core == 0, first, second)
            found.append(y_now * 2 + x_now)
        return found

    def gather_groups(self, groups, gates, early):
        packed = [
            group[0] if len(group) == 1 else jnp.concatenate(group, axis=1) for group in groups
        ]
        table = []
        for core in (self.core, 1 - self.core):
            for outer_at in self.near_order(core, [(0, 0), (0, 1), (1, 0), (1, 1)]):
                for z_now in self.z_pair(core):
                    table.append(z_now * 4 + outer_at)
        last = len(groups) - 1
        held, others, twos, fours, tokens = {}, {}, {}, {}, {}

        def first_stage(k, gates, late):
            own = after(packed[k], *gates)
            came = after(lax.ppermute(own, EVERY, Z_STRAIGHT), *late)
            held[k] = jnp.where(self.own_half, own, came)
            others[k] = lax.ppermute(held[k], "inner", Z_PAIR)

        def second_stage(k, late):
            twos[k] = jnp.stack([held[k], after(others[k], *late)])

        def third_stage(k, late):
            came = after(lax.ppermute(twos[k], EVERY, NEAR_FIRST), *late)
            fours[k] = jnp.concatenate([twos[k], came])

        first_stage(0, (), early[0]())
        second_stage(0, early[1](held[0]))
        first_stage(1, (held[0],), (twos[0],))
        third_stage(0, early[2](twos[0]))
        second_stage(1, (fours[0],))
        for k in range(len(groups)):
            if k + 1 < last:
                first_stage(k + 2, (twos[k + 1],), ())
            far_four = lax.ppermute(fours[k], EVERY, NEAR_SECOND)
            mate_four = lax.ppermute(fours[k], "blk", SWAP)
            if k < last:
                far_four = after(far_four, twos[k + 1])
            else:
                far_four = after(far_four, tokens[k - 1])
            if k < last:
                third_stage(k + 1, (far_four,))
            mate_far = lax.ppermute(far_four, "blk", SWAP)
            if k < last:
                mate_far = after(mate_far, fours[k + 1])
            sources = [fours[k], far_four, mate_four, mate_far]
            widths = [part.shape[1] for part in groups[k]]
            tokens[k] = gates[k](
                [part.reshape(-1, part.shape[-1]) for part in place_blocks(sources, table, widths)]
            )
            if k + 1 < last:
                second_stage(k + 2, (tokens[k],))

    def share(self, value):
        tokens = value.reshape(-1, value.shape[-1])
        return tokens, lax.ppermute(tokens, "blk", SWAP)

    def start_grads(self, pairs):
        return StagedGrads(self, pairs)

    def update(self, state, rate, parts):
        lanes = [array.reshape(-1, 128) for array in state]
        sizes = [rows * cols // (16 * 128) for rows, cols in mat_shapes()]
        results = None
        for entries in parts:
            if isinstance(entries[0][0], StagedGrads) and entries[0][0].stage == 3:
                for part, _, _ in sum(parts, []):
                    if isinstance(part, StagedGrads) and part.stage == 3:
                        part.add(results[0])
            pieces = []
            for part, start, number in entries:
                grad = part.both if isinstance(part, StagedGrads) else part
                pieces.append((grad, start, mat_shapes()[number][1]))
            first = entries[0][2]
            results = update_rows(pieces, lanes, sum(sizes[:first]), rate, results)
        return [result.reshape(-1) for result in results]

    def gather_slots(self, own, between=None):
        four = jnp.concatenate(
            [own] + [lax.ppermute(own, "inner", route) for route in (UP, DOWN, ACROSS)]
        )
        self.token = four
        if between is not None:
            four = after(four, between())
        return jnp.concatenate(
            [four] + [lax.ppermute(four, "outer", route) for route in (OUT_X, OUT_Y, OUT_XY)]
        )

    def swap_slots(self, parts, between):
        parts = parts.reshape((4, 4) + parts.shape[1:])
        four = jnp.stack(
            [parts[0]]
            + [
                lax.ppermute(parts[1 + at], "outer", route)
                for at, route in enumerate((OUT_X, OUT_Y, OUT_XY))
            ]
        )
        four = after(four, between())
        return jnp.stack(
            [four[:, 0]]
            + [
                lax.ppermute(four[:, 1 + at], "inner", route)
                for at, route in enumerate((DOWN, UP, ACROSS))
            ],
        )

    def reduce_slots(self, parts, late):
        parts = parts.reshape((4, 4) + parts.shape[1:])
        four = parts[0]
        for at, route in enumerate((OUT_X, OUT_Y, OUT_XY)):
            four = four + after(lax.ppermute(parts[1 + at], "outer", route), late)
        self.token = four
        total = four[0]
        for at, route in enumerate((DOWN, UP, ACROSS)):
            total = total + lax.ppermute(four[1 + at], "inner", route)
        return total

    def slot_rows(self):
        found = []
        for z_now in range(4):
            away = (z_now - self.z_at) % 4
            z_slot = jnp.where(away == 0, 0, jnp.where(away == 3, 1, jnp.where(away == 1, 2, 3)))
            for outer_now in range(4):
                flip = jnp.bitwise_xor(outer_now, self.y_at * 2 + self.x_at)
                found.append((flip, z_slot))
        return found

    def rows_in_order(self, slots):
        table = [flip * 4 + z_slot for flip, z_slot in self.slot_rows()]
        return jnp.take(slots, jnp.stack(table), axis=0)

    def swapped_in_order(self, came):
        table = []
        for flip, z_slot in self.slot_rows():
            came_at = jnp.where(z_slot == 1, 2, jnp.where(z_slot == 2, 1, z_slot))
            table.append(came_at * 4 + flip)
        return jnp.take(came.reshape(16, -1), jnp.stack(table), axis=0)


class StagedGrads:
    def __init__(self, moves, pairs):
        self.moves = moves
        low_bit = moves.z_at % 2
        table = [moves.core]
        for outer_at in moves.near_order(moves.core, [(1, 1), (1, 0), (0, 1), (0, 0)]):
            for z_now in (low_bit, 1 - low_bit):
                table.append(z_now * 4 + outer_at)
        table = jnp.stack(table).astype(jnp.int32)
        total = sum(right[0].shape[-1] for _, right in pairs)
        start, found = 0, None
        for left, right in pairs:
            found = half_grads(table, left, right, start, total, found)
            start += right[0].shape[-1]
        self.give, self.keep = found
        self.token = self.give
        self.stage = 0

    def send(self, *gates):
        self.give = after(self.give, *gates) if gates else self.give
        axes, route = (
            (EVERY, NEAR_SECOND),
            (EVERY, NEAR_FIRST),
            ("inner", Z_PAIR),
            (EVERY, flipped(Z_STRAIGHT)),
        )[self.stage]
        self.came = lax.ppermute(self.give, axes, route)

    def add(self, *late):
        came = after(self.came, *late) if late else self.came
        total = self.keep.astype(jnp.float32) + came.astype(jnp.float32)
        if self.stage == 0:
            self.give = total[:2].astype(LOW)
            self.keep = total[2:].astype(LOW)
        elif self.stage == 1:
            self.give = total[1].astype(LOW)
            self.keep = total[0].astype(LOW)
        else:
            self.give = self.keep = total.astype(LOW)
        if self.stage == 3:
            mate = lax.ppermute(self.give, "blk", SWAP)
            self.both = jnp.where(self.moves.own_half, self.give, mate)
        self.token = self.give
        self.stage += 1


def outer_sum(left_arr, right_arr):
    return jnp.einsum("sni,snj->ij", left_arr, right_arr, preferred_element_type=jnp.float32)


class DirectGrads:
    def __init__(self, pairs):
        self.parts = [outer_sum(left[0], right[0]).astype(LOW) for left, right in pairs]
        self.token = self.parts[0]

    def send(self, *gates):
        pass

    def add(self, *late):
        pass

    @functools.cached_property
    def result(self):
        found = []
        for grad in self.parts:
            part = lax.psum_scatter(grad, GROUP, scatter_dimension=0, tiled=True)
            found.append(lax.psum(part, "blk").astype(jnp.float32))
        return found


class Direct:
    def __init__(self):
        self.core = lax.axis_index("blk")
        self.own_row = lax.axis_index("inner") * lax.axis_size("outer") + lax.axis_index("outer")

    def gather_groups(self, groups, gates, early):
        early[0]()
        early[1](groups[0][0])
        early[2](groups[0][0])
        for group, gate in zip(groups, gates):
            gate([lax.all_gather(part, GROUP, axis=0, tiled=True) for part in group])

    def share(self, value):
        return (value,)

    def start_grads(self, pairs):
        return DirectGrads(pairs)

    def update(self, state, rate, parts):
        found = {}
        for part, start, number in sum(parts, []):
            whole = jnp.concatenate(part.result, axis=1) if isinstance(part, DirectGrads) else part
            found[number] = whole[:, start : start + mat_shapes()[number][1]]
        grad = jnp.concatenate([found[number].reshape(-1) for number in sorted(found)])
        return updated(grad, *state, rate)

    def gather_slots(self, own, between=None):
        self.token = own
        if between is not None:
            between()
        return lax.all_gather(own, GROUP, axis=0, tiled=True)

    def reduce_slots(self, parts, late):
        self.token = parts
        return lax.psum_scatter(parts, GROUP, scatter_dimension=0, tiled=False)

    def swap_slots(self, parts, between):
        between()
        return lax.all_gather(parts, GROUP, axis=0)

    def rows_in_order(self, slots):
        return slots

    def swapped_in_order(self, came):
        mine = lax.dynamic_index_in_dim(came, self.own_row, 1, keepdims=False)
        return mine.reshape(mine.shape[0], -1)


def time_embed(steps_t):
    half_dim = D // 2
    frequency = jnp.exp(-math.log(10000.0) * jnp.arange(half_dim, dtype=jnp.float32) / half_dim)
    angles = steps_t.astype(jnp.float32)[:, None] * frequency[None, :]
    return jnp.concatenate([jnp.cos(angles), jnp.sin(angles)], axis=1)


def modulate(values, scale_v, shift_v):
    center = values - jnp.mean(values, axis=-1, keepdims=True)
    normed = center * lax.rsqrt(jnp.mean(center * center, axis=-1, keepdims=True) + EPS_NORM)
    return normed * (1.0 + scale_v[:, None, :]) + shift_v[:, None, :]


def gelu_tanh(values):
    return jax.nn.gelu(values, approximate=True)


def rms_unit(values):
    return values * lax.rsqrt(jnp.mean(values * values, axis=-1, keepdims=True) + EPS_NORM)


def matmul(left_arr, right_arr):
    return jnp.einsum("...i,ij->...j", left_arr, right_arr, preferred_element_type=jnp.float32)


def matmul_t(left_arr, right_arr):
    return jnp.einsum("...j,ij->...i", left_arr, right_arr, preferred_element_type=jnp.float32)


def column_sum(tensor):
    return jnp.sum(tensor.astype(jnp.float32), axis=(0, 1))


def attention(queries, near_kv, far_kv):
    images, rows, _ = queries.shape
    heads = D // E

    def kernel(q_ref, near_ref, far_ref, out_ref):
        for head in range(heads):
            own = pl.ds(head * E, E)
            other = pl.ds(D + head * E, E)
            q_now = q_ref[0, :, own]
            keys = jnp.concatenate([near_ref[0, :, own], far_ref[0, :, own]], axis=0)
            values = jnp.concatenate([near_ref[0, :, other], far_ref[0, :, other]], axis=0)
            scores = dot_nt(keys, q_now) * E ** (-0.5)
            top = jnp.max(scores, axis=0, keepdims=True)
            weight = jnp.exp(scores - top)
            probs = weight * (1.0 / jnp.sum(weight, axis=0, keepdims=True))
            out_ref[0, :, own] = dot_tn(probs.astype(LOW), values).astype(LOW)

    block = pl.BlockSpec((1, rows, D), lambda i: (i, 0, 0))
    block_kv = pl.BlockSpec((1, rows, 2 * D), lambda i: (i, 0, 0))
    return pl.pallas_call(
        kernel,
        grid=(images,),
        in_specs=[block, block_kv, block_kv],
        out_specs=block,
        out_shape=jax.ShapeDtypeStruct(queries.shape, LOW),
        compiler_params=pltpu.CompilerParams(vmem_limit_bytes=32 * 1024 * 1024),
        cost_estimate=about(14 * images / 4),
        name="attention",
    )(queries, near_kv, far_kv)


def attention_grads(queries, near_kv, far_kv, grad_att):
    images, rows, _ = queries.shape
    heads = D // E

    def kernel(q_ref, near_ref, far_ref, grad_ref, dq_ref, dnear_ref, dfar_ref):
        for head in range(heads):
            own = pl.ds(head * E, E)
            other = pl.ds(D + head * E, E)
            q_now = q_ref[0, :, own]
            g_now = grad_ref[0, :, own]
            keys = jnp.concatenate([near_ref[0, :, own], far_ref[0, :, own]], axis=0)
            values = jnp.concatenate([near_ref[0, :, other], far_ref[0, :, other]], axis=0)
            scores = dot_nt(keys, q_now) * E ** (-0.5)
            top = jnp.max(scores, axis=0, keepdims=True)
            weight = jnp.exp(scores - top)
            probs = weight * (1.0 / jnp.sum(weight, axis=0, keepdims=True))
            grad_probs = dot_nt(values, g_now)
            delta = jnp.sum(probs * grad_probs, axis=0, keepdims=True)
            grad_scores = (probs * (grad_probs - delta)).astype(LOW)
            dq_ref[0, :, own] = (dot_tn(grad_scores, keys) * E ** (-0.5)).astype(LOW)
            grad_keys = dot_nn(grad_scores, q_now) * E ** (-0.5)
            grad_values = dot_nn(probs.astype(LOW), g_now)
            dnear_ref[0, :, own] = grad_keys[:rows]
            dnear_ref[0, :, other] = grad_values[:rows]
            dfar_ref[0, :, own] = grad_keys[rows:].astype(LOW)
            dfar_ref[0, :, other] = grad_values[rows:].astype(LOW)

    block = pl.BlockSpec((1, rows, D), lambda i: (i, 0, 0))
    block_kv = pl.BlockSpec((1, rows, 2 * D), lambda i: (i, 0, 0))
    return pl.pallas_call(
        kernel,
        grid=(images,),
        in_specs=[block, block_kv, block_kv, block],
        out_specs=[block, block_kv, block_kv],
        out_shape=[
            jax.ShapeDtypeStruct(queries.shape, LOW),
            jax.ShapeDtypeStruct(near_kv.shape, jnp.float32),
            jax.ShapeDtypeStruct(far_kv.shape, LOW),
        ],
        compiler_params=pltpu.CompilerParams(vmem_limit_bytes=32 * 1024 * 1024),
        cost_estimate=about(21 * images / 4),
        name="attention_grads",
    )(queries, near_kv, far_kv, grad_att)


def dot_nn(left, right):
    return lax.dot_general(
        left, right, (((1,), (0,)), ((), ())), preferred_element_type=jnp.float32
    )


def dot_nt(left, right):
    return lax.dot_general(
        left, right, (((1,), (1,)), ((), ())), preferred_element_type=jnp.float32
    )


def dot_tn(left, right):
    return lax.dot_general(
        left, right, (((0,), (0,)), ((), ())), preferred_element_type=jnp.float32
    )


def body(
    hidden,
    labels,
    steps_t,
    live_slots,
    label_table,
    targets,
    cotangent,
    weights,
    weight_momentum,
    weight_average,
    biases,
    bias_momentum,
    bias_average,
):
    n_inner = lax.axis_size("inner")
    n_outer = lax.axis_size("outer")
    blocks = n_inner * n_outer
    slots = hidden.shape[0]
    local_tok = hidden.shape[1]
    moves = Staged() if (n_inner, n_outer) == (4, 4) else Direct()
    p_qkv, p_proj, p_up, p_down, p_ada, p_one, p_two, p_three = split_shard(
        weights.astype(LOW), mat_shapes(), blocks
    )
    bias_low = biases.astype(LOW)
    condition = label_table[labels].astype(jnp.float32) + time_embed(steps_t)
    cond_act, silu_cond = jax.vjp(jax.nn.silu, condition)
    cond_low = cond_act.astype(LOW)
    kept = {}
    rows_d = D // blocks
    half_ada = 3 * D

    def early_gather():
        packed = jnp.concatenate([cond_low, bias_low.reshape(slots, -1)], axis=1)
        kept["packed"] = moves.gather_slots(packed)
        return (moves.token,)

    def early_product(gate):
        packed_all = after(kept["packed"], gate)
        cond_own = lax.dynamic_slice_in_dim(
            packed_all[:, :D], moves.own_row * rows_d, rows_d, 1
        )
        ada_half = lax.dynamic_slice_in_dim(p_ada, moves.core * half_ada, half_ada, 1)
        mod_part = matmul(cond_own, ada_half).reshape(blocks, slots, half_ada)
        kept.update(cond_own=cond_own, mod_part=mod_part)
        return (mod_part,)

    def early_modulation(gate):
        mod_half = moves.reduce_slots(kept["mod_part"], gate)
        late = moves.token
        mod_mate = lax.ppermute(mod_half, "blk", SWAP)
        bias_all = moves.rows_in_order(kept["packed"][:, D:].reshape(blocks, -1))
        biases_now = unpack_rows(bias_all.astype(jnp.float32), bias_shapes())
        b_ada = biases_now[5]
        kept["biases"] = biases_now
        modulation = (
            jnp.concatenate(
                [
                    jnp.where(moves.core == 0, mod_half, mod_mate),
                    jnp.where(moves.core == 0, mod_mate, mod_half),
                ],
                axis=1,
            )
            + b_ada
        )
        shift_a, scale_a, gate_a, shift_m, scale_m, gate_m = [
            modulation[:, part_idx * D : (part_idx + 1) * D] for part_idx in range(6)
        ]
        hidden_f = hidden.astype(jnp.float32)
        mixed_a, pull_a = jax.vjp(modulate, hidden_f, scale_a, shift_a)
        mixed_a_low = mixed_a.astype(LOW)
        left_qkv = moves.share(mixed_a_low)
        kept.update(
            gates=(gate_a, gate_m), scale_m=scale_m, shift_m=shift_m, hidden_f=hidden_f,
            mixed_a_low=mixed_a_low, pull_a=pull_a, left_qkv=left_qkv,
        )
        return (late,)

    def use_first(arrived):
        b_q, b_v = kept["biases"][:2]
        (w_qkv,) = arrived
        qkv_bias = jnp.concatenate([b_q, jnp.zeros((D,), jnp.float32), b_v])
        qkv_low = (matmul(kept["mixed_a_low"], w_qkv) + qkv_bias).astype(LOW)
        near_kv = qkv_low[..., D:]
        far_kv = passed_along(near_kv, "blk", 1)
        kept.update(w_qkv=w_qkv, queries=qkv_low[..., :D], near_kv=near_kv, far_kv=far_kv)
        return far_kv
    def use_second(arrived):
        w_proj, w_one = arrived
        b_proj = kept["biases"][2]
        queries, near_kv, far_kv = kept["queries"], kept["near_kv"], kept["far_kv"]
        queries = after(queries, w_proj)
        att_low = attention(queries, near_kv, far_kv)
        left_proj = moves.share(att_low)
        branch_a = matmul(att_low, w_proj) + b_proj
        residual = kept["hidden_f"] + kept["gates"][0][:, None, :] * branch_a
        mixed_m, pull_m = jax.vjp(modulate, residual, kept["scale_m"], kept["shift_m"])
        mixed_m_low = mixed_m.astype(LOW)
        left_up = moves.share(mixed_m_low)
        kept.update(
            w_proj=w_proj, w_one=w_one, left_proj=left_proj,
            branch_a=branch_a, residual=residual, pull_m=pull_m, left_up=left_up,
            mixed_m_low=mixed_m_low,
        )
        return mixed_m_low

    def use_third(arrived):
        (w_up,) = arrived
        b_up = kept["biases"][3]
        pre_act = matmul(kept["mixed_m_low"], w_up) + b_up
        activated, gelu_pull = jax.vjp(gelu_tanh, pre_act)
        act_low = activated.astype(LOW)
        gelu_slope = gelu_pull(jnp.ones_like(pre_act))[0]
        left_down = moves.share(act_low)
        act_low, gelu_slope = lax.optimization_barrier((act_low, gelu_slope))
        kept.update(w_up=w_up, gelu_slope=gelu_slope, act_low=act_low, left_down=left_down)
        return act_low

    def use_fourth(arrived):
        (w_down,) = arrived
        b_down, c_one = kept["biases"][4], kept["biases"][6]
        branch_m = matmul(kept["act_low"], w_down) + b_down
        output = kept["residual"] + kept["gates"][1][:, None, :] * branch_m
        out_low = output.astype(LOW)
        left_one = moves.share(out_low)
        hid_one = matmul(out_low, kept["w_one"]) + c_one
        act_one, silu_one = jax.vjp(jax.nn.silu, hid_one)
        one_low = act_one.astype(LOW)
        left_two = moves.share(one_low)
        kept.update(
            w_down=w_down, branch_m=branch_m, out_low=out_low, left_one=left_one,
            silu_one=silu_one, one_low=one_low, left_two=left_two,
        )
        return one_low

    def use_fifth(arrived):
        w_two, w_three = arrived
        c_two, c_three = kept["biases"][7:]
        hid_two = matmul(kept["one_low"], w_two) + c_two
        act_two, silu_two = jax.vjp(jax.nn.silu, hid_two)
        two_low = act_two.astype(LOW)
        left_three = moves.share(two_low)
        projection = matmul(two_low, w_three) + c_three
        kept.update(
            w_two=w_two, w_three=w_three, silu_two=silu_two, left_three=left_three,
            projection=projection,
        )

    moves.gather_groups(
        [[p_qkv], [p_proj, p_one], [p_up], [p_down], [p_two, p_three]],
        [use_first, use_second, use_third, use_fourth, use_fifth],
        [early_gather, early_product, early_modulation],
    )
    w_qkv, w_proj, w_up, w_down, w_one, w_two, w_three = [
        kept[name] for name in ("w_qkv", "w_proj", "w_up", "w_down", "w_one", "w_two", "w_three")
    ]
    gate_a, gate_m = kept["gates"]
    cond_own = kept["cond_own"]
    pull_a, left_qkv = kept["pull_a"], kept["left_qkv"]
    queries, near_kv, far_kv = [kept[name] for name in ("queries", "near_kv", "far_kv")]
    branch_a, branch_m, out_low, projection = [
        kept[name] for name in ("branch_a", "branch_m", "out_low", "projection")
    ]
    pull_m, gelu_slope, silu_one, silu_two = [
        kept[name] for name in ("pull_m", "gelu_slope", "silu_one", "silu_two")
    ]
    live_f = live_slots.astype(jnp.float32)[:, None, None]
    unit_proj, unit_pull = jax.vjp(rms_unit, projection)
    grad_proj = unit_pull(-LAMBDA_REPA * live_f * rms_unit(targets.astype(jnp.float32)))[0].astype(
        LOW
    )
    right_three = moves.share(grad_proj)
    grad_cthree = column_sum(grad_proj)
    grad_htwo = silu_two(matmul_t(grad_proj, w_three))[0].astype(LOW)
    right_two = moves.share(grad_htwo)
    grad_ctwo = column_sum(grad_htwo)
    grad_hone = silu_one(matmul_t(grad_htwo, w_two))[0].astype(LOW)
    right_one = moves.share(grad_hone)
    grads_fourth = moves.start_grads(
        [(kept["left_two"], right_two), (kept["left_three"], right_three)]
    )
    grad_cone = column_sum(grad_hone)
    grads_fourth.send()
    right_one = after_all(right_one, grads_fourth.token)
    grads_one = moves.start_grads([(kept["left_one"], right_one)])
    grads_one.send()
    grad_hone = after(grad_hone, grads_one.token)
    grad_output = cotangent.astype(jnp.float32) * live_f + matmul_t(grad_hone, w_one)
    grad_gate_m = jnp.sum(grad_output * branch_m, axis=1)
    grad_bm = (gate_m[:, None, :] * grad_output).astype(LOW)
    right_down = moves.share(grad_bm)
    grad_bdown = column_sum(grad_bm)
    grad_pre = (matmul_t(grad_bm, w_down) * gelu_slope).astype(LOW)
    right_up = moves.share(grad_pre)
    grads_down = moves.start_grads([(kept["left_down"], right_down)])
    grad_bup = column_sum(grad_pre)
    grads_down.send()
    grads_fourth.add(grads_down.token)
    grads_fourth.send()
    grad_pre = after(grad_pre, grads_down.token, grads_fourth.token)
    grad_res_m, grad_scale_m, grad_shift_m = pull_m(matmul_t(grad_pre, w_up))
    grad_residual = grad_output + grad_res_m
    grad_gate_a = jnp.sum(grad_residual * branch_a, axis=1)
    grad_ba = (gate_a[:, None, :] * grad_residual).astype(LOW)
    right_proj = moves.share(grad_ba)
    grad_bproj = column_sum(grad_ba)
    grad_att = matmul_t(grad_ba, w_proj).astype(LOW)
    grads_one.add(grad_att)
    grads_one.send()
    grads_fourth.add(grad_att)
    grads_fourth.send()
    right_up = after_all(right_up, grads_fourth.token, grads_one.token)
    grads_up = moves.start_grads([(kept["left_up"], right_up), (kept["left_proj"], right_proj)])
    grads_up.send()
    grads_down.add(grads_up.token)
    grads_down.send()
    grads_one.add(grads_up.token)
    grads_one.send()
    grads_fourth.add(grads_up.token)
    grads_fourth.send()
    grad_att = after(
        grad_att, grads_up.token, grads_down.token, grads_one.token, grads_fourth.token
    )
    grad_query, near_dkv, far_dkv = attention_grads(queries, near_kv, far_kv, grad_att)
    home_dkv = passed_along(far_dkv, "blk", -1)
    grads_down.add(grad_query)
    grads_down.send()
    grads_fourth.add(grad_query)
    grads_one.add(grad_query)
    grads_one.send()
    home_dkv = after(home_dkv, grads_down.token, grads_one.token, grads_fourth.token)
    grad_kv = (near_dkv + home_dkv.astype(jnp.float32)).astype(LOW)
    grad_qkv = jnp.concatenate([grad_query, grad_kv], axis=-1)
    grads_first = moves.start_grads([(left_qkv, moves.share(grad_qkv))])
    qkv_sums = column_sum(grad_qkv)
    grads_first.send()
    grads_down.add(grads_first.token)
    grads_down.send()
    grads_one.add(grads_first.token)
    grad_qkv = after(grad_qkv, grads_first.token, grads_down.token, grads_one.token)
    grad_hid_a, grad_scale_a, grad_shift_a = pull_a(matmul_t(grad_qkv, w_qkv))
    grad_input = grad_residual + grad_hid_a
    grad_mod_part = jnp.concatenate(
        [grad_shift_a, grad_scale_a, grad_gate_a, grad_shift_m, grad_scale_m, grad_gate_m], axis=1
    )
    bias_terms = (
        qkv_sums[:D],
        qkv_sums[2 * D :],
        grad_bproj,
        grad_bup,
        grad_bdown,
        grad_cone,
        grad_ctwo,
        grad_cthree,
    )
    bias_grid = jnp.concatenate(
        [segment.reshape(blocks, -1) for segment in bias_terms], axis=1
    ).reshape(slots, -1)
    grad_small = jnp.concatenate([grad_mod_part, bias_grid], axis=1)
    small_came = lax.ppermute(grad_small, "blk", SWAP)
    grads_up.add(grad_small)
    grads_up.send()
    grads_first.add(grads_up.token)
    grads_first.send()
    small_came = after(small_came, grads_up.token, grads_first.token)
    grad_small = (grad_small + small_came).astype(LOW)
    small_all = moves.gather_slots(grad_small)
    grads_first.add(small_all)
    grads_first.send()
    grads_up.add(small_all)
    grads_up.send()
    small_all = after(small_all, grads_first.token, grads_up.token)

    def between_swaps():
        grads_first.add()
        grads_first.send()
        grads_up.add()
        grads_up.send()
        return lax.optimization_barrier((grads_up.token, grads_first.token))[0]

    grad_mod = small_all[:, : 6 * D]
    cond_cols = matmul_t(grad_mod, p_ada).reshape(blocks, slots, rows_d)
    cond_rows = moves.swapped_in_order(moves.swap_slots(cond_cols, between_swaps))
    grad_cond = silu_cond(
        cond_rows.reshape(blocks, slots, rows_d).transpose(1, 0, 2).reshape(slots, D)
    )[0]
    grad_wada = jnp.einsum("si,sj->ij", cond_own, grad_mod, preferred_element_type=jnp.float32)
    grad_bada = lax.dynamic_index_in_dim(
        jnp.sum(grad_mod.astype(jnp.float32), axis=0).reshape(blocks, -1),
        moves.own_row,
        0,
        keepdims=False,
    )
    bias_sums = jnp.sum(
        small_all[:, 6 * D :].astype(jnp.float32).reshape(blocks, slots, -1), axis=0
    )
    bias_own = lax.dynamic_index_in_dim(
        bias_sums.reshape(blocks, -1), moves.own_row, 0, keepdims=False
    )
    ada_at = (3 * D + FF + D) // blocks
    grad_b_flat = jnp.concatenate([bias_own[:ada_at], grad_bada, bias_own[ada_at:]])
    grads_down.add(grad_mod_part)
    grads_first.add()
    grad_wada = after(grad_wada, grads_first.token)
    images_all = slots * blocks
    tokens_img = local_tok * lax.axis_size("blk")
    rate_w = LR_COEF / math.sqrt(images_all * tokens_img)
    rate_b = BIAS_FACTOR * rate_w
    mom_w, new_w, low_w, avg_w = moves.update(
        (weights, weight_momentum, weight_average),
        rate_w,
        [
            [(grads_fourth, 0, 6)],
            [(grads_fourth, PH, 7)],
            [(grads_one, 0, 5)],
            [(grads_down, 0, 3)],
            [(grad_wada, 0, 4)],
            [(grads_up, 0, 2)],
            [(grads_first, 0, 0), (grads_up, FF, 1)],
        ],
    )
    mom_b = MOMENTUM * bias_momentum + grad_b_flat
    new_b = biases - rate_b * (grad_b_flat + MOMENTUM * mom_b)
    avg_b = AVERAGE * bias_average + (1.0 - AVERAGE) * new_b
    return (
        out_low,
        grad_input,
        grad_cond,
        mom_w,
        new_w,
        low_w,
        avg_w,
        mom_b,
        new_b,
        new_b.astype(LOW),
        avg_b,
    )


def solution(mesh):
    in_specs = (
        P(("inner", "outer"), "blk", None),
        P(("inner", "outer")),
        P(("inner", "outer")),
        P(("inner", "outer")),
        P(),
        P(("inner", "outer"), "blk", None),
        P(("inner", "outer"), "blk", None),
        P(("inner", "outer")),
        P(("inner", "outer")),
        P(("inner", "outer")),
        P(("inner", "outer")),
        P(("inner", "outer")),
        P(("inner", "outer")),
    )
    out_specs = (
        P(("inner", "outer"), "blk", None),
        P(("inner", "outer"), "blk", None),
        P(("inner", "outer"), None),
        P(("inner", "outer")),
        P(("inner", "outer")),
        P(("inner", "outer")),
        P(("inner", "outer")),
        P(("inner", "outer")),
        P(("inner", "outer")),
        P(("inner", "outer")),
        P(("inner", "outer")),
    )
    return jax.shard_map(body, mesh=mesh, in_specs=in_specs, out_specs=out_specs, check_vma=False)
```
